128 devices in a mesh: kv: 4 (over y), blk: 32 (over z, x, core).
Axes of the slice: x: 4, y: 4, z: 4, core: 2. Of those that a mesh axis runs over, the one named last changes fastest.
Arguments:
- queries: bfloat16 [128, 4096], P('blk', 'kv'), may hold values from -120 to 120
- cache_keys: bfloat16 [128, 4096, 4, 128], P('blk', None, 'kv'), may hold values from -5 to 5
- cache_values: bfloat16 [128, 4096, 4, 128], P('blk', None, 'kv'), may hold values from -6 to 6
- lengths: int32 [128], replicated, may hold values from 1 to 32768, as said below
- sinks: float32 [32], P('kv'), may hold values from 5 to 11
- out_proj: bfloat16 [4096, 2048], P('kv'), may hold values from -0.09375 to 0.09375
- decode_resid: bfloat16 [128, 2048], P(('blk', 'kv')), may hold values from -4 to 4
- prefill_hidden: bfloat16 [128, 111, 2048], P(('blk', 'kv')), may hold values from -6 to 6
- norm_gain: float32 [2048], replicated, may hold values from 0.1 to 1.9
- router: bfloat16 [2048, 128], replicated, may hold values from -80 to 80
- routes: int32 [128, 112, 8], P(('blk', 'kv')), may hold values from 0 to 127, all different within a row; in each aligned block of 112 rows (0 to 111, 112 to 223, ..., all dimensions but the last counted through in order) at most 14 rows name the same one
- expert_gate: bfloat16 [128, 2048, 768], P(('kv', 'blk')), may hold values from -0.125 to 0.125
- expert_up: bfloat16 [128, 2048, 768], P(('kv', 'blk')), may hold values from -0.125 to 0.125
- expert_down: bfloat16 [128, 768, 2048], P(('kv', 'blk')), may hold values from -0.21875 to 0.21875
Outputs:
- layer_out: bfloat16 [128, 112, 2048], P(('blk', 'kv'))
The draws below stay inside these ranges and needn't reach their ends.
Inputs may be any that keep to these rules, and one draw needn't show every extreme that they name: `lengths`: at least one request has exactly 32768 cached positions. `routes`: within the rows of one device (112 rows, aligned blocks) no expert is named by more than 14 rows, and in every draw some expert reaches 14 in some block.
All inputs are finite; a program needn't handle non-finite values.
Results may differ from the reference program's by a relative error of at most 0.0094.
Values may be sent and summed in bfloat16 or wider, within the bound.
A program may use at most 128 MiB of HBM per device.

```python
import math
import jax
import jax.numpy as jnp
import numpy as np
from jax import lax

D = 2048
FF = 768
HQ = 32
KVH = 4
HD = 128
TOP = 8
WIN = 4096
CONTEXT = 32768
PREF_DEV = 111
EXPERTS = 128
REQ = 128
TOK_DEV = 112
CAP = 14
N_KV = 4
N_BLK = 32


def shared_keys(key):
    base = jax.random.fold_in(key, 7)
    raw = jnp.clip(jax.random.normal(base, (REQ, WIN, KVH, HD), jnp.float32), -5.0, 5.0)
    return raw


def draw_cache_keys(key, part):
    return shared_keys(key).astype(jnp.bfloat16)


def draw_queries(key, part):
    own_key = jax.random.fold_in(key, 11)
    raw = jnp.clip(2.5 * jax.random.normal(own_key, (REQ, HQ * HD), jnp.float32), -12.5, 12.5)
    return raw.astype(jnp.bfloat16)


def draw_router(key, part):
    base_key = jax.random.fold_in(key, 13)
    raw = jnp.clip(jax.random.normal(base_key, (D, EXPERTS), jnp.float32), -4.0, 4.0) / math.sqrt(D)
    return raw.astype(jnp.bfloat16)


def draw_lengths(key, part):
    first_key, second_key, third_key, fourth_key = jax.random.split(key, 4)
    short_len = jax.random.randint(first_key, (REQ,), 1, WIN + 1)
    long_len = jax.random.randint(second_key, (REQ,), WIN, CONTEXT + 1)
    picker = jax.random.randint(third_key, (REQ,), 0, 2)
    chosen_len = jnp.where(picker == 0, short_len, long_len)
    position = jax.random.randint(fourth_key, (), 0, REQ)
    return chosen_len.at[position].set(CONTEXT).astype(jnp.int32)


def block_levels(key, extent, cuts, low, largest):
    loudness = 1.0
    for axis_at, shards_of in cuts:
        heights = jax.random.uniform(jax.random.fold_in(jax.random.fold_in(key, 6), axis_at), (shards_of,), jnp.float32, low / len(cuts), largest / len(cuts))
        loudness = loudness * jnp.repeat(jnp.exp(heights), extent[axis_at] // shards_of).reshape((-1,) + (1,) * (len(extent) - 1 - axis_at))
    return loudness


def assign_block(stream_key, own, number, rows, amount, top, bound, skew):
    order = jax.random.permutation(stream_key, amount)
    crowded, usual = load_shares(amount, rows * top, bound, skew, True), load_shares(amount, rows * top, bound, skew, False)
    places = jnp.arange(amount)

    def named(tallies, offset_by):
        used = int((tallies > 0).sum())
        fixed = max(1, used // 4)
        moved = fixed + (places - fixed + offset_by * (used - fixed)) % max(1, amount - fixed)
        return jnp.zeros((amount,), jnp.int32).at[order[jnp.where(places < fixed, places, moved)]].set(jnp.asarray(tallies, jnp.int32))

    tallies = jnp.where(number % 4 == 0, named(crowded, number // 4), named(usual, number - number // 4 - 1))
    mixed = jax.random.permutation(jax.random.fold_in(own, 3), amount)
    source_of, receiver = mixed[0:amount // 2 * 2:2], mixed[1:amount // 2 * 2:2]
    margin = jnp.minimum(tallies[source_of] - 1, bound - tallies[receiver]) // 2
    margin = jnp.where((source_of == order[0]) | (receiver == order[0]) | (tallies[receiver] == 0), 0, jnp.maximum(margin, 0))
    moved = jax.random.randint(jax.random.fold_in(own, 4), (amount // 2,), 0, 1 << 20) % (margin + 1)
    tallies = tallies.at[source_of].add(-moved).at[receiver].add(moved)
    items = jnp.searchsorted(jnp.cumsum(tallies), jnp.arange(rows * top), side="right").astype(jnp.int32)
    table = items.reshape(top, rows).T
    table = table[jax.random.permutation(jax.random.fold_in(own, 1), rows)]
    offset_by = jax.random.randint(jax.random.fold_in(own, 2), (rows, 1), 0, top)
    return jnp.take_along_axis(table, (jnp.arange(top)[None, :] + offset_by) % top, axis=1)


def load_shares(count, total, most, lean, full):
    weights = [(1 << 20) // math.isqrt(standing ** lean) + 1 for standing in range(1, count + 1)]
    largest = most if full else min(most, max(-(-total // count), total * weights[0] // sum(weights)))
    least = 1 if total - largest >= count - 1 else 0
    counts, rest = [largest] + [least] * (count - 1), total - largest - least * (count - 1)
    while rest > 0:
        candidates = [i for i in range(1, count) if counts[i] < largest] or [i for i in range(1, count) if counts[i] < most]
        pool, left = sum([weights[i] for i in candidates]), rest
        for i in candidates:
            addition = min(most - counts[i], max(1, left * weights[i] // pool), rest)
            counts[i] = counts[i] + addition
            rest = rest - addition
    return np.array(counts)


def gaussian(stream_key, extent, spread, bound, cuts=(), kind=jnp.bfloat16):
    array = jax.random.normal(stream_key, extent, jnp.float32) * spread
    if len(cuts) > 0:
        array = block_levels(stream_key, extent, cuts, -0.22, 0.18) * array
    return jnp.clip(array, min=-bound, max=bound).astype(kind)


def setup_inputs(seed: int = 0) -> dict:
    key_list = jax.random.split(jax.random.key(seed), 15)
    queries = draw_queries(jax.random.fold_in(key_list[14], 71), 0)
    cache_keys = draw_cache_keys(jax.random.fold_in(key_list[14], 71), 0)
    cache_values = gaussian(key_list[2], (REQ, WIN, KVH, HD), 1.0, 6.0, ((0, 32), (2, 4)))
    lengths = draw_lengths(jax.random.fold_in(key_list[14], 71), 0)
    sinks = jnp.clip(5.0 + 6.0 * jax.random.uniform(key_list[4], (HQ,), jnp.float32) ** block_levels(key_list[4], (HQ,), ((0, 4),), -0.2, 0.2), 5.0, 11.0)
    out_proj = gaussian(key_list[5], (HQ * HD, D), (HQ * HD) ** -0.5, 0.09375, ((0, 4),))
    decode_resid = gaussian(key_list[6], (REQ, D), 0.5, 4.0, ((0, 128),))
    prefill_hidden = gaussian(key_list[7], (REQ, PREF_DEV, D), 1.0, 6.0, ((0, 128),))
    norm_gain = jnp.clip(1.0 + 0.18 * jax.random.normal(key_list[8], (D,), jnp.float32), 0.1, 1.9)
    router = draw_router(jax.random.fold_in(key_list[14], 71), 0)
    routes_keys = jax.random.split(jax.random.fold_in(key_list[10], 1), REQ * TOK_DEV // TOK_DEV)
    routes_turns = jax.random.permutation(jax.random.fold_in(key_list[10], 3), REQ * TOK_DEV // TOK_DEV)
    routes = jax.vmap(lambda own, number: assign_block(jax.random.fold_in(key_list[10], 2), own, number, TOK_DEV, EXPERTS, TOP, CAP, 1))(routes_keys, routes_turns).reshape((REQ, TOK_DEV, TOP))
    expert_gate = gaussian(key_list[11], (EXPERTS, D, FF), D ** -0.5, 0.125, ((0, 128),))
    expert_up = gaussian(key_list[12], (EXPERTS, D, FF), D ** -0.5, 0.125, ((0, 128),))
    expert_down = gaussian(key_list[13], (EXPERTS, FF, D), FF ** -0.5, 0.21875, ((0, 128),))
    return dict(queries=queries, cache_keys=cache_keys, cache_values=cache_values, lengths=lengths, sinks=sinks, out_proj=out_proj, decode_resid=decode_resid, prefill_hidden=prefill_hidden, norm_gain=norm_gain, router=router, routes=routes, expert_gate=expert_gate, expert_up=expert_up, expert_down=expert_down)


NEG_FILL = -1e+30
EPSILON = 1e-06

def reference(queries, cache_keys, cache_values, lengths, sinks, out_proj, decode_resid, prefill_hidden, norm_gain, router, routes, expert_gate, expert_up, expert_down):
    per_group = HQ // KVH
    sink_grid = sinks.reshape(KVH, per_group)

    def attend(packed):
        one_query, key_rows, value_rows, length = packed
        grouped_q = one_query.reshape(KVH, per_group, HD).astype(jnp.float32)
        scores = jnp.einsum('gqd,jgd->gqj', grouped_q, key_rows.astype(jnp.float32)) * (1.0 / math.sqrt(HD))
        first_valid = WIN - jnp.minimum(length, WIN)
        is_valid = (jnp.arange(WIN, dtype=jnp.int32) >= first_valid)[None, None, :]
        masked = jnp.where(is_valid, scores, NEG_FILL)
        top_limit = jnp.maximum(lax.optimization_barrier(jnp.max(masked, axis=2)), sink_grid)
        weights = jnp.where(is_valid, jnp.exp(masked - top_limit[..., None]), 0.0)
        denominator = lax.optimization_barrier(jnp.sum(weights, axis=2)) + jnp.exp(sink_grid - top_limit)
        rounded = lax.optimization_barrier(weights.astype(jnp.bfloat16))
        numerator = jnp.einsum('gqj,jgd->gqd', rounded.astype(jnp.float32), value_rows.astype(jnp.float32))
        return (numerator / denominator[..., None]).astype(jnp.bfloat16).reshape(HQ * HD)
    attended = lax.map(attend, (queries, cache_keys, cache_values, lengths))
    projected = jnp.dot(attended, out_proj, preferred_element_type=jnp.float32)
    decoded = (decode_resid.astype(jnp.float32) + projected).astype(jnp.bfloat16)
    hidden = jnp.concatenate([decoded[:, None, :], prefill_hidden], axis=1).reshape(-1, D)
    hidden_f = hidden.astype(jnp.float32)
    mean_sq = lax.optimization_barrier(jnp.mean(hidden_f * hidden_f, axis=1, keepdims=True))
    normed = (hidden_f * lax.rsqrt(mean_sq + EPSILON) * norm_gain).astype(jnp.bfloat16)
    logits = jnp.dot(normed, router, preferred_element_type=jnp.float32)
    flat_routes = routes.reshape(-1, TOP)
    chosen = jnp.take_along_axis(logits, flat_routes, axis=1)
    gate_probs = jax.nn.softmax(chosen, axis=1).reshape(-1)
    flat_ids = flat_routes.reshape(-1)
    max_rows = N_KV * N_BLK * CAP

    def one_expert(running, expert):
        row_order = jnp.argsort((flat_ids != expert).astype(jnp.int32), stable=True)[:max_rows].astype(jnp.int32)
        is_hit = flat_ids[row_order] == expert
        token_rows = row_order // TOP
        picked = normed[token_rows]
        gate_act = jnp.dot(picked, expert_gate[expert], preferred_element_type=jnp.float32)
        up_act = jnp.dot(picked, expert_up[expert], preferred_element_type=jnp.float32)
        inner_act = (jax.nn.silu(gate_act) * up_act).astype(jnp.bfloat16)
        output = jnp.dot(inner_act, expert_down[expert], preferred_element_type=jnp.float32)
        output = lax.optimization_barrier(output.astype(jnp.bfloat16)).astype(jnp.float32)
        weighted = jnp.where(is_hit, gate_probs[row_order], 0.0)[:, None] * output
        return (running.at[token_rows].add(weighted), None)
    running, ignored = lax.scan(one_expert, jnp.zeros((hidden.shape[0], D), jnp.float32), jnp.arange(EXPERTS, dtype=jnp.int32))
    return (hidden_f + running).astype(jnp.bfloat16).reshape(REQ, TOK_DEV, D)
```

```python
import math

import jax
import jax.numpy as jnp
from jax import lax
from jax.experimental import pallas as pl
from jax.experimental.pallas import tpu as pltpu
from jax.sharding import PartitionSpec as P

NEG_FILL = -1e30
EPSILON = 1e-06
MESH = pl.DeviceIdType.MESH


def kv_reduce_kernel(n_kv, part_ref, out_ref, held, send_sem, recv_sem):
    me = lax.axis_index("kv")
    blk = lax.axis_index("blk")
    barrier = pltpu.get_barrier_semaphore()
    for step in range(1, n_kv):
        peer = lax.rem(me + step, n_kv)
        pl.semaphore_signal(barrier, inc=1, device_id=(peer, blk), device_id_type=MESH)
    pl.semaphore_wait(barrier, n_kv - 1)
    for step in range(1, n_kv):
        peer = lax.rem(me + step, n_kv)
        pltpu.make_async_remote_copy(
            src_ref=part_ref.at[peer],
            dst_ref=held.at[me],
            send_sem=send_sem.at[peer],
            recv_sem=recv_sem.at[me],
            device_id=(peer, blk),
            device_id_type=MESH,
        ).start()
    own = part_ref[me]
    for step in range(1, n_kv):
        peer = lax.rem(me + step, n_kv)
        arrival = pltpu.make_async_remote_copy(
            src_ref=part_ref.at[peer],
            dst_ref=held.at[peer],
            send_sem=send_sem.at[peer],
            recv_sem=recv_sem.at[peer],
            device_id=(peer, blk),
            device_id_type=MESH,
        )
        arrival.wait_send()
        arrival.wait_recv()
    total = own
    for step in range(1, n_kv):
        peer = lax.rem(me + step, n_kv)
        total = total + held[peer]
    out_ref[...] = total


def kv_reduce(partial, n_kv):
    rows, width = partial.shape
    return pl.pallas_call(
        lambda *refs: kv_reduce_kernel(n_kv, *refs),
        out_shape=jax.ShapeDtypeStruct((1, width), jnp.float32),
        in_specs=[pl.BlockSpec(memory_space=pltpu.VMEM)],
        out_specs=pl.BlockSpec(memory_space=pltpu.VMEM),
        scratch_shapes=[
            pltpu.VMEM((n_kv, 1, width), jnp.float32),
            pltpu.SemaphoreType.DMA((n_kv,)),
            pltpu.SemaphoreType.DMA((n_kv,)),
        ],
        compiler_params=pltpu.CompilerParams(collective_id=0, has_side_effects=True),
    )(partial.reshape(rows, 1, width))


def expert_block(slots, gate_weights, up_weights, down_weights):
    gate_act = jnp.dot(slots, gate_weights[0], preferred_element_type=jnp.float32)
    up_act = jnp.dot(slots, up_weights[0], preferred_element_type=jnp.float32)
    inner_act = (jax.nn.silu(gate_act) * up_act).astype(jnp.bfloat16)
    result = jnp.dot(inner_act, down_weights[0], preferred_element_type=jnp.float32)
    return result.astype(jnp.bfloat16)


def body(
    queries,
    cache_keys,
    cache_values,
    lengths,
    sinks,
    out_proj,
    decode_resid,
    prefill_hidden,
    norm_gain,
    router,
    routes,
    expert_gate,
    expert_up,
    expert_down,
):
    n_kv = lax.axis_size("kv")
    my_block = lax.axis_index("blk")
    per_block = queries.shape[0]
    head_count = sinks.shape[0]
    head_dim = cache_keys.shape[3]
    window = cache_keys.shape[1]
    grouped_q = queries.reshape(per_block, head_count, head_dim)
    key_rows = cache_keys[:, :, 0, :]
    value_rows = cache_values[:, :, 0, :]
    my_lengths = lax.dynamic_slice_in_dim(lengths, my_block * per_block, per_block)
    scores = jnp.einsum("rgd,rjd->rgj", grouped_q, key_rows, preferred_element_type=jnp.float32) * (
        1.0 / math.sqrt(head_dim)
    )
    first_valid = window - jnp.minimum(my_lengths, window)
    is_valid = (jnp.arange(window, dtype=jnp.int32)[None, :] >= first_valid[:, None])[:, None, :]
    masked = jnp.where(is_valid, scores, NEG_FILL)
    top_limit = jnp.maximum(jnp.max(masked, axis=2), sinks[None, :])
    weights = jnp.where(is_valid, jnp.exp(masked - top_limit[..., None]), 0.0)
    denominator = jnp.sum(weights, axis=2) + jnp.exp(sinks[None, :] - top_limit)
    numerator = jnp.einsum(
        "rgj,rjd->rgd", weights.astype(jnp.bfloat16), value_rows, preferred_element_type=jnp.float32
    )
    attended = (
        (numerator / denominator[..., None])
        .astype(jnp.bfloat16)
        .reshape(per_block, head_count * head_dim)
    )
    partial_proj = jnp.dot(attended, out_proj, preferred_element_type=jnp.float32)
    projected = kv_reduce(partial_proj, n_kv)
    decoded = (decode_resid.astype(jnp.float32) + projected).astype(jnp.bfloat16)
    hidden = jnp.concatenate([decoded, prefill_hidden[0]], axis=0)
    hidden_f = hidden.astype(jnp.float32)
    mean_sq = jnp.mean(hidden_f * hidden_f, axis=1, keepdims=True)
    normed = (hidden_f * lax.rsqrt(mean_sq + EPSILON) * norm_gain).astype(jnp.bfloat16)

    experts = router.shape[1]
    chosen_ids = routes[0]
    tokens, top_k = chosen_ids.shape
    capacity = max(2, (2 * tokens * top_k + experts - 1) // experts)
    logits = jnp.dot(normed, router, preferred_element_type=jnp.float32)
    one_hot = chosen_ids[..., None] == jnp.arange(experts, dtype=jnp.int32)
    chosen = jnp.sum(jnp.where(one_hot, logits[:, None, :], 0.0), axis=2)
    gate_probs = jax.nn.softmax(chosen, axis=1)
    row_hot = jnp.any(one_hot, axis=1).astype(jnp.int32)
    earlier = jnp.cumsum(row_hot, axis=0) - row_hot
    slot_rank = jnp.sum(jnp.where(one_hot, earlier[:, None, :], 0), axis=2)
    rank_hot = slot_rank[..., None] == jnp.arange(capacity, dtype=jnp.int32)
    place = jnp.einsum(
        "tke,tkc->tec",
        one_hot.astype(jnp.bfloat16),
        rank_hot.astype(jnp.bfloat16),
        preferred_element_type=jnp.float32,
    )
    place = place.reshape(tokens, experts * capacity)
    outgoing = jnp.einsum(
        "ts,td->sd", place.astype(jnp.bfloat16), normed, preferred_element_type=jnp.float32
    ).astype(jnp.bfloat16)
    processed = expert_block(
        lax.all_to_all(outgoing, ("kv", "blk"), split_axis=0, concat_axis=0, tiled=True),
        expert_gate,
        expert_up,
        expert_down,
    )
    returned = lax.all_to_all(processed, ("kv", "blk"), split_axis=0, concat_axis=0, tiled=True)
    mix = jnp.einsum(
        "tke,tkc->tec",
        jnp.where(one_hot, gate_probs[..., None], 0.0),
        rank_hot.astype(jnp.float32),
        precision=lax.Precision.HIGHEST,
        preferred_element_type=jnp.float32,
    )
    mix = mix.reshape(tokens, experts * capacity)
    mix_hi = mix.astype(jnp.bfloat16)
    mix_lo = (mix - mix_hi.astype(jnp.float32)).astype(jnp.bfloat16)
    combined = jnp.einsum(
        "ts,sd->td", mix_hi, returned, preferred_element_type=jnp.float32
    ) + jnp.einsum("ts,sd->td", mix_lo, returned, preferred_element_type=jnp.float32)
    layer_sum = (hidden_f + combined).astype(jnp.bfloat16)
    return layer_sum[None]


def solution(mesh):
    return jax.shard_map(
        body,
        mesh=mesh,
        in_specs=(
            P("blk", "kv"),
            P("blk", None, "kv", None),
            P("blk", None, "kv", None),
            P(),
            P("kv"),
            P("kv", None),
            P(("blk", "kv"), None),
            P(("blk", "kv"), None, None),
            P(),
            P(),
            P(("blk", "kv"), None, None),
            P(("kv", "blk"), None, None),
            P(("kv", "blk"), None, None),
            P(("kv", "blk"), None, None),
        ),
        out_specs=P(("blk", "kv"), None, None),
        check_vma=False,
    )
```

```python
import math

import jax
import jax.numpy as jnp
from jax import lax
from jax.experimental import pallas as pl
from jax.experimental.pallas import tpu as pltpu
from jax.sharding import PartitionSpec as P

NEG_FILL = -1e30
EPSILON = 1e-06
MESH = pl.DeviceIdType.MESH


def kv_reduce_kernel(n_kv, part_ref, out_ref, held, send_sem, recv_sem):
    me = lax.axis_index("kv")
    blk = lax.axis_index("blk")
    barrier = pltpu.get_barrier_semaphore()
    for step in range(1, n_kv):
        peer = lax.rem(me + step, n_kv)
        pl.semaphore_signal(barrier, inc=1, device_id=(peer, blk), device_id_type=MESH)
    pl.semaphore_wait(barrier, n_kv - 1)
    for step in range(1, n_kv):
        peer = lax.rem(me + step, n_kv)
        pltpu.make_async_remote_copy(
            src_ref=part_ref.at[peer],
            dst_ref=held.at[me],
            send_sem=send_sem.at[peer],
            recv_sem=recv_sem.at[me],
            device_id=(peer, blk),
            device_id_type=MESH,
        ).start()
    own = part_ref[me]
    for step in range(1, n_kv):
        peer = lax.rem(me + step, n_kv)
        arrival = pltpu.make_async_remote_copy(
            src_ref=part_ref.at[peer],
            dst_ref=held.at[peer],
            send_sem=send_sem.at[peer],
            recv_sem=recv_sem.at[peer],
            device_id=(peer, blk),
            device_id_type=MESH,
        )
        arrival.wait_send()
        arrival.wait_recv()
    total = own
    for step in range(1, n_kv):
        peer = lax.rem(me + step, n_kv)
        total = total + held[peer]
    out_ref[...] = total


def kv_reduce(partial, n_kv):
    rows, width = partial.shape
    return pl.pallas_call(
        lambda *refs: kv_reduce_kernel(n_kv, *refs),
        out_shape=jax.ShapeDtypeStruct((1, width), jnp.float32),
        in_specs=[pl.BlockSpec(memory_space=pltpu.VMEM)],
        out_specs=pl.BlockSpec(memory_space=pltpu.VMEM),
        scratch_shapes=[
            pltpu.VMEM((n_kv, 1, width), jnp.float32),
            pltpu.SemaphoreType.DMA((n_kv,)),
            pltpu.SemaphoreType.DMA((n_kv,)),
        ],
        compiler_params=pltpu.CompilerParams(collective_id=0, has_side_effects=True),
    )(partial.reshape(rows, 1, width))


def expert_block(slots, gate_weights, up_weights, down_weights):
    gate_act = jnp.dot(slots, gate_weights[0], preferred_element_type=jnp.float32)
    up_act = jnp.dot(slots, up_weights[0], preferred_element_type=jnp.float32)
    inner_act = (gate_act / (1.0 + jnp.exp(-gate_act)) * up_act).astype(jnp.bfloat16)
    result = jnp.dot(inner_act, down_weights[0], preferred_element_type=jnp.float32)
    return result.astype(jnp.bfloat16)


def body(
    queries,
    cache_keys,
    cache_values,
    lengths,
    sinks,
    out_proj,
    decode_resid,
    prefill_hidden,
    norm_gain,
    router,
    routes,
    expert_gate,
    expert_up,
    expert_down,
):
    n_kv = lax.axis_size("kv")
    my_block = lax.axis_index("blk")
    per_block = queries.shape[0]
    head_count = sinks.shape[0]
    head_dim = cache_keys.shape[3]
    window = cache_keys.shape[1]
    grouped_q = queries.reshape(per_block, head_count, head_dim)
    key_rows = cache_keys[:, :, 0, :]
    value_rows = cache_values[:, :, 0, :]
    my_lengths = lax.dynamic_slice_in_dim(lengths, my_block * per_block, per_block)
    scores = jnp.einsum("rgd,rjd->rgj", grouped_q, key_rows, preferred_element_type=jnp.float32) * (
        1.0 / math.sqrt(head_dim)
    )
    first_valid = window - jnp.minimum(my_lengths, window)
    is_valid = (jnp.arange(window, dtype=jnp.int32)[None, :] >= first_valid[:, None])[:, None, :]
    masked = jnp.where(is_valid, scores, NEG_FILL)
    top_limit = jnp.maximum(jnp.max(masked, axis=2), sinks[None, :])
    weights = jnp.where(is_valid, jnp.exp(masked - top_limit[..., None]), 0.0)
    denominator = jnp.sum(weights, axis=2) + jnp.exp(sinks[None, :] - top_limit)
    numerator = jnp.einsum(
        "rgj,rjd->rgd", weights.astype(jnp.bfloat16), value_rows, preferred_element_type=jnp.float32
    )
    attended = (
        (numerator / denominator[..., None])
        .astype(jnp.bfloat16)
        .reshape(per_block, head_count * head_dim)
    )
    partial_proj = jnp.dot(attended, out_proj, preferred_element_type=jnp.float32)
    projected = kv_reduce(partial_proj, n_kv)
    decoded = (decode_resid.astype(jnp.float32) + projected).astype(jnp.bfloat16)
    hidden = jnp.concatenate([decoded, prefill_hidden[0]], axis=0)
    hidden_f = hidden.astype(jnp.float32)
    mean_sq = jnp.mean(hidden_f * hidden_f, axis=1, keepdims=True)
    normed = (hidden_f * lax.rsqrt(mean_sq + EPSILON) * norm_gain).astype(jnp.bfloat16)

    experts = router.shape[1]
    chosen_ids = routes[0]
    tokens, top_k = chosen_ids.shape
    model_width = hidden.shape[1]
    capacity = 16
    logits = jnp.dot(normed, router, preferred_element_type=jnp.float32)
    one_hot = chosen_ids[..., None] == jnp.arange(experts, dtype=jnp.int32)
    chosen = jnp.sum(jnp.where(one_hot, logits[:, None, :], 0.0), axis=2)
    gate_probs = jax.nn.softmax(chosen, axis=1)
    row_hot = jnp.any(one_hot, axis=1).astype(jnp.int32)
    earlier = jnp.cumsum(row_hot, axis=0) - row_hot
    slot_rank = jnp.sum(jnp.where(one_hot, earlier[:, None, :], 0), axis=2)
    rank_hot = slot_rank[..., None] == jnp.arange(capacity, dtype=jnp.int32)
    fills = one_hot[..., None] & rank_hot[:, :, None, :]
    place = jnp.any(fills, axis=1).reshape(tokens, experts * capacity).astype(jnp.bfloat16)
    outgoing = jnp.einsum("ts,td->sd", place, normed, preferred_element_type=jnp.float32)
    outgoing = outgoing.astype(jnp.bfloat16).reshape(experts, capacity, model_width)
    arrived = lax.all_to_all(outgoing, ("kv", "blk"), split_axis=0, concat_axis=0, tiled=True)
    processed = expert_block(
        arrived.reshape(experts * capacity, model_width), expert_gate, expert_up, expert_down
    )
    returned = lax.all_to_all(
        processed.reshape(experts, capacity, model_width),
        ("kv", "blk"),
        split_axis=0,
        concat_axis=0,
        tiled=True,
    ).reshape(experts * capacity, model_width)
    mix = jnp.sum(jnp.where(fills, gate_probs[..., None, None], 0.0), axis=1)
    mix = mix.reshape(tokens, experts * capacity)
    mix_hi = mix.astype(jnp.bfloat16)
    mix_lo = (mix - mix_hi.astype(jnp.float32)).astype(jnp.bfloat16)
    both = jnp.dot(
        jnp.concatenate([mix_hi, mix_lo], axis=0), returned, preferred_element_type=jnp.float32
    )
    combined = both[:tokens] + both[tokens:]
    layer_sum = (hidden_f + combined).astype(jnp.bfloat16)
    return layer_sum[None]


def solution(mesh):
    return jax.shard_map(
        body,
        mesh=mesh,
        in_specs=(
            P("blk", "kv"),
            P("blk", None, "kv", None),
            P("blk", None, "kv", None),
            P(),
            P("kv"),
            P("kv", None),
            P(("blk", "kv"), None),
            P(("blk", "kv"), None, None),
            P(),
            P(),
            P(("blk", "kv"), None, None),
            P(("kv", "blk"), None, None),
            P(("kv", "blk"), None, None),
            P(("kv", "blk"), None, None),
        ),
        out_specs=P(("blk", "kv"), None, None),
        check_vma=False,
    )
```

```python
import math

import jax
import jax.numpy as jnp
from jax import lax
from jax.experimental import pallas as pl
from jax.experimental.pallas import tpu as pltpu
from jax.sharding import PartitionSpec as P

NEG_FILL = -1e30
EPSILON = 1e-06
MESH = pl.DeviceIdType.MESH


def kv_reduce_kernel(n_kv, part_ref, out_ref, held, send_sem, recv_sem):
    me = lax.axis_index("kv")
    blk = lax.axis_index("blk")
    barrier = pltpu.get_barrier_semaphore()
    for step in range(1, n_kv):
        peer = lax.rem(me + step, n_kv)
        pl.semaphore_signal(barrier, inc=1, device_id=(peer, blk), device_id_type=MESH)
    pl.semaphore_wait(barrier, n_kv - 1)
    for step in range(1, n_kv):
        peer = lax.rem(me + step, n_kv)
        pltpu.make_async_remote_copy(
            src_ref=part_ref.at[peer],
            dst_ref=held.at[me],
            send_sem=send_sem.at[peer],
            recv_sem=recv_sem.at[me],
            device_id=(peer, blk),
            device_id_type=MESH,
        ).start()
    own = part_ref[me]
    for step in range(1, n_kv):
        peer = lax.rem(me + step, n_kv)
        arrival = pltpu.make_async_remote_copy(
            src_ref=part_ref.at[peer],
            dst_ref=held.at[peer],
            send_sem=send_sem.at[peer],
            recv_sem=recv_sem.at[peer],
            device_id=(peer, blk),
            device_id_type=MESH,
        )
        arrival.wait_send()
        arrival.wait_recv()
    total = own
    for step in range(1, n_kv):
        peer = lax.rem(me + step, n_kv)
        total = total + held[peer]
    out_ref[...] = total


def kv_reduce(partial, n_kv):
    rows, width = partial.shape
    return pl.pallas_call(
        lambda *refs: kv_reduce_kernel(n_kv, *refs),
        out_shape=jax.ShapeDtypeStruct((1, width), jnp.float32),
        in_specs=[pl.BlockSpec(memory_space=pltpu.VMEM)],
        out_specs=pl.BlockSpec(memory_space=pltpu.VMEM),
        scratch_shapes=[
            pltpu.VMEM((n_kv, 1, width), jnp.float32),
            pltpu.SemaphoreType.DMA((n_kv,)),
            pltpu.SemaphoreType.DMA((n_kv,)),
        ],
        compiler_params=pltpu.CompilerParams(collective_id=0, has_side_effects=True),
    )(partial.reshape(rows, 1, width))


def expert_block(slots, gate_weights, up_weights, down_weights):
    gate_act = jnp.dot(slots, gate_weights[0], preferred_element_type=jnp.float32)
    up_act = jnp.dot(slots, up_weights[0], preferred_element_type=jnp.float32)
    inner_act = (gate_act / (1.0 + jnp.exp(-gate_act)) * up_act).astype(jnp.bfloat16)
    result = jnp.dot(inner_act, down_weights[0], preferred_element_type=jnp.float32)
    return result.astype(jnp.bfloat16)


def body(
    queries,
    cache_keys,
    cache_values,
    lengths,
    sinks,
    out_proj,
    decode_resid,
    prefill_hidden,
    norm_gain,
    router,
    routes,
    expert_gate,
    expert_up,
    expert_down,
):
    n_kv = lax.axis_size("kv")
    my_block = lax.axis_index("blk")
    per_block = queries.shape[0]
    head_count = sinks.shape[0]
    head_dim = cache_keys.shape[3]
    window = cache_keys.shape[1]
    grouped_q = queries.reshape(per_block, head_count, head_dim)
    key_rows = cache_keys[:, :, 0, :]
    value_rows = cache_values[:, :, 0, :]
    my_lengths = lax.dynamic_slice_in_dim(lengths, my_block * per_block, per_block)
    scores = jnp.einsum("rgd,rjd->rgj", grouped_q, key_rows, preferred_element_type=jnp.float32) * (
        1.0 / math.sqrt(head_dim)
    )
    first_valid = window - jnp.minimum(my_lengths, window)
    is_valid = (jnp.arange(window, dtype=jnp.int32)[None, :] >= first_valid[:, None])[:, None, :]
    masked = jnp.where(is_valid, scores, NEG_FILL)
    top_limit = jnp.maximum(jnp.max(masked, axis=2), sinks[None, :])
    weights = jnp.where(is_valid, jnp.exp(masked - top_limit[..., None]), 0.0)
    denominator = jnp.sum(weights, axis=2) + jnp.exp(sinks[None, :] - top_limit)
    numerator = jnp.einsum(
        "rgj,rjd->rgd", weights.astype(jnp.bfloat16), value_rows, preferred_element_type=jnp.float32
    )
    attended = (
        (numerator / denominator[..., None])
        .astype(jnp.bfloat16)
        .reshape(per_block, head_count * head_dim)
    )
    partial_proj = jnp.dot(attended, out_proj, preferred_element_type=jnp.float32)
    projected = kv_reduce(partial_proj, n_kv)
    decoded = (decode_resid.astype(jnp.float32) + projected).astype(jnp.bfloat16)
    hidden = jnp.concatenate([decoded, prefill_hidden[0]], axis=0)
    hidden_f = hidden.astype(jnp.float32)
    mean_sq = jnp.mean(hidden_f * hidden_f, axis=1, keepdims=True)
    normed = (hidden_f * lax.rsqrt(mean_sq + EPSILON) * norm_gain).astype(jnp.bfloat16)

    experts = router.shape[1]
    chosen_ids = routes[0]
    tokens, top_k = chosen_ids.shape
    model_width = hidden.shape[1]
    capacity = 16
    logits = jnp.dot(normed, router, preferred_element_type=jnp.float32)
    one_hot = chosen_ids[..., None] == jnp.arange(experts, dtype=jnp.int32)
    chosen = jnp.sum(jnp.where(one_hot, logits[:, None, :], 0.0), axis=2)
    gate_probs = jax.nn.softmax(chosen, axis=1)
    row_hot = jnp.any(one_hot, axis=1).astype(jnp.int32)
    earlier = jnp.cumsum(row_hot, axis=0) - row_hot
    slot_rank = jnp.sum(jnp.where(one_hot, earlier[:, None, :], 0), axis=2)
    rank_hot = slot_rank[..., None] == jnp.arange(capacity, dtype=jnp.int32)
    fills = one_hot[..., None] & rank_hot[:, :, None, :]
    place = jnp.any(fills, axis=1).reshape(tokens, experts * capacity).astype(jnp.bfloat16)
    pieces = 2
    piece = model_width // pieces
    arrived = []
    for i in range(pieces):
        sent = jnp.einsum(
            "ts,td->sd",
            place,
            normed[:, i * piece : (i + 1) * piece],
            preferred_element_type=jnp.float32,
        ).astype(jnp.bfloat16)
        arrived.append(
            lax.all_to_all(
                sent.reshape(experts, capacity, piece),
                ("kv", "blk"),
                split_axis=0,
                concat_axis=0,
                tiled=True,
            ).reshape(experts * capacity, piece)
        )
    gate_w, up_w, down_w = expert_gate[0], expert_up[0], expert_down[0]
    gate_act = sum(
        jnp.dot(arrived[i], gate_w[i * piece : (i + 1) * piece], preferred_element_type=jnp.float32)
        for i in range(pieces)
    )
    up_act = sum(
        jnp.dot(arrived[i], up_w[i * piece : (i + 1) * piece], preferred_element_type=jnp.float32)
        for i in range(pieces)
    )
    inner_act = (gate_act / (1.0 + jnp.exp(-gate_act)) * up_act).astype(jnp.bfloat16)
    mix = jnp.sum(jnp.where(fills, gate_probs[..., None, None], 0.0), axis=1)
    mix = mix.reshape(tokens, experts * capacity)
    mix_hi = mix.astype(jnp.bfloat16)
    mix_lo = (mix - mix_hi.astype(jnp.float32)).astype(jnp.bfloat16)
    mix_both = jnp.concatenate([mix_hi, mix_lo], axis=0)
    combined_parts = []
    for i in range(pieces):
        processed = jnp.dot(
            inner_act, down_w[:, i * piece : (i + 1) * piece], preferred_element_type=jnp.float32
        ).astype(jnp.bfloat16)
        returned = lax.all_to_all(
            processed.reshape(experts, capacity, piece),
            ("kv", "blk"),
            split_axis=0,
            concat_axis=0,
            tiled=True,
        ).reshape(experts * capacity, piece)
        both = jnp.dot(mix_both, returned, preferred_element_type=jnp.float32)
        combined_parts.append(both[:tokens] + both[tokens:])
    combined = jnp.concatenate(combined_parts, axis=1)
    layer_sum = (hidden_f + combined).astype(jnp.bfloat16)
    return layer_sum[None]


def solution(mesh):
    return jax.shard_map(
        body,
        mesh=mesh,
        in_specs=(
            P("blk", "kv"),
            P("blk", None, "kv", None),
            P("blk", None, "kv", None),
            P(),
            P("kv"),
            P("kv", None),
            P(("blk", "kv"), None),
            P(("blk", "kv"), None, None),
            P(),
            P(),
            P(("blk", "kv"), None, None),
            P(("kv", "blk"), None, None),
            P(("kv", "blk"), None, None),
            P(("kv", "blk"), None, None),
        ),
        out_specs=P(("blk", "kv"), None, None),
        check_vma=False,
    )
```

```python
import math

import jax
import jax.numpy as jnp
from jax import lax
from jax.experimental import pallas as pl
from jax.experimental.pallas import tpu as pltpu
from jax.sharding import PartitionSpec as P

NEG_FILL = -1e30
EPSILON = 1e-06
MESH = pl.DeviceIdType.MESH


def kv_reduce_kernel(n_kv, part_ref, out_ref, held, send_sem, recv_sem):
    me = lax.axis_index("kv")
    blk = lax.axis_index("blk")
    barrier = pltpu.get_barrier_semaphore()
    for step in range(1, n_kv):
        peer = lax.rem(me + step, n_kv)
        pl.semaphore_signal(barrier, inc=1, device_id=(peer, blk), device_id_type=MESH)
    pl.semaphore_wait(barrier, n_kv - 1)
    for step in range(1, n_kv):
        peer = lax.rem(me + step, n_kv)
        pltpu.make_async_remote_copy(
            src_ref=part_ref.at[peer],
            dst_ref=held.at[me],
            send_sem=send_sem.at[peer],
            recv_sem=recv_sem.at[me],
            device_id=(peer, blk),
            device_id_type=MESH,
        ).start()
    own = part_ref[me]
    for step in range(1, n_kv):
        peer = lax.rem(me + step, n_kv)
        arrival = pltpu.make_async_remote_copy(
            src_ref=part_ref.at[peer],
            dst_ref=held.at[peer],
            send_sem=send_sem.at[peer],
            recv_sem=recv_sem.at[peer],
            device_id=(peer, blk),
            device_id_type=MESH,
        )
        arrival.wait_send()
        arrival.wait_recv()
    total = own
    for step in range(1, n_kv):
        peer = lax.rem(me + step, n_kv)
        total = total + held[peer]
    out_ref[...] = total


def kv_reduce(partial, n_kv):
    rows, width = partial.shape
    return pl.pallas_call(
        lambda *refs: kv_reduce_kernel(n_kv, *refs),
        out_shape=jax.ShapeDtypeStruct((1, width), jnp.float32),
        in_specs=[pl.BlockSpec(memory_space=pltpu.VMEM)],
        out_specs=pl.BlockSpec(memory_space=pltpu.VMEM),
        scratch_shapes=[
            pltpu.VMEM((n_kv, 1, width), jnp.float32),
            pltpu.SemaphoreType.DMA((n_kv,)),
            pltpu.SemaphoreType.DMA((n_kv,)),
        ],
        compiler_params=pltpu.CompilerParams(collective_id=0, has_side_effects=True),
    )(partial.reshape(rows, 1, width))


def expert_block(slots, gate_weights, up_weights, down_weights):
    gate_act = jnp.dot(slots, gate_weights[0], preferred_element_type=jnp.float32)
    up_act = jnp.dot(slots, up_weights[0], preferred_element_type=jnp.float32)
    inner_act = (gate_act / (1.0 + jnp.exp(-gate_act)) * up_act).astype(jnp.bfloat16)
    result = jnp.dot(inner_act, down_weights[0], preferred_element_type=jnp.float32)
    return result.astype(jnp.bfloat16)


def body(
    queries,
    cache_keys,
    cache_values,
    lengths,
    sinks,
    out_proj,
    decode_resid,
    prefill_hidden,
    norm_gain,
    router,
    routes,
    expert_gate,
    expert_up,
    expert_down,
):
    n_kv = lax.axis_size("kv")
    my_block = lax.axis_index("blk")
    per_block = queries.shape[0]
    head_count = sinks.shape[0]
    head_dim = cache_keys.shape[3]
    window = cache_keys.shape[1]
    grouped_q = queries.reshape(per_block, head_count, head_dim)
    key_rows = cache_keys[:, :, 0, :]
    value_rows = cache_values[:, :, 0, :]
    my_lengths = lax.dynamic_slice_in_dim(lengths, my_block * per_block, per_block)
    scores = jnp.einsum("rgd,rjd->rgj", grouped_q, key_rows, preferred_element_type=jnp.float32) * (
        1.0 / math.sqrt(head_dim)
    )
    first_valid = window - jnp.minimum(my_lengths, window)
    is_valid = (jnp.arange(window, dtype=jnp.int32)[None, :] >= first_valid[:, None])[:, None, :]
    masked = jnp.where(is_valid, scores, NEG_FILL)
    top_limit = jnp.maximum(jnp.max(masked, axis=2), sinks[None, :])
    weights = jnp.where(is_valid, jnp.exp(masked - top_limit[..., None]), 0.0)
    denominator = jnp.sum(weights, axis=2) + jnp.exp(sinks[None, :] - top_limit)
    numerator = jnp.einsum(
        "rgj,rjd->rgd", weights.astype(jnp.bfloat16), value_rows, preferred_element_type=jnp.float32
    )
    attended = (
        (numerator / denominator[..., None])
        .astype(jnp.bfloat16)
        .reshape(per_block, head_count * head_dim)
    )
    partial_proj = jnp.dot(attended, out_proj, preferred_element_type=jnp.float32)
    projected = kv_reduce(partial_proj, n_kv)
    decoded = (decode_resid.astype(jnp.float32) + projected).astype(jnp.bfloat16)
    hidden = jnp.concatenate([decoded, prefill_hidden[0]], axis=0)
    hidden_f = hidden.astype(jnp.float32)
    mean_sq = jnp.mean(hidden_f * hidden_f, axis=1, keepdims=True)
    normed = (hidden_f * lax.rsqrt(mean_sq + EPSILON) * norm_gain).astype(jnp.bfloat16)

    experts = router.shape[1]
    chosen_ids = routes[0]
    tokens, top_k = chosen_ids.shape
    model_width = hidden.shape[1]
    capacity = 16
    logits = jnp.dot(normed, router, preferred_element_type=jnp.float32)
    one_hot = chosen_ids[..., None] == jnp.arange(experts, dtype=jnp.int32)
    chosen = jnp.sum(jnp.where(one_hot, logits[:, None, :], 0.0), axis=2)
    gate_probs = jax.nn.softmax(chosen, axis=1)
    row_hot = jnp.any(one_hot, axis=1).astype(jnp.int32)
    earlier = jnp.cumsum(row_hot, axis=0) - row_hot
    slot_rank = jnp.sum(jnp.where(one_hot, earlier[:, None, :], 0), axis=2)
    slot_id = chosen_ids * capacity + slot_rank
    slot_iota = jnp.arange(experts * capacity, dtype=jnp.int32)
    place_t = jnp.any(
        slot_id[None, :, :] == slot_iota[:, None, None], axis=2
    ).astype(jnp.bfloat16)
    outgoing = jnp.dot(place_t, normed, preferred_element_type=jnp.float32)
    outgoing = outgoing.astype(jnp.bfloat16).reshape(experts, capacity, model_width)
    arrived = lax.all_to_all(outgoing, ("kv", "blk"), split_axis=0, concat_axis=0, tiled=True)
    processed = expert_block(
        arrived.reshape(experts * capacity, model_width), expert_gate, expert_up, expert_down
    )
    returned = lax.all_to_all(
        processed.reshape(experts, capacity, model_width),
        ("kv", "blk"),
        split_axis=0,
        concat_axis=0,
        tiled=True,
    ).reshape(experts * capacity, model_width)
    mix = jnp.sum(
        jnp.where(slot_id[:, :, None] == slot_iota[None, None, :], gate_probs[..., None], 0.0),
        axis=1,
    )
    mix_hi = mix.astype(jnp.bfloat16)
    mix_lo = (mix - mix_hi.astype(jnp.float32)).astype(jnp.bfloat16)
    both = jnp.dot(
        jnp.concatenate([mix_hi, mix_lo], axis=0), returned, preferred_element_type=jnp.float32
    )
    combined = both[:tokens] + both[tokens:]
    layer_sum = (hidden_f + combined).astype(jnp.bfloat16)
    return layer_sum[None]


def solution(mesh):
    return jax.shard_map(
        body,
        mesh=mesh,
        in_specs=(
            P("blk", "kv"),
            P("blk", None, "kv", None),
            P("blk", None, "kv", None),
            P(),
            P("kv"),
            P("kv", None),
            P(("blk", "kv"), None),
            P(("blk", "kv"), None, None),
            P(),
            P(),
            P(("blk", "kv"), None, None),
            P(("kv", "blk"), None, None),
            P(("kv", "blk"), None, None),
            P(("kv", "blk"), None, None),
        ),
        out_specs=P(("blk", "kv"), None, None),
        check_vma=False,
    )
```

```python
import math

import jax
import jax.numpy as jnp
from jax import lax
from jax.experimental import pallas as pl
from jax.experimental.pallas import tpu as pltpu
from jax.sharding import PartitionSpec as P

NEG_FILL = -1e30
EPSILON = 1e-06
MESH = pl.DeviceIdType.MESH


def attend_reduce_kernel(
    n_kv, q_ref, k_ref, v_ref, first_ref, sink_ref, proj_ref, out_ref, att, part, held, send_sem, recv_sem
):
    me = lax.axis_index("kv")
    blk = lax.axis_index("blk")
    barrier = pltpu.get_barrier_semaphore()
    for step in range(1, n_kv):
        peer = lax.rem(me + step, n_kv)
        pl.semaphore_signal(barrier, inc=1, device_id=(peer, blk), device_id_type=MESH)
    requests, heads, head_dim = q_ref.shape
    window = k_ref.shape[1]
    scale = 1.0 / math.sqrt(head_dim)
    sink = sink_ref[...]
    positions = lax.broadcasted_iota(jnp.int32, (heads, window), 1)
    for r in range(requests):
        scores = lax.dot_general(
            q_ref[r], k_ref[r], (((1,), (1,)), ((), ())), preferred_element_type=jnp.float32
        ) * scale
        valid = positions >= first_ref[pl.ds(r, 1), :]
        masked = jnp.where(valid, scores, NEG_FILL)
        top = jnp.maximum(jnp.max(masked, axis=1, keepdims=True), sink)
        weights = jnp.where(valid, jnp.exp(masked - top), 0.0)
        denominator = jnp.sum(weights, axis=1, keepdims=True) + jnp.exp(sink - top)
        numerator = jnp.dot(
            weights.astype(jnp.bfloat16), v_ref[r], preferred_element_type=jnp.float32
        )
        att[:, pl.ds(r, 1), :] = (numerator / denominator).astype(jnp.bfloat16).astype(
            jnp.float32
        )[:, None, :]
    total = jnp.zeros((requests, proj_ref.shape[1]), jnp.float32)
    for h in range(heads):
        total = total + jnp.dot(
            att[h].astype(jnp.bfloat16),
            proj_ref[pl.ds(h * head_dim, head_dim), :],
            preferred_element_type=jnp.float32,
        )
    part[...] = total[:, None, :]
    pl.semaphore_wait(barrier, n_kv - 1)
    for step in range(1, n_kv):
        peer = lax.rem(me + step, n_kv)
        pltpu.make_async_remote_copy(
            src_ref=part.at[peer],
            dst_ref=held.at[me],
            send_sem=send_sem.at[peer],
            recv_sem=recv_sem.at[me],
            device_id=(peer, blk),
            device_id_type=MESH,
        ).start()
    own = part[me]
    for step in range(1, n_kv):
        peer = lax.rem(me + step, n_kv)
        arrival = pltpu.make_async_remote_copy(
            src_ref=part.at[peer],
            dst_ref=held.at[peer],
            send_sem=send_sem.at[peer],
            recv_sem=recv_sem.at[peer],
            device_id=(peer, blk),
            device_id_type=MESH,
        )
        arrival.wait_send()
        arrival.wait_recv()
    for step in range(1, n_kv):
        peer = lax.rem(me + step, n_kv)
        own = own + held[peer]
    out_ref[...] = own


def attend_reduce(queries, keys, values, first_valid, sinks, out_proj, n_kv):
    requests = queries.shape[0]
    heads = sinks.shape[0]
    head_dim = keys.shape[2]
    width = out_proj.shape[1]
    return pl.pallas_call(
        lambda *refs: attend_reduce_kernel(n_kv, *refs),
        out_shape=jax.ShapeDtypeStruct((1, width), jnp.float32),
        in_specs=[pl.BlockSpec(memory_space=pltpu.VMEM)] * 6,
        out_specs=pl.BlockSpec(memory_space=pltpu.VMEM),
        scratch_shapes=[
            pltpu.VMEM((heads, requests, head_dim), jnp.float32),
            pltpu.VMEM((requests, 1, width), jnp.float32),
            pltpu.VMEM((n_kv, 1, width), jnp.float32),
            pltpu.SemaphoreType.DMA((n_kv,)),
            pltpu.SemaphoreType.DMA((n_kv,)),
        ],
        compiler_params=pltpu.CompilerParams(
            collective_id=0, has_side_effects=True, vmem_limit_bytes=48 * 1024 * 1024
        ),
    )(
        queries.reshape(requests, heads, head_dim),
        keys,
        values,
        first_valid.reshape(requests, 1),
        sinks.reshape(heads, 1),
        out_proj,
    )


def expert_block(slots, gate_weights, up_weights, down_weights):
    gate_act = jnp.dot(slots, gate_weights[0], preferred_element_type=jnp.float32)
    up_act = jnp.dot(slots, up_weights[0], preferred_element_type=jnp.float32)
    inner_act = (gate_act / (1.0 + jnp.exp(-gate_act)) * up_act).astype(jnp.bfloat16)
    result = jnp.dot(inner_act, down_weights[0], preferred_element_type=jnp.float32)
    return result.astype(jnp.bfloat16)


def body(
    queries,
    cache_keys,
    cache_values,
    lengths,
    sinks,
    out_proj,
    decode_resid,
    prefill_hidden,
    norm_gain,
    router,
    routes,
    expert_gate,
    expert_up,
    expert_down,
):
    n_kv = lax.axis_size("kv")
    my_block = lax.axis_index("blk")
    per_block = queries.shape[0]
    head_count = sinks.shape[0]
    head_dim = cache_keys.shape[3]
    window = cache_keys.shape[1]
    my_lengths = lax.dynamic_slice_in_dim(lengths, my_block * per_block, per_block)
    first_valid = window - jnp.minimum(my_lengths, window)
    projected = attend_reduce(
        queries,
        cache_keys[:, :, 0, :],
        cache_values[:, :, 0, :],
        first_valid,
        sinks,
        out_proj,
        n_kv,
    )
    decoded = (decode_resid.astype(jnp.float32) + projected).astype(jnp.bfloat16)
    hidden = jnp.concatenate([decoded, prefill_hidden[0]], axis=0)
    hidden_f = hidden.astype(jnp.float32)
    mean_sq = jnp.mean(hidden_f * hidden_f, axis=1, keepdims=True)
    normed = (hidden_f * lax.rsqrt(mean_sq + EPSILON) * norm_gain).astype(jnp.bfloat16)

    experts = router.shape[1]
    chosen_ids = routes[0]
    tokens, top_k = chosen_ids.shape
    model_width = hidden.shape[1]
    capacity = 16
    logits = jnp.dot(normed, router, preferred_element_type=jnp.float32)
    one_hot = chosen_ids[..., None] == jnp.arange(experts, dtype=jnp.int32)
    chosen = jnp.sum(jnp.where(one_hot, logits[:, None, :], 0.0), axis=2)
    gate_probs = jax.nn.softmax(chosen, axis=1)
    row_hot = jnp.any(one_hot, axis=1).astype(jnp.int32)
    earlier = jnp.cumsum(row_hot, axis=0) - row_hot
    slot_rank = jnp.sum(jnp.where(one_hot, earlier[:, None, :], 0), axis=2)
    rank_hot = slot_rank[..., None] == jnp.arange(capacity, dtype=jnp.int32)
    fills = one_hot[..., None] & rank_hot[:, :, None, :]
    place = jnp.any(fills, axis=1).reshape(tokens, experts * capacity).astype(jnp.bfloat16)
    outgoing = jnp.einsum("ts,td->sd", place, normed, preferred_element_type=jnp.float32)
    outgoing = outgoing.astype(jnp.bfloat16).reshape(experts, capacity, model_width)
    arrived = lax.all_to_all(outgoing, ("kv", "blk"), split_axis=0, concat_axis=0, tiled=True)
    processed = expert_block(
        arrived.reshape(experts * capacity, model_width), expert_gate, expert_up, expert_down
    )
    returned = lax.all_to_all(
        processed.reshape(experts, capacity, model_width),
        ("kv", "blk"),
        split_axis=0,
        concat_axis=0,
        tiled=True,
    ).reshape(experts * capacity, model_width)
    mix = jnp.sum(jnp.where(fills, gate_probs[..., None, None], 0.0), axis=1)
    mix = mix.reshape(tokens, experts * capacity)
    mix_hi = mix.astype(jnp.bfloat16)
    mix_lo = (mix - mix_hi.astype(jnp.float32)).astype(jnp.bfloat16)
    both = jnp.dot(
        jnp.concatenate([mix_hi, mix_lo], axis=0), returned, preferred_element_type=jnp.float32
    )
    combined = both[:tokens] + both[tokens:]
    layer_sum = (hidden_f + combined).astype(jnp.bfloat16)
    return layer_sum[None]


def solution(mesh):
    return jax.shard_map(
        body,
        mesh=mesh,
        in_specs=(
            P("blk", "kv"),
            P("blk", None, "kv", None),
            P("blk", None, "kv", None),
            P(),
            P("kv"),
            P("kv", None),
            P(("blk", "kv"), None),
            P(("blk", "kv"), None, None),
            P(),
            P(),
            P(("blk", "kv"), None, None),
            P(("kv", "blk"), None, None),
            P(("kv", "blk"), None, None),
            P(("kv", "blk"), None, None),
        ),
        out_specs=P(("blk", "kv"), None, None),
        check_vma=False,
    )
```

```python
import math

import jax
import jax.numpy as jnp
from jax import lax
from jax.experimental import pallas as pl
from jax.experimental.pallas import tpu as pltpu
from jax.sharding import PartitionSpec as P

NEG_FILL = -1e30
EPSILON = 1e-06
MESH = pl.DeviceIdType.MESH


def attend_reduce_kernel(
    n_kv, q_ref, k_ref, v_ref, first_ref, sink_ref, proj_ref, out_ref, att, part, held, send_sem, recv_sem
):
    me = lax.axis_index("kv")
    blk = lax.axis_index("blk")
    barrier = pltpu.get_barrier_semaphore()
    for step in range(1, n_kv):
        peer = lax.rem(me + step, n_kv)
        pl.semaphore_signal(barrier, inc=1, device_id=(peer, blk), device_id_type=MESH)
    requests, heads, head_dim = q_ref.shape
    window = k_ref.shape[1]
    scale = 1.0 / math.sqrt(head_dim)
    sink = sink_ref[...]
    positions = lax.broadcasted_iota(jnp.int32, (heads, window), 1)
    for r in range(requests):
        scores = lax.dot_general(
            q_ref[r], k_ref[r], (((1,), (1,)), ((), ())), preferred_element_type=jnp.float32
        ) * scale
        valid = positions >= first_ref[pl.ds(r, 1), :]
        masked = jnp.where(valid, scores, NEG_FILL)
        top = jnp.maximum(jnp.max(masked, axis=1, keepdims=True), sink)
        weights = jnp.where(valid, jnp.exp(masked - top), 0.0)
        denominator = jnp.sum(weights, axis=1, keepdims=True) + jnp.exp(sink - top)
        numerator = jnp.dot(
            weights.astype(jnp.bfloat16), v_ref[r], preferred_element_type=jnp.float32
        )
        att[:, pl.ds(r, 1), :] = (numerator / denominator).astype(jnp.bfloat16).astype(
            jnp.float32
        )[:, None, :]
    total = jnp.zeros((requests, proj_ref.shape[1]), jnp.float32)
    for h in range(heads):
        total = total + jnp.dot(
            att[h].astype(jnp.bfloat16),
            proj_ref[pl.ds(h * head_dim, head_dim), :],
            preferred_element_type=jnp.float32,
        )
    part[...] = total[:, None, :]
    pl.semaphore_wait(barrier, n_kv - 1)
    for step in range(1, n_kv):
        peer = lax.rem(me + step, n_kv)
        pltpu.make_async_remote_copy(
            src_ref=part.at[peer],
            dst_ref=held.at[me],
            send_sem=send_sem.at[peer],
            recv_sem=recv_sem.at[me],
            device_id=(peer, blk),
            device_id_type=MESH,
        ).start()
    own = part[me]
    for step in range(1, n_kv):
        peer = lax.rem(me + step, n_kv)
        arrival = pltpu.make_async_remote_copy(
            src_ref=part.at[peer],
            dst_ref=held.at[peer],
            send_sem=send_sem.at[peer],
            recv_sem=recv_sem.at[peer],
            device_id=(peer, blk),
            device_id_type=MESH,
        )
        arrival.wait_send()
        arrival.wait_recv()
    for step in range(1, n_kv):
        peer = lax.rem(me + step, n_kv)
        own = own + held[peer]
    out_ref[...] = own


def attend_reduce(queries, keys, values, first_valid, sinks, out_proj, n_kv):
    requests = queries.shape[0]
    heads = sinks.shape[0]
    head_dim = keys.shape[2]
    width = out_proj.shape[1]
    return pl.pallas_call(
        lambda *refs: attend_reduce_kernel(n_kv, *refs),
        out_shape=jax.ShapeDtypeStruct((1, width), jnp.float32),
        in_specs=[pl.BlockSpec(memory_space=pltpu.VMEM)] * 6,
        out_specs=pl.BlockSpec(memory_space=pltpu.VMEM),
        scratch_shapes=[
            pltpu.VMEM((heads, requests, head_dim), jnp.float32),
            pltpu.VMEM((requests, 1, width), jnp.float32),
            pltpu.VMEM((n_kv, 1, width), jnp.float32),
            pltpu.SemaphoreType.DMA((n_kv,)),
            pltpu.SemaphoreType.DMA((n_kv,)),
        ],
        compiler_params=pltpu.CompilerParams(
            collective_id=0, has_side_effects=True, vmem_limit_bytes=48 * 1024 * 1024
        ),
    )(
        queries.reshape(requests, heads, head_dim),
        keys,
        values,
        first_valid.reshape(requests, 1),
        sinks.reshape(heads, 1),
        out_proj,
    )


LANE = 256
TILE = 256
SLOT_STRIDE = 16


def _wire_shape(width, used):
    return ((width // LANE) * used, LANE)


def dispatch_kernel(used, place_ref, rows_ref, out_ref, staged):
    chunks = out_ref.shape[0]
    pieces = rows_ref.shape[1] // LANE
    for q in range(pieces):
        staged[...] = jnp.dot(
            place_ref[...], rows_ref[:, pl.ds(q * LANE, LANE)], preferred_element_type=jnp.float32
        )

        def put(e, carry, q=q):
            start = pl.multiple_of(e * SLOT_STRIDE, SLOT_STRIDE)
            out_ref[e, pl.ds(q * used, used), :] = staged[pl.ds(start, used), :].astype(
                out_ref.dtype
            )
            return carry

        lax.fori_loop(0, chunks, put, 0)


def dispatch(place_t, rows, used):
    slots = place_t.shape[0]
    width = rows.shape[1]
    chunks = slots // SLOT_STRIDE
    return pl.pallas_call(
        lambda *refs: dispatch_kernel(used, *refs),
        out_shape=jax.ShapeDtypeStruct((chunks,) + _wire_shape(width, used), jnp.bfloat16),
        in_specs=[pl.BlockSpec(memory_space=pltpu.VMEM)] * 2,
        out_specs=pl.BlockSpec(memory_space=pltpu.VMEM),
        scratch_shapes=[pltpu.VMEM((slots, LANE), jnp.float32)],
        compiler_params=pltpu.CompilerParams(vmem_limit_bytes=48 * 1024 * 1024),
    )(place_t, rows)


def expert_kernel(x_ref, gate_ref, up_ref, down_ref, out_ref, rows_in, rows_out):
    chunks, wire_rows, _ = x_ref.shape
    width = gate_ref.shape[0]
    pieces = width // LANE
    used = wire_rows // pieces
    group = TILE // SLOT_STRIDE
    rows_in[...] = jnp.zeros(rows_in.shape, rows_in.dtype)

    def tile(i, carry):
        for jl in range(group):
            j = i * group + jl
            for q in range(pieces):
                rows_in[pl.ds(jl * SLOT_STRIDE, used), pl.ds(q * LANE, LANE)] = x_ref[
                    j, pl.ds(q * used, used), :
                ]
        rows = rows_in[...]
        gate_act = jnp.dot(rows, gate_ref[...], preferred_element_type=jnp.float32)
        up_act = jnp.dot(rows, up_ref[...], preferred_element_type=jnp.float32)
        inner_act = (gate_act / (1.0 + jnp.exp(-gate_act)) * up_act).astype(jnp.bfloat16)
        rows_out[...] = jnp.dot(
            inner_act, down_ref[...], preferred_element_type=jnp.float32
        ).astype(rows_out.dtype)
        for jl in range(group):
            j = i * group + jl
            for q in range(pieces):
                out_ref[j, pl.ds(q * used, used), :] = rows_out[
                    pl.ds(jl * SLOT_STRIDE, used), pl.ds(q * LANE, LANE)
                ]
        return carry

    lax.fori_loop(0, chunks // group, tile, 0)


def expert_block(arrived, gate_weights, up_weights, down_weights):
    width = gate_weights.shape[1]
    return pl.pallas_call(
        expert_kernel,
        out_shape=jax.ShapeDtypeStruct(arrived.shape, jnp.bfloat16),
        in_specs=[pl.BlockSpec(memory_space=pltpu.VMEM)] * 4,
        out_specs=pl.BlockSpec(memory_space=pltpu.VMEM),
        scratch_shapes=[
            pltpu.VMEM((TILE, width), jnp.bfloat16),
            pltpu.VMEM((TILE, width), jnp.bfloat16),
        ],
        compiler_params=pltpu.CompilerParams(vmem_limit_bytes=60 * 1024 * 1024),
    )(arrived, gate_weights[0], up_weights[0], down_weights[0])


def combine_kernel(ret_ref, mix_ref, hidden_ref, out_ref, rows):
    chunks, wire_rows, _ = ret_ref.shape
    width = rows.shape[1]
    pieces = width // LANE
    used = wire_rows // pieces
    tokens = hidden_ref.shape[0]
    rows[...] = jnp.zeros(rows.shape, rows.dtype)

    def fill(e, carry):
        start = pl.multiple_of(e * SLOT_STRIDE, SLOT_STRIDE)
        for q in range(pieces):
            rows[pl.ds(start, used), pl.ds(q * LANE, LANE)] = ret_ref[e, pl.ds(q * used, used), :]
        return carry

    lax.fori_loop(0, chunks, fill, 0)
    both = jnp.dot(mix_ref[...], rows[...], preferred_element_type=jnp.float32)
    out_ref[...] = (
        hidden_ref[...].astype(jnp.float32) + both[:tokens] + both[tokens:]
    ).astype(out_ref.dtype)


def combine(returned, mix_both, hidden):
    chunks = returned.shape[0]
    width = hidden.shape[1]
    return pl.pallas_call(
        combine_kernel,
        out_shape=jax.ShapeDtypeStruct(hidden.shape, jnp.bfloat16),
        in_specs=[pl.BlockSpec(memory_space=pltpu.VMEM)] * 3,
        out_specs=pl.BlockSpec(memory_space=pltpu.VMEM),
        scratch_shapes=[pltpu.VMEM((chunks * SLOT_STRIDE, width), jnp.bfloat16)],
        compiler_params=pltpu.CompilerParams(vmem_limit_bytes=48 * 1024 * 1024),
    )(returned, mix_both, hidden)


def body(
    queries,
    cache_keys,
    cache_values,
    lengths,
    sinks,
    out_proj,
    decode_resid,
    prefill_hidden,
    norm_gain,
    router,
    routes,
    expert_gate,
    expert_up,
    expert_down,
):
    n_kv = lax.axis_size("kv")
    my_block = lax.axis_index("blk")
    per_block = queries.shape[0]
    head_count = sinks.shape[0]
    head_dim = cache_keys.shape[3]
    window = cache_keys.shape[1]
    my_lengths = lax.dynamic_slice_in_dim(lengths, my_block * per_block, per_block)
    first_valid = window - jnp.minimum(my_lengths, window)
    projected = attend_reduce(
        queries,
        cache_keys[:, :, 0, :],
        cache_values[:, :, 0, :],
        first_valid,
        sinks,
        out_proj,
        n_kv,
    )
    decoded = (decode_resid.astype(jnp.float32) + projected).astype(jnp.bfloat16)
    hidden = jnp.concatenate([decoded, prefill_hidden[0]], axis=0)
    hidden_f = hidden.astype(jnp.float32)
    mean_sq = jnp.mean(hidden_f * hidden_f, axis=1, keepdims=True)
    normed = (hidden_f * lax.rsqrt(mean_sq + EPSILON) * norm_gain).astype(jnp.bfloat16)

    experts = router.shape[1]
    chosen_ids = routes[0]
    tokens, top_k = chosen_ids.shape
    model_width = hidden.shape[1]
    capacity = 16
    logits = jnp.dot(normed, router, preferred_element_type=jnp.float32)
    one_hot = chosen_ids[..., None] == jnp.arange(experts, dtype=jnp.int32)
    chosen = jnp.sum(jnp.where(one_hot, logits[:, None, :], 0.0), axis=2)
    gate_probs = jax.nn.softmax(chosen, axis=1)
    row_hot = jnp.any(one_hot, axis=1).astype(jnp.int32)
    earlier = jnp.cumsum(row_hot, axis=0) - row_hot
    slot_rank = jnp.sum(jnp.where(one_hot, earlier[:, None, :], 0), axis=2)
    rank_hot = slot_rank[..., None] == jnp.arange(capacity, dtype=jnp.int32)
    fills = one_hot[..., None] & rank_hot[:, :, None, :]
    place = jnp.any(fills, axis=1).reshape(tokens, experts * capacity).astype(jnp.bfloat16)
    outgoing = dispatch(place.T, normed, 14)
    arrived = lax.all_to_all(outgoing, ("kv", "blk"), split_axis=0, concat_axis=0, tiled=True)
    processed = expert_block(arrived, expert_gate, expert_up, expert_down)
    returned = lax.all_to_all(processed, ("kv", "blk"), split_axis=0, concat_axis=0, tiled=True)
    mix = jnp.sum(jnp.where(fills, gate_probs[..., None, None], 0.0), axis=1)
    mix = mix.reshape(tokens, experts * capacity)
    mix_hi = mix.astype(jnp.bfloat16)
    mix_lo = (mix - mix_hi.astype(jnp.float32)).astype(jnp.bfloat16)
    layer_sum = combine(returned, jnp.concatenate([mix_hi, mix_lo], axis=0), hidden)
    return layer_sum[None]


def solution(mesh):
    return jax.shard_map(
        body,
        mesh=mesh,
        in_specs=(
            P("blk", "kv"),
            P("blk", None, "kv", None),
            P("blk", None, "kv", None),
            P(),
            P("kv"),
            P("kv", None),
            P(("blk", "kv"), None),
            P(("blk", "kv"), None, None),
            P(),
            P(),
            P(("blk", "kv"), None, None),
            P(("kv", "blk"), None, None),
            P(("kv", "blk"), None, None),
            P(("kv", "blk"), None, None),
        ),
        out_specs=P(("blk", "kv"), None, None),
        check_vma=False,
    )
```

```python
import math

import jax
import jax.numpy as jnp
from jax import lax
from jax.experimental import pallas as pl
from jax.experimental.pallas import tpu as pltpu
from jax.sharding import PartitionSpec as P

NEG_FILL = -1e30
EPSILON = 1e-06
MESH = pl.DeviceIdType.MESH


def attend_reduce_kernel(
    n_kv, q_ref, k_ref, v_ref, first_ref, sink_ref, proj_ref, out_ref, att, part, held, send_sem, recv_sem
):
    me = lax.axis_index("kv")
    blk = lax.axis_index("blk")
    barrier = pltpu.get_barrier_semaphore()
    for step in range(1, n_kv):
        peer = lax.rem(me + step, n_kv)
        pl.semaphore_signal(barrier, inc=1, device_id=(peer, blk), device_id_type=MESH)
    requests, heads, head_dim = q_ref.shape
    window = k_ref.shape[1]
    scale = 1.0 / math.sqrt(head_dim)
    sink = sink_ref[...]
    positions = lax.broadcasted_iota(jnp.int32, (heads, window), 1)
    for r in range(requests):
        scores = lax.dot_general(
            q_ref[r], k_ref[r], (((1,), (1,)), ((), ())), preferred_element_type=jnp.float32
        ) * scale
        valid = positions >= first_ref[pl.ds(r, 1), :]
        masked = jnp.where(valid, scores, NEG_FILL)
        top = jnp.maximum(jnp.max(masked, axis=1, keepdims=True), sink)
        weights = jnp.where(valid, jnp.exp(masked - top), 0.0)
        denominator = jnp.sum(weights, axis=1, keepdims=True) + jnp.exp(sink - top)
        numerator = jnp.dot(
            weights.astype(jnp.bfloat16), v_ref[r], preferred_element_type=jnp.float32
        )
        att[:, pl.ds(r, 1), :] = (numerator / denominator).astype(jnp.bfloat16).astype(
            jnp.float32
        )[:, None, :]
    total = jnp.zeros((requests, proj_ref.shape[1]), jnp.float32)
    for h in range(heads):
        total = total + jnp.dot(
            att[h].astype(jnp.bfloat16),
            proj_ref[pl.ds(h * head_dim, head_dim), :],
            preferred_element_type=jnp.float32,
        )
    part[...] = total[:, None, :]
    pl.semaphore_wait(barrier, n_kv - 1)
    for step in range(1, n_kv):
        peer = lax.rem(me + step, n_kv)
        pltpu.make_async_remote_copy(
            src_ref=part.at[peer],
            dst_ref=held.at[me],
            send_sem=send_sem.at[peer],
            recv_sem=recv_sem.at[me],
            device_id=(peer, blk),
            device_id_type=MESH,
        ).start()
    own = part[me]
    for step in range(1, n_kv):
        peer = lax.rem(me + step, n_kv)
        arrival = pltpu.make_async_remote_copy(
            src_ref=part.at[peer],
            dst_ref=held.at[peer],
            send_sem=send_sem.at[peer],
            recv_sem=recv_sem.at[peer],
            device_id=(peer, blk),
            device_id_type=MESH,
        )
        arrival.wait_send()
        arrival.wait_recv()
    for step in range(1, n_kv):
        peer = lax.rem(me + step, n_kv)
        own = own + held[peer]
    out_ref[...] = own


def attend_reduce(queries, keys, values, first_valid, sinks, out_proj, n_kv):
    requests = queries.shape[0]
    heads = sinks.shape[0]
    head_dim = keys.shape[2]
    width = out_proj.shape[1]
    return pl.pallas_call(
        lambda *refs: attend_reduce_kernel(n_kv, *refs),
        out_shape=jax.ShapeDtypeStruct((1, width), jnp.float32),
        in_specs=[pl.BlockSpec(memory_space=pltpu.VMEM)] * 6,
        out_specs=pl.BlockSpec(memory_space=pltpu.VMEM),
        scratch_shapes=[
            pltpu.VMEM((heads, requests, head_dim), jnp.float32),
            pltpu.VMEM((requests, 1, width), jnp.float32),
            pltpu.VMEM((n_kv, 1, width), jnp.float32),
            pltpu.SemaphoreType.DMA((n_kv,)),
            pltpu.SemaphoreType.DMA((n_kv,)),
        ],
        compiler_params=pltpu.CompilerParams(
            collective_id=0, has_side_effects=True, vmem_limit_bytes=48 * 1024 * 1024
        ),
    )(
        queries.reshape(requests, heads, head_dim),
        keys,
        values,
        first_valid.reshape(requests, 1),
        sinks.reshape(heads, 1),
        out_proj,
    )


LANE = 256
TILE = 256
SLOT_STRIDE = 16


def _wire_shape(width, used):
    return ((width // LANE) * used, LANE)


def dispatch_kernel(used, place_ref, rows_ref, out_ref, staged):
    chunks = out_ref.shape[0]
    pieces = rows_ref.shape[1] // LANE
    group = TILE // SLOT_STRIDE

    def tile(i, carry):
        start = pl.multiple_of(i * TILE, TILE)
        staged[...] = jnp.dot(
            place_ref[pl.ds(start, TILE), :], rows_ref[...], preferred_element_type=jnp.float32
        ).astype(staged.dtype)
        for jl in range(group):
            j = i * group + jl
            for q in range(pieces):
                out_ref[j, pl.ds(q * used, used), :] = staged[
                    pl.ds(jl * SLOT_STRIDE, used), pl.ds(q * LANE, LANE)
                ]
        return carry

    lax.fori_loop(0, chunks // group, tile, 0)


def dispatch(place_t, rows, used):
    slots = place_t.shape[0]
    width = rows.shape[1]
    chunks = slots // SLOT_STRIDE
    return pl.pallas_call(
        lambda *refs: dispatch_kernel(used, *refs),
        out_shape=jax.ShapeDtypeStruct((chunks,) + _wire_shape(width, used), jnp.bfloat16),
        in_specs=[pl.BlockSpec(memory_space=pltpu.VMEM)] * 2,
        out_specs=pl.BlockSpec(memory_space=pltpu.VMEM),
        scratch_shapes=[pltpu.VMEM((TILE, width), jnp.bfloat16)],
        compiler_params=pltpu.CompilerParams(vmem_limit_bytes=48 * 1024 * 1024),
    )(place_t, rows)


def expert_kernel(x_ref, gate_ref, up_ref, down_ref, out_ref, rows_in, rows_out):
    chunks, wire_rows, _ = x_ref.shape
    width = gate_ref.shape[0]
    pieces = width // LANE
    used = wire_rows // pieces
    group = TILE // SLOT_STRIDE
    rows_in[...] = jnp.zeros(rows_in.shape, rows_in.dtype)

    def tile(i, carry):
        for jl in range(group):
            j = i * group + jl
            for q in range(pieces):
                rows_in[pl.ds(jl * SLOT_STRIDE, used), pl.ds(q * LANE, LANE)] = x_ref[
                    j, pl.ds(q * used, used), :
                ]
        rows = rows_in[...]
        gate_act = jnp.dot(rows, gate_ref[...], preferred_element_type=jnp.float32)
        up_act = jnp.dot(rows, up_ref[...], preferred_element_type=jnp.float32)
        inner_act = (gate_act / (1.0 + jnp.exp(-gate_act)) * up_act).astype(jnp.bfloat16)
        rows_out[...] = jnp.dot(
            inner_act, down_ref[...], preferred_element_type=jnp.float32
        ).astype(rows_out.dtype)
        for jl in range(group):
            j = i * group + jl
            for q in range(pieces):
                out_ref[j, pl.ds(q * used, used), :] = rows_out[
                    pl.ds(jl * SLOT_STRIDE, used), pl.ds(q * LANE, LANE)
                ]
        return carry

    lax.fori_loop(0, chunks // group, tile, 0)


def expert_block(arrived, gate_weights, up_weights, down_weights):
    width = gate_weights.shape[1]
    return pl.pallas_call(
        expert_kernel,
        out_shape=jax.ShapeDtypeStruct(arrived.shape, jnp.bfloat16),
        in_specs=[pl.BlockSpec(memory_space=pltpu.VMEM)] * 4,
        out_specs=pl.BlockSpec(memory_space=pltpu.VMEM),
        scratch_shapes=[
            pltpu.VMEM((TILE, width), jnp.bfloat16),
            pltpu.VMEM((TILE, width), jnp.bfloat16),
        ],
        compiler_params=pltpu.CompilerParams(vmem_limit_bytes=60 * 1024 * 1024),
    )(arrived, gate_weights[0], up_weights[0], down_weights[0])


def combine_kernel(ret_ref, mix_ref, hidden_ref, out_ref, rows):
    chunks, wire_rows, _ = ret_ref.shape
    width = rows.shape[1]
    pieces = width // LANE
    used = wire_rows // pieces
    tokens = hidden_ref.shape[0]
    rows[...] = jnp.zeros(rows.shape, rows.dtype)

    def fill(e, carry):
        start = pl.multiple_of(e * SLOT_STRIDE, SLOT_STRIDE)
        for q in range(pieces):
            rows[pl.ds(start, used), pl.ds(q * LANE, LANE)] = ret_ref[e, pl.ds(q * used, used), :]
        return carry

    lax.fori_loop(0, chunks, fill, 0)
    both = jnp.dot(mix_ref[...], rows[...], preferred_element_type=jnp.float32)
    out_ref[...] = (
        hidden_ref[...].astype(jnp.float32) + both[:tokens] + both[tokens:]
    ).astype(out_ref.dtype)


def combine(returned, mix_both, hidden):
    chunks = returned.shape[0]
    width = hidden.shape[1]
    return pl.pallas_call(
        combine_kernel,
        out_shape=jax.ShapeDtypeStruct(hidden.shape, jnp.bfloat16),
        in_specs=[pl.BlockSpec(memory_space=pltpu.VMEM)] * 3,
        out_specs=pl.BlockSpec(memory_space=pltpu.VMEM),
        scratch_shapes=[pltpu.VMEM((chunks * SLOT_STRIDE, width), jnp.bfloat16)],
        compiler_params=pltpu.CompilerParams(vmem_limit_bytes=48 * 1024 * 1024),
    )(returned, mix_both, hidden)


def body(
    queries,
    cache_keys,
    cache_values,
    lengths,
    sinks,
    out_proj,
    decode_resid,
    prefill_hidden,
    norm_gain,
    router,
    routes,
    expert_gate,
    expert_up,
    expert_down,
):
    n_kv = lax.axis_size("kv")
    my_block = lax.axis_index("blk")
    per_block = queries.shape[0]
    head_count = sinks.shape[0]
    head_dim = cache_keys.shape[3]
    window = cache_keys.shape[1]
    my_lengths = lax.dynamic_slice_in_dim(lengths, my_block * per_block, per_block)
    first_valid = window - jnp.minimum(my_lengths, window)
    projected = attend_reduce(
        queries,
        cache_keys[:, :, 0, :],
        cache_values[:, :, 0, :],
        first_valid,
        sinks,
        out_proj,
        n_kv,
    )
    decoded = (decode_resid.astype(jnp.float32) + projected).astype(jnp.bfloat16)
    hidden = jnp.concatenate([decoded, prefill_hidden[0]], axis=0)
    hidden_f = hidden.astype(jnp.float32)
    mean_sq = jnp.mean(hidden_f * hidden_f, axis=1, keepdims=True)
    normed = (hidden_f * lax.rsqrt(mean_sq + EPSILON) * norm_gain).astype(jnp.bfloat16)

    experts = router.shape[1]
    chosen_ids = routes[0]
    tokens, top_k = chosen_ids.shape
    model_width = hidden.shape[1]
    capacity = 16
    logits = jnp.dot(normed, router, preferred_element_type=jnp.float32)
    one_hot = chosen_ids[..., None] == jnp.arange(experts, dtype=jnp.int32)
    chosen = jnp.sum(jnp.where(one_hot, logits[:, None, :], 0.0), axis=2)
    gate_probs = jax.nn.softmax(chosen, axis=1)
    row_hot = jnp.any(one_hot, axis=1).astype(jnp.int32)
    earlier = jnp.cumsum(row_hot, axis=0) - row_hot
    slot_rank = jnp.sum(jnp.where(one_hot, earlier[:, None, :], 0), axis=2)
    rank_hot = slot_rank[..., None] == jnp.arange(capacity, dtype=jnp.int32)
    fills = one_hot[..., None] & rank_hot[:, :, None, :]
    place = jnp.any(fills, axis=1).reshape(tokens, experts * capacity).astype(jnp.bfloat16)
    outgoing = dispatch(place.T, normed, 14)
    arrived = lax.all_to_all(outgoing, ("kv", "blk"), split_axis=0, concat_axis=0, tiled=True)
    processed = expert_block(arrived, expert_gate, expert_up, expert_down)
    returned = lax.all_to_all(processed, ("kv", "blk"), split_axis=0, concat_axis=0, tiled=True)
    mix = jnp.sum(jnp.where(fills, gate_probs[..., None, None], 0.0), axis=1)
    mix = mix.reshape(tokens, experts * capacity)
    mix_hi = mix.astype(jnp.bfloat16)
    mix_lo = (mix - mix_hi.astype(jnp.float32)).astype(jnp.bfloat16)
    layer_sum = combine(returned, jnp.concatenate([mix_hi, mix_lo], axis=0), hidden)
    return layer_sum[None]


def solution(mesh):
    return jax.shard_map(
        body,
        mesh=mesh,
        in_specs=(
            P("blk", "kv"),
            P("blk", None, "kv", None),
            P("blk", None, "kv", None),
            P(),
            P("kv"),
            P("kv", None),
            P(("blk", "kv"), None),
            P(("blk", "kv"), None, None),
            P(),
            P(),
            P(("blk", "kv"), None, None),
            P(("kv", "blk"), None, None),
            P(("kv", "blk"), None, None),
            P(("kv", "blk"), None, None),
        ),
        out_specs=P(("blk", "kv"), None, None),
        check_vma=False,
    )
```

```python
import math

import jax
import jax.numpy as jnp
from jax import lax
from jax.experimental import pallas as pl
from jax.experimental.pallas import tpu as pltpu
from jax.sharding import PartitionSpec as P

NEG_FILL = -1e30
EPSILON = 1e-06
MESH = pl.DeviceIdType.MESH


def attend_reduce_kernel(
    n_kv, q_ref, k_ref, v_ref, first_ref, sink_ref, proj_ref, out_ref, att, part, held, send_sem, recv_sem
):
    me = lax.axis_index("kv")
    blk = lax.axis_index("blk")
    barrier = pltpu.get_barrier_semaphore()
    for step in range(1, n_kv):
        peer = lax.rem(me + step, n_kv)
        pl.semaphore_signal(barrier, inc=1, device_id=(peer, blk), device_id_type=MESH)
    requests, heads, head_dim = q_ref.shape
    window = k_ref.shape[1]
    scale = 1.0 / math.sqrt(head_dim)
    sink = sink_ref[...]
    positions = lax.broadcasted_iota(jnp.int32, (heads, window), 1)
    for r in range(requests):
        scores = lax.dot_general(
            q_ref[r], k_ref[r], (((1,), (1,)), ((), ())), preferred_element_type=jnp.float32
        ) * scale
        valid = positions >= first_ref[pl.ds(r, 1), :]
        masked = jnp.where(valid, scores, NEG_FILL)
        top = jnp.maximum(jnp.max(masked, axis=1, keepdims=True), sink)
        weights = jnp.where(valid, jnp.exp(masked - top), 0.0)
        denominator = jnp.sum(weights, axis=1, keepdims=True) + jnp.exp(sink - top)
        numerator = jnp.dot(
            weights.astype(jnp.bfloat16), v_ref[r], preferred_element_type=jnp.float32
        )
        att[:, pl.ds(r, 1), :] = (numerator / denominator).astype(jnp.bfloat16).astype(
            jnp.float32
        )[:, None, :]
    total = jnp.zeros((requests, proj_ref.shape[1]), jnp.float32)
    for h in range(heads):
        total = total + jnp.dot(
            att[h].astype(jnp.bfloat16),
            proj_ref[pl.ds(h * head_dim, head_dim), :],
            preferred_element_type=jnp.float32,
        )
    part[...] = total[:, None, :]
    pl.semaphore_wait(barrier, n_kv - 1)
    for step in range(1, n_kv):
        peer = lax.rem(me + step, n_kv)
        pltpu.make_async_remote_copy(
            src_ref=part.at[peer],
            dst_ref=held.at[me],
            send_sem=send_sem.at[peer],
            recv_sem=recv_sem.at[me],
            device_id=(peer, blk),
            device_id_type=MESH,
        ).start()
    own = part[me]
    for step in range(1, n_kv):
        peer = lax.rem(me + step, n_kv)
        arrival = pltpu.make_async_remote_copy(
            src_ref=part.at[peer],
            dst_ref=held.at[peer],
            send_sem=send_sem.at[peer],
            recv_sem=recv_sem.at[peer],
            device_id=(peer, blk),
            device_id_type=MESH,
        )
        arrival.wait_send()
        arrival.wait_recv()
    for step in range(1, n_kv):
        peer = lax.rem(me + step, n_kv)
        own = own + held[peer]
    out_ref[...] = own


def attend_reduce(queries, keys, values, first_valid, sinks, out_proj, n_kv):
    requests = queries.shape[0]
    heads = sinks.shape[0]
    head_dim = keys.shape[2]
    width = out_proj.shape[1]
    return pl.pallas_call(
        lambda *refs: attend_reduce_kernel(n_kv, *refs),
        out_shape=jax.ShapeDtypeStruct((1, width), jnp.float32),
        in_specs=[pl.BlockSpec(memory_space=pltpu.VMEM)] * 6,
        out_specs=pl.BlockSpec(memory_space=pltpu.VMEM),
        scratch_shapes=[
            pltpu.VMEM((heads, requests, head_dim), jnp.float32),
            pltpu.VMEM((requests, 1, width), jnp.float32),
            pltpu.VMEM((n_kv, 1, width), jnp.float32),
            pltpu.SemaphoreType.DMA((n_kv,)),
            pltpu.SemaphoreType.DMA((n_kv,)),
        ],
        compiler_params=pltpu.CompilerParams(
            collective_id=0, has_side_effects=True, vmem_limit_bytes=48 * 1024 * 1024
        ),
    )(
        queries.reshape(requests, heads, head_dim),
        keys,
        values,
        first_valid.reshape(requests, 1),
        sinks.reshape(heads, 1),
        out_proj,
    )


LANE = 256
GROUP = 16


def _wire_shape(width, used):
    return ((width // LANE) * used, LANE)


def dispatch_kernel(used, place_ref, rows_ref, out_ref, staged):
    chunks = out_ref.shape[0]
    pieces = rows_ref.shape[1] // LANE
    tile_rows = GROUP * used

    def tile(i, carry):
        staged[...] = jnp.dot(
            place_ref[i], rows_ref[...], preferred_element_type=jnp.float32
        ).astype(staged.dtype)
        for jl in range(GROUP):
            j = i * GROUP + jl
            for q in range(pieces):
                out_ref[j, pl.ds(q * used, used), :] = staged[
                    pl.ds(jl * used, used), pl.ds(q * LANE, LANE)
                ]
        return carry

    lax.fori_loop(0, chunks // GROUP, tile, 0)


def dispatch(place_t, rows, used):
    tiles, tile_rows, _ = place_t.shape
    width = rows.shape[1]
    chunks = tiles * GROUP
    return pl.pallas_call(
        lambda *refs: dispatch_kernel(used, *refs),
        out_shape=jax.ShapeDtypeStruct((chunks,) + _wire_shape(width, used), jnp.bfloat16),
        in_specs=[pl.BlockSpec(memory_space=pltpu.VMEM)] * 2,
        out_specs=pl.BlockSpec(memory_space=pltpu.VMEM),
        scratch_shapes=[pltpu.VMEM((tile_rows, width), jnp.bfloat16)],
        compiler_params=pltpu.CompilerParams(vmem_limit_bytes=48 * 1024 * 1024),
    )(place_t, rows)


def _gather_tile(i, used, src_ref, dst):
    pieces = dst.shape[1] // LANE
    for jl in range(GROUP):
        j = i * GROUP + jl
        for q in range(pieces):
            dst[pl.ds(jl * used, used), pl.ds(q * LANE, LANE)] = src_ref[j, pl.ds(q * used, used), :]


def expert_kernel(x_ref, gate_ref, up_ref, down_ref, out_ref, rows_in, rows_out):
    chunks, wire_rows, _ = x_ref.shape
    width = gate_ref.shape[0]
    pieces = width // LANE
    used = wire_rows // pieces

    def tile(i, carry):
        _gather_tile(i, used, x_ref, rows_in)
        rows = rows_in[...]
        gate_act = jnp.dot(rows, gate_ref[...], preferred_element_type=jnp.float32)
        up_act = jnp.dot(rows, up_ref[...], preferred_element_type=jnp.float32)
        inner_act = (gate_act / (1.0 + jnp.exp(-gate_act)) * up_act).astype(jnp.bfloat16)
        rows_out[...] = jnp.dot(
            inner_act, down_ref[...], preferred_element_type=jnp.float32
        ).astype(rows_out.dtype)
        for jl in range(GROUP):
            j = i * GROUP + jl
            for q in range(pieces):
                out_ref[j, pl.ds(q * used, used), :] = rows_out[
                    pl.ds(jl * used, used), pl.ds(q * LANE, LANE)
                ]
        return carry

    lax.fori_loop(0, chunks // GROUP, tile, 0)


def expert_block(arrived, gate_weights, up_weights, down_weights):
    chunks, wire_rows, _ = arrived.shape
    width = gate_weights.shape[1]
    used = wire_rows // (width // LANE)
    return pl.pallas_call(
        expert_kernel,
        out_shape=jax.ShapeDtypeStruct(arrived.shape, jnp.bfloat16),
        in_specs=[pl.BlockSpec(memory_space=pltpu.VMEM)] * 4,
        out_specs=pl.BlockSpec(memory_space=pltpu.VMEM),
        scratch_shapes=[
            pltpu.VMEM((GROUP * used, width), jnp.bfloat16),
            pltpu.VMEM((GROUP * used, width), jnp.bfloat16),
        ],
        compiler_params=pltpu.CompilerParams(vmem_limit_bytes=60 * 1024 * 1024),
    )(arrived, gate_weights[0], up_weights[0], down_weights[0])


def combine_kernel(ret_ref, mix_ref, hidden_ref, out_ref, rows, total):
    chunks, wire_rows, _ = ret_ref.shape
    width = rows.shape[1]
    used = wire_rows // (width // LANE)
    tokens = hidden_ref.shape[0]
    total[...] = jnp.zeros(total.shape, total.dtype)

    def tile(i, carry):
        _gather_tile(i, used, ret_ref, rows)
        total[...] += jnp.dot(mix_ref[i], rows[...], preferred_element_type=jnp.float32)
        return carry

    lax.fori_loop(0, chunks // GROUP, tile, 0)
    both = total[...]
    out_ref[...] = (
        hidden_ref[...].astype(jnp.float32) + both[:tokens] + both[tokens:]
    ).astype(out_ref.dtype)


def combine(returned, mix_both, hidden):
    chunks, wire_rows, _ = returned.shape
    width = hidden.shape[1]
    used = wire_rows // (width // LANE)
    return pl.pallas_call(
        combine_kernel,
        out_shape=jax.ShapeDtypeStruct(hidden.shape, jnp.bfloat16),
        in_specs=[pl.BlockSpec(memory_space=pltpu.VMEM)] * 3,
        out_specs=pl.BlockSpec(memory_space=pltpu.VMEM),
        scratch_shapes=[
            pltpu.VMEM((GROUP * used, width), jnp.bfloat16),
            pltpu.VMEM((mix_both.shape[1], width), jnp.float32),
        ],
        compiler_params=pltpu.CompilerParams(vmem_limit_bytes=48 * 1024 * 1024),
    )(returned, mix_both, hidden)


def body(
    queries,
    cache_keys,
    cache_values,
    lengths,
    sinks,
    out_proj,
    decode_resid,
    prefill_hidden,
    norm_gain,
    router,
    routes,
    expert_gate,
    expert_up,
    expert_down,
):
    n_kv = lax.axis_size("kv")
    my_block = lax.axis_index("blk")
    per_block = queries.shape[0]
    head_count = sinks.shape[0]
    head_dim = cache_keys.shape[3]
    window = cache_keys.shape[1]
    my_lengths = lax.dynamic_slice_in_dim(lengths, my_block * per_block, per_block)
    first_valid = window - jnp.minimum(my_lengths, window)
    projected = attend_reduce(
        queries,
        cache_keys[:, :, 0, :],
        cache_values[:, :, 0, :],
        first_valid,
        sinks,
        out_proj,
        n_kv,
    )
    decoded = (decode_resid.astype(jnp.float32) + projected).astype(jnp.bfloat16)
    hidden = jnp.concatenate([decoded, prefill_hidden[0]], axis=0)
    hidden_f = hidden.astype(jnp.float32)
    mean_sq = jnp.mean(hidden_f * hidden_f, axis=1, keepdims=True)
    normed = (hidden_f * lax.rsqrt(mean_sq + EPSILON) * norm_gain).astype(jnp.bfloat16)

    experts = router.shape[1]
    chosen_ids = routes[0]
    tokens, top_k = chosen_ids.shape
    model_width = hidden.shape[1]
    capacity = 14
    logits = jnp.dot(normed, router, preferred_element_type=jnp.float32)
    one_hot = chosen_ids[..., None] == jnp.arange(experts, dtype=jnp.int32)
    chosen = jnp.sum(jnp.where(one_hot, logits[:, None, :], 0.0), axis=2)
    gate_probs = jax.nn.softmax(chosen, axis=1)
    row_hot = jnp.any(one_hot, axis=1).astype(jnp.int32)
    earlier = jnp.cumsum(row_hot, axis=0) - row_hot
    slot_rank = jnp.sum(jnp.where(one_hot, earlier[:, None, :], 0), axis=2)
    rank_hot = slot_rank[..., None] == jnp.arange(capacity, dtype=jnp.int32)
    fills = one_hot[..., None] & rank_hot[:, :, None, :]
    place = jnp.any(fills, axis=1).reshape(tokens, experts * capacity).astype(jnp.bfloat16)
    tiles = experts // GROUP
    tile_rows = GROUP * capacity
    place_t = place.T.reshape(tiles, tile_rows, tokens)
    outgoing = dispatch(place_t, normed, capacity)
    arrived = lax.all_to_all(outgoing, ("kv", "blk"), split_axis=0, concat_axis=0, tiled=True)
    processed = expert_block(arrived, expert_gate, expert_up, expert_down)
    returned = lax.all_to_all(processed, ("kv", "blk"), split_axis=0, concat_axis=0, tiled=True)
    mix = jnp.sum(jnp.where(fills, gate_probs[..., None, None], 0.0), axis=1)
    mix = mix.reshape(tokens, experts * capacity)
    mix_hi = mix.astype(jnp.bfloat16)
    mix_lo = (mix - mix_hi.astype(jnp.float32)).astype(jnp.bfloat16)
    mix_both = jnp.concatenate([mix_hi, mix_lo], axis=0)
    mix_tiles = mix_both.reshape(2 * tokens, tiles, tile_rows).transpose(1, 0, 2)
    layer_sum = combine(returned, mix_tiles, hidden)
    return layer_sum[None]


def solution(mesh):
    return jax.shard_map(
        body,
        mesh=mesh,
        in_specs=(
            P("blk", "kv"),
            P("blk", None, "kv", None),
            P("blk", None, "kv", None),
            P(),
            P("kv"),
            P("kv", None),
            P(("blk", "kv"), None),
            P(("blk", "kv"), None, None),
            P(),
            P(),
            P(("blk", "kv"), None, None),
            P(("kv", "blk"), None, None),
            P(("kv", "blk"), None, None),
            P(("kv", "blk"), None, None),
        ),
        out_specs=P(("blk", "kv"), None, None),
        check_vma=False,
    )
```

```python
import math

import jax
import jax.numpy as jnp
from jax import lax
from jax.experimental import pallas as pl
from jax.experimental.pallas import tpu as pltpu
from jax.sharding import PartitionSpec as P

NEG_FILL = -1e30
EPSILON = 1e-06
MESH = pl.DeviceIdType.MESH


def attend_reduce_kernel(
    n_kv, q_ref, k_ref, v_ref, first_ref, sink_ref, proj_ref, out_ref, att, part, held, send_sem, recv_sem
):
    me = lax.axis_index("kv")
    blk = lax.axis_index("blk")
    barrier = pltpu.get_barrier_semaphore()
    for step in range(1, n_kv):
        peer = lax.rem(me + step, n_kv)
        pl.semaphore_signal(barrier, inc=1, device_id=(peer, blk), device_id_type=MESH)
    requests, heads, head_dim = q_ref.shape
    window = k_ref.shape[1]
    scale = 1.0 / math.sqrt(head_dim)
    sink = sink_ref[...]
    positions = lax.broadcasted_iota(jnp.int32, (heads, window), 1)
    for r in range(requests):
        scores = lax.dot_general(
            q_ref[r], k_ref[r], (((1,), (1,)), ((), ())), preferred_element_type=jnp.float32
        ) * scale
        valid = positions >= first_ref[pl.ds(r, 1), :]
        masked = jnp.where(valid, scores, NEG_FILL)
        top = jnp.maximum(jnp.max(masked, axis=1, keepdims=True), sink)
        weights = jnp.where(valid, jnp.exp(masked - top), 0.0)
        denominator = jnp.sum(weights, axis=1, keepdims=True) + jnp.exp(sink - top)
        numerator = jnp.dot(
            weights.astype(jnp.bfloat16), v_ref[r], preferred_element_type=jnp.float32
        )
        att[:, pl.ds(r, 1), :] = (numerator / denominator).astype(jnp.bfloat16).astype(
            jnp.float32
        )[:, None, :]
    total = jnp.zeros((requests, proj_ref.shape[1]), jnp.float32)
    for h in range(heads):
        total = total + jnp.dot(
            att[h].astype(jnp.bfloat16),
            proj_ref[pl.ds(h * head_dim, head_dim), :],
            preferred_element_type=jnp.float32,
        )
    part[...] = total[:, None, :]
    pl.semaphore_wait(barrier, n_kv - 1)
    for step in range(1, n_kv):
        peer = lax.rem(me + step, n_kv)
        pltpu.make_async_remote_copy(
            src_ref=part.at[peer],
            dst_ref=held.at[me],
            send_sem=send_sem.at[peer],
            recv_sem=recv_sem.at[me],
            device_id=(peer, blk),
            device_id_type=MESH,
        ).start()
    own = part[me]
    for step in range(1, n_kv):
        peer = lax.rem(me + step, n_kv)
        arrival = pltpu.make_async_remote_copy(
            src_ref=part.at[peer],
            dst_ref=held.at[peer],
            send_sem=send_sem.at[peer],
            recv_sem=recv_sem.at[peer],
            device_id=(peer, blk),
            device_id_type=MESH,
        )
        arrival.wait_send()
        arrival.wait_recv()
    for step in range(1, n_kv):
        peer = lax.rem(me + step, n_kv)
        own = own + held[peer]
    out_ref[...] = own


def attend_reduce(queries, keys, values, first_valid, sinks, out_proj, n_kv):
    requests = queries.shape[0]
    heads = sinks.shape[0]
    head_dim = keys.shape[2]
    width = out_proj.shape[1]
    return pl.pallas_call(
        lambda *refs: attend_reduce_kernel(n_kv, *refs),
        out_shape=jax.ShapeDtypeStruct((1, width), jnp.float32),
        in_specs=[pl.BlockSpec(memory_space=pltpu.VMEM)] * 6,
        out_specs=pl.BlockSpec(memory_space=pltpu.VMEM),
        scratch_shapes=[
            pltpu.VMEM((heads, requests, head_dim), jnp.float32),
            pltpu.VMEM((requests, 1, width), jnp.float32),
            pltpu.VMEM((n_kv, 1, width), jnp.float32),
            pltpu.SemaphoreType.DMA((n_kv,)),
            pltpu.SemaphoreType.DMA((n_kv,)),
        ],
        compiler_params=pltpu.CompilerParams(
            collective_id=0, has_side_effects=True, vmem_limit_bytes=48 * 1024 * 1024
        ),
    )(
        queries.reshape(requests, heads, head_dim),
        keys,
        values,
        first_valid.reshape(requests, 1),
        sinks.reshape(heads, 1),
        out_proj,
    )


LANE = 256
GROUP = 16


def _wire_shape(width, used):
    return ((width // LANE) * used, LANE)


def dispatch_kernel(used, ids_ref, rows_ref, out_ref, staged):
    chunks = out_ref.shape[0]
    pieces = rows_ref.shape[1] // LANE
    tile_rows = GROUP * used
    top_k, tokens = ids_ref.shape

    def tile(i, carry):
        slot = lax.broadcasted_iota(jnp.int32, (tile_rows, tokens), 0) + i * tile_rows
        ids = ids_ref[...]
        hit = slot == ids[0:1, :]
        for k in range(1, top_k):
            hit = jnp.logical_or(hit, slot == ids[k : k + 1, :])
        staged[...] = jnp.dot(
            hit.astype(jnp.bfloat16), rows_ref[...], preferred_element_type=jnp.float32
        ).astype(staged.dtype)
        for jl in range(GROUP):
            j = i * GROUP + jl
            for q in range(pieces):
                out_ref[j, pl.ds(q * used, used), :] = staged[
                    pl.ds(jl * used, used), pl.ds(q * LANE, LANE)
                ]
        return carry

    lax.fori_loop(0, chunks // GROUP, tile, 0)


def dispatch(slot_ids_t, rows, chunks, used):
    width = rows.shape[1]
    return pl.pallas_call(
        lambda *refs: dispatch_kernel(used, *refs),
        out_shape=jax.ShapeDtypeStruct((chunks,) + _wire_shape(width, used), jnp.bfloat16),
        in_specs=[pl.BlockSpec(memory_space=pltpu.VMEM)] * 2,
        out_specs=pl.BlockSpec(memory_space=pltpu.VMEM),
        scratch_shapes=[pltpu.VMEM((GROUP * used, width), jnp.bfloat16)],
        compiler_params=pltpu.CompilerParams(vmem_limit_bytes=48 * 1024 * 1024),
    )(slot_ids_t, rows)


def _gather_tile(i, used, src_ref, dst):
    pieces = dst.shape[1] // LANE
    for jl in range(GROUP):
        j = i * GROUP + jl
        for q in range(pieces):
            dst[pl.ds(jl * used, used), pl.ds(q * LANE, LANE)] = src_ref[j, pl.ds(q * used, used), :]


def expert_kernel(x_ref, gate_ref, up_ref, down_ref, out_ref, rows_in, rows_out):
    chunks, wire_rows, _ = x_ref.shape
    width = gate_ref.shape[0]
    pieces = width // LANE
    used = wire_rows // pieces

    def tile(i, carry):
        _gather_tile(i, used, x_ref, rows_in)
        rows = rows_in[...]
        gate_act = jnp.dot(rows, gate_ref[...], preferred_element_type=jnp.float32)
        up_act = jnp.dot(rows, up_ref[...], preferred_element_type=jnp.float32)
        inner_act = (gate_act / (1.0 + jnp.exp(-gate_act)) * up_act).astype(jnp.bfloat16)
        rows_out[...] = jnp.dot(
            inner_act, down_ref[...], preferred_element_type=jnp.float32
        ).astype(rows_out.dtype)
        for jl in range(GROUP):
            j = i * GROUP + jl
            for q in range(pieces):
                out_ref[j, pl.ds(q * used, used), :] = rows_out[
                    pl.ds(jl * used, used), pl.ds(q * LANE, LANE)
                ]
        return carry

    lax.fori_loop(0, chunks // GROUP, tile, 0)


def expert_block(arrived, gate_weights, up_weights, down_weights):
    chunks, wire_rows, _ = arrived.shape
    width = gate_weights.shape[1]
    used = wire_rows // (width // LANE)
    return pl.pallas_call(
        expert_kernel,
        out_shape=jax.ShapeDtypeStruct(arrived.shape, jnp.bfloat16),
        in_specs=[pl.BlockSpec(memory_space=pltpu.VMEM)] * 4,
        out_specs=pl.BlockSpec(memory_space=pltpu.VMEM),
        scratch_shapes=[
            pltpu.VMEM((GROUP * used, width), jnp.bfloat16),
            pltpu.VMEM((GROUP * used, width), jnp.bfloat16),
        ],
        compiler_params=pltpu.CompilerParams(vmem_limit_bytes=60 * 1024 * 1024),
    )(arrived, gate_weights[0], up_weights[0], down_weights[0])


def combine_kernel(ret_ref, mix_ref, hidden_ref, out_ref, rows, total):
    chunks, wire_rows, _ = ret_ref.shape
    width = rows.shape[1]
    used = wire_rows // (width // LANE)
    tokens = hidden_ref.shape[0]
    total[...] = jnp.zeros(total.shape, total.dtype)

    def tile(i, carry):
        _gather_tile(i, used, ret_ref, rows)
        total[...] += jnp.dot(mix_ref[i], rows[...], preferred_element_type=jnp.float32)
        return carry

    lax.fori_loop(0, chunks // GROUP, tile, 0)
    both = total[...]
    out_ref[...] = (
        hidden_ref[...].astype(jnp.float32) + both[:tokens] + both[tokens:]
    ).astype(out_ref.dtype)


def combine(returned, mix_both, hidden):
    chunks, wire_rows, _ = returned.shape
    width = hidden.shape[1]
    used = wire_rows // (width // LANE)
    return pl.pallas_call(
        combine_kernel,
        out_shape=jax.ShapeDtypeStruct(hidden.shape, jnp.bfloat16),
        in_specs=[pl.BlockSpec(memory_space=pltpu.VMEM)] * 3,
        out_specs=pl.BlockSpec(memory_space=pltpu.VMEM),
        scratch_shapes=[
            pltpu.VMEM((GROUP * used, width), jnp.bfloat16),
            pltpu.VMEM((mix_both.shape[1], width), jnp.float32),
        ],
        compiler_params=pltpu.CompilerParams(vmem_limit_bytes=48 * 1024 * 1024),
    )(returned, mix_both, hidden)


def body(
    queries,
    cache_keys,
    cache_values,
    lengths,
    sinks,
    out_proj,
    decode_resid,
    prefill_hidden,
    norm_gain,
    router,
    routes,
    expert_gate,
    expert_up,
    expert_down,
):
    n_kv = lax.axis_size("kv")
    my_block = lax.axis_index("blk")
    per_block = queries.shape[0]
    head_count = sinks.shape[0]
    head_dim = cache_keys.shape[3]
    window = cache_keys.shape[1]
    my_lengths = lax.dynamic_slice_in_dim(lengths, my_block * per_block, per_block)
    first_valid = window - jnp.minimum(my_lengths, window)
    projected = attend_reduce(
        queries,
        cache_keys[:, :, 0, :],
        cache_values[:, :, 0, :],
        first_valid,
        sinks,
        out_proj,
        n_kv,
    )
    decoded = (decode_resid.astype(jnp.float32) + projected).astype(jnp.bfloat16)
    hidden = jnp.concatenate([decoded, prefill_hidden[0]], axis=0)
    hidden_f = hidden.astype(jnp.float32)
    mean_sq = jnp.mean(hidden_f * hidden_f, axis=1, keepdims=True)
    normed = (hidden_f * lax.rsqrt(mean_sq + EPSILON) * norm_gain).astype(jnp.bfloat16)

    experts = router.shape[1]
    chosen_ids = routes[0]
    tokens, top_k = chosen_ids.shape
    model_width = hidden.shape[1]
    capacity = 14
    logits = jnp.dot(normed, router, preferred_element_type=jnp.float32)
    one_hot = chosen_ids[..., None] == jnp.arange(experts, dtype=jnp.int32)
    chosen = jnp.sum(jnp.where(one_hot, logits[:, None, :], 0.0), axis=2)
    gate_probs = jax.nn.softmax(chosen, axis=1)
    row_hot = jnp.any(one_hot, axis=1).astype(jnp.int32)
    earlier = jnp.cumsum(row_hot, axis=0) - row_hot
    slot_rank = jnp.sum(jnp.where(one_hot, earlier[:, None, :], 0), axis=2)
    rank_hot = slot_rank[..., None] == jnp.arange(capacity, dtype=jnp.int32)
    fills = one_hot[..., None] & rank_hot[:, :, None, :]
    tiles = experts // GROUP
    tile_rows = GROUP * capacity
    slot_ids = chosen_ids * capacity + slot_rank
    outgoing = dispatch(slot_ids.T, normed, experts, capacity)
    arrived = lax.all_to_all(outgoing, ("kv", "blk"), split_axis=0, concat_axis=0, tiled=True)
    processed = expert_block(arrived, expert_gate, expert_up, expert_down)
    returned = lax.all_to_all(processed, ("kv", "blk"), split_axis=0, concat_axis=0, tiled=True)
    mix = jnp.sum(jnp.where(fills, gate_probs[..., None, None], 0.0), axis=1)
    mix = mix.reshape(tokens, experts * capacity)
    mix_hi = mix.astype(jnp.bfloat16)
    mix_lo = (mix - mix_hi.astype(jnp.float32)).astype(jnp.bfloat16)
    mix_both = jnp.concatenate([mix_hi, mix_lo], axis=0)
    mix_tiles = mix_both.reshape(2 * tokens, tiles, tile_rows).transpose(1, 0, 2)
    layer_sum = combine(returned, mix_tiles, hidden)
    return layer_sum[None]


def solution(mesh):
    return jax.shard_map(
        body,
        mesh=mesh,
        in_specs=(
            P("blk", "kv"),
            P("blk", None, "kv", None),
            P("blk", None, "kv", None),
            P(),
            P("kv"),
            P("kv", None),
            P(("blk", "kv"), None),
            P(("blk", "kv"), None, None),
            P(),
            P(),
            P(("blk", "kv"), None, None),
            P(("kv", "blk"), None, None),
            P(("kv", "blk"), None, None),
            P(("kv", "blk"), None, None),
        ),
        out_specs=P(("blk", "kv"), None, None),
        check_vma=False,
    )
```

```python
import math

import jax
import jax.numpy as jnp
from jax import lax
from jax.experimental import pallas as pl
from jax.experimental.pallas import tpu as pltpu
from jax.sharding import PartitionSpec as P

NEG_FILL = -1e30
EPSILON = 1e-06
MESH = pl.DeviceIdType.MESH


def attend_reduce_kernel(
    n_kv, q_ref, k_ref, v_ref, first_ref, sink_ref, proj_ref, out_ref, att, part, held, send_sem, recv_sem
):
    me = lax.axis_index("kv")
    blk = lax.axis_index("blk")
    barrier = pltpu.get_barrier_semaphore()
    for step in range(1, n_kv):
        peer = lax.rem(me + step, n_kv)
        pl.semaphore_signal(barrier, inc=1, device_id=(peer, blk), device_id_type=MESH)
    requests, heads, head_dim = q_ref.shape
    window = k_ref.shape[1]
    scale = 1.0 / math.sqrt(head_dim)
    sink = sink_ref[...]
    positions = lax.broadcasted_iota(jnp.int32, (heads, window), 1)
    for r in range(requests):
        scores = lax.dot_general(
            q_ref[r], k_ref[r], (((1,), (1,)), ((), ())), preferred_element_type=jnp.float32
        ) * scale
        valid = positions >= first_ref[pl.ds(r, 1), :]
        masked = jnp.where(valid, scores, NEG_FILL)
        top = jnp.maximum(jnp.max(masked, axis=1, keepdims=True), sink)
        weights = jnp.where(valid, jnp.exp(masked - top), 0.0)
        denominator = jnp.sum(weights, axis=1, keepdims=True) + jnp.exp(sink - top)
        numerator = jnp.dot(
            weights.astype(jnp.bfloat16), v_ref[r], preferred_element_type=jnp.float32
        )
        att[:, pl.ds(r, 1), :] = (numerator / denominator).astype(jnp.bfloat16).astype(
            jnp.float32
        )[:, None, :]
    total = jnp.zeros((requests, proj_ref.shape[1]), jnp.float32)
    for h in range(heads):
        total = total + jnp.dot(
            att[h].astype(jnp.bfloat16),
            proj_ref[pl.ds(h * head_dim, head_dim), :],
            preferred_element_type=jnp.float32,
        )
    part[...] = total[:, None, :]
    pl.semaphore_wait(barrier, n_kv - 1)
    for step in range(1, n_kv):
        peer = lax.rem(me + step, n_kv)
        pltpu.make_async_remote_copy(
            src_ref=part.at[peer],
            dst_ref=held.at[me],
            send_sem=send_sem.at[peer],
            recv_sem=recv_sem.at[me],
            device_id=(peer, blk),
            device_id_type=MESH,
        ).start()
    own = part[me]
    for step in range(1, n_kv):
        peer = lax.rem(me + step, n_kv)
        arrival = pltpu.make_async_remote_copy(
            src_ref=part.at[peer],
            dst_ref=held.at[peer],
            send_sem=send_sem.at[peer],
            recv_sem=recv_sem.at[peer],
            device_id=(peer, blk),
            device_id_type=MESH,
        )
        arrival.wait_send()
        arrival.wait_recv()
    for step in range(1, n_kv):
        peer = lax.rem(me + step, n_kv)
        own = own + held[peer]
    out_ref[...] = own


def attend_reduce(queries, keys, values, first_valid, sinks, out_proj, n_kv):
    requests = queries.shape[0]
    heads = sinks.shape[0]
    head_dim = keys.shape[2]
    width = out_proj.shape[1]
    return pl.pallas_call(
        lambda *refs: attend_reduce_kernel(n_kv, *refs),
        out_shape=jax.ShapeDtypeStruct((1, width), jnp.float32),
        in_specs=[pl.BlockSpec(memory_space=pltpu.VMEM)] * 6,
        out_specs=pl.BlockSpec(memory_space=pltpu.VMEM),
        scratch_shapes=[
            pltpu.VMEM((heads, requests, head_dim), jnp.float32),
            pltpu.VMEM((requests, 1, width), jnp.float32),
            pltpu.VMEM((n_kv, 1, width), jnp.float32),
            pltpu.SemaphoreType.DMA((n_kv,)),
            pltpu.SemaphoreType.DMA((n_kv,)),
        ],
        compiler_params=pltpu.CompilerParams(
            collective_id=0, has_side_effects=True, vmem_limit_bytes=48 * 1024 * 1024
        ),
    )(
        queries.reshape(requests, heads, head_dim),
        keys,
        values,
        first_valid.reshape(requests, 1),
        sinks.reshape(heads, 1),
        out_proj,
    )


LANE = 256
GROUP = 16


def _wire_shape(width, used):
    return ((width // LANE) * used, LANE)


def dispatch_kernel(used, ids_ref, rows_ref, out_ref, staged):
    chunks = out_ref.shape[0]
    pieces = rows_ref.shape[1] // LANE
    tile_rows = GROUP * used
    top_k, tokens = ids_ref.shape

    def tile(i, carry):
        slot = lax.broadcasted_iota(jnp.int32, (tile_rows, tokens), 0) + i * tile_rows
        ids = ids_ref[...]
        hit = slot == ids[0:1, :]
        for k in range(1, top_k):
            hit = jnp.logical_or(hit, slot == ids[k : k + 1, :])
        staged[...] = jnp.dot(
            hit.astype(jnp.bfloat16), rows_ref[...], preferred_element_type=jnp.float32
        ).astype(staged.dtype)
        for jl in range(GROUP):
            j = i * GROUP + jl
            for q in range(pieces):
                out_ref[j, pl.ds(q * used, used), :] = staged[
                    pl.ds(jl * used, used), pl.ds(q * LANE, LANE)
                ]
        return carry

    lax.fori_loop(0, chunks // GROUP, tile, 0)


def dispatch(slot_ids_t, rows, chunks, used):
    width = rows.shape[1]
    return pl.pallas_call(
        lambda *refs: dispatch_kernel(used, *refs),
        out_shape=jax.ShapeDtypeStruct((chunks,) + _wire_shape(width, used), jnp.bfloat16),
        in_specs=[pl.BlockSpec(memory_space=pltpu.VMEM)] * 2,
        out_specs=pl.BlockSpec(memory_space=pltpu.VMEM),
        scratch_shapes=[pltpu.VMEM((GROUP * used, width), jnp.bfloat16)],
        compiler_params=pltpu.CompilerParams(vmem_limit_bytes=48 * 1024 * 1024),
    )(slot_ids_t, rows)


def _gather_tile(i, used, src_ref, dst):
    pieces = dst.shape[1] // LANE
    for jl in range(GROUP):
        j = i * GROUP + jl
        for q in range(pieces):
            dst[pl.ds(jl * used, used), pl.ds(q * LANE, LANE)] = src_ref[j, pl.ds(q * used, used), :]


def expert_kernel(x_ref, gate_ref, up_ref, down_ref, order_ref, out_ref, rows_in, rows_out):
    chunks, wire_rows, _ = x_ref.shape
    width = gate_ref.shape[0]
    pieces = width // LANE
    used = wire_rows // pieces

    def tile(i, carry):
        _gather_tile(i, used, x_ref, rows_in)
        rows = rows_in[...]
        gate_act = jnp.dot(rows, gate_ref[...], preferred_element_type=jnp.float32)
        up_act = jnp.dot(rows, up_ref[...], preferred_element_type=jnp.float32)
        inner_act = (gate_act / (1.0 + jnp.exp(-gate_act)) * up_act).astype(jnp.bfloat16)
        rows_out[...] = jnp.dot(
            inner_act, down_ref[...], preferred_element_type=jnp.float32
        ).astype(rows_out.dtype)
        for jl in range(GROUP):
            j = i * GROUP + jl
            for q in range(pieces):
                out_ref[j, pl.ds(q * used, used), :] = rows_out[
                    pl.ds(jl * used, used), pl.ds(q * LANE, LANE)
                ]
        return carry

    lax.fori_loop(0, chunks // GROUP, tile, 0)


def expert_block(arrived, gate_weights, up_weights, down_weights, order):
    chunks, wire_rows, _ = arrived.shape
    width = gate_weights.shape[1]
    used = wire_rows // (width // LANE)
    return pl.pallas_call(
        expert_kernel,
        out_shape=jax.ShapeDtypeStruct(arrived.shape, jnp.bfloat16),
        in_specs=[pl.BlockSpec(memory_space=pltpu.VMEM)] * 4 + [pl.BlockSpec(memory_space=pl.ANY)],
        out_specs=pl.BlockSpec(memory_space=pltpu.VMEM),
        scratch_shapes=[
            pltpu.VMEM((GROUP * used, width), jnp.bfloat16),
            pltpu.VMEM((GROUP * used, width), jnp.bfloat16),
        ],
        compiler_params=pltpu.CompilerParams(vmem_limit_bytes=60 * 1024 * 1024),
    )(arrived, gate_weights[0], up_weights[0], down_weights[0], order)


def combine_kernel(ret_ref, mix_ref, hidden_ref, out_ref, rows, total):
    chunks, wire_rows, _ = ret_ref.shape
    width = rows.shape[1]
    used = wire_rows // (width // LANE)
    tokens = hidden_ref.shape[0]
    total[...] = jnp.zeros(total.shape, total.dtype)

    def tile(i, carry):
        _gather_tile(i, used, ret_ref, rows)
        total[...] += jnp.dot(mix_ref[i], rows[...], preferred_element_type=jnp.float32)
        return carry

    lax.fori_loop(0, chunks // GROUP, tile, 0)
    both = total[...]
    out_ref[...] = (
        hidden_ref[...].astype(jnp.float32) + both[:tokens] + both[tokens:]
    ).astype(out_ref.dtype)


def combine(returned, mix_both, hidden):
    chunks, wire_rows, _ = returned.shape
    width = hidden.shape[1]
    used = wire_rows // (width // LANE)
    return pl.pallas_call(
        combine_kernel,
        out_shape=jax.ShapeDtypeStruct(hidden.shape, jnp.bfloat16),
        in_specs=[pl.BlockSpec(memory_space=pltpu.VMEM)] * 3,
        out_specs=pl.BlockSpec(memory_space=pltpu.VMEM),
        scratch_shapes=[
            pltpu.VMEM((GROUP * used, width), jnp.bfloat16),
            pltpu.VMEM((mix_both.shape[1], width), jnp.float32),
        ],
        compiler_params=pltpu.CompilerParams(vmem_limit_bytes=48 * 1024 * 1024),
    )(returned, mix_both, hidden)


def body(
    queries,
    cache_keys,
    cache_values,
    lengths,
    sinks,
    out_proj,
    decode_resid,
    prefill_hidden,
    norm_gain,
    router,
    routes,
    expert_gate,
    expert_up,
    expert_down,
):
    n_kv = lax.axis_size("kv")
    my_block = lax.axis_index("blk")
    per_block = queries.shape[0]
    head_count = sinks.shape[0]
    head_dim = cache_keys.shape[3]
    window = cache_keys.shape[1]
    my_lengths = lax.dynamic_slice_in_dim(lengths, my_block * per_block, per_block)
    first_valid = window - jnp.minimum(my_lengths, window)
    projected = attend_reduce(
        queries,
        cache_keys[:, :, 0, :],
        cache_values[:, :, 0, :],
        first_valid,
        sinks,
        out_proj,
        n_kv,
    )
    decoded = (decode_resid.astype(jnp.float32) + projected).astype(jnp.bfloat16)
    hidden = jnp.concatenate([decoded, prefill_hidden[0]], axis=0)
    hidden_f = hidden.astype(jnp.float32)
    mean_sq = jnp.mean(hidden_f * hidden_f, axis=1, keepdims=True)
    normed = (hidden_f * lax.rsqrt(mean_sq + EPSILON) * norm_gain).astype(jnp.bfloat16)

    experts = router.shape[1]
    chosen_ids = routes[0]
    tokens, top_k = chosen_ids.shape
    model_width = hidden.shape[1]
    capacity = 14
    logits = jnp.dot(normed, router, preferred_element_type=jnp.float32)
    one_hot = chosen_ids[..., None] == jnp.arange(experts, dtype=jnp.int32)
    chosen = jnp.sum(jnp.where(one_hot, logits[:, None, :], 0.0), axis=2)
    gate_probs = jax.nn.softmax(chosen, axis=1)
    row_hot = jnp.any(one_hot, axis=1).astype(jnp.int32)
    earlier = jnp.cumsum(row_hot, axis=0) - row_hot
    slot_rank = jnp.sum(jnp.where(one_hot, earlier[:, None, :], 0), axis=2)
    rank_hot = slot_rank[..., None] == jnp.arange(capacity, dtype=jnp.int32)
    fills = one_hot[..., None] & rank_hot[:, :, None, :]
    tiles = experts // GROUP
    tile_rows = GROUP * capacity
    slot_ids = chosen_ids * capacity + slot_rank
    outgoing = dispatch(slot_ids.T, normed, experts, capacity)
    mix = jnp.sum(jnp.where(fills, gate_probs[..., None, None], 0.0), axis=1)
    mix = mix.reshape(tokens, experts * capacity)
    mix_hi = mix.astype(jnp.bfloat16)
    mix_lo = (mix - mix_hi.astype(jnp.float32)).astype(jnp.bfloat16)
    mix_both = jnp.concatenate([mix_hi, mix_lo], axis=0)
    mix_tiles = mix_both.reshape(2 * tokens, tiles, tile_rows).transpose(1, 0, 2)
    arrived = lax.all_to_all(outgoing, ("kv", "blk"), split_axis=0, concat_axis=0, tiled=True)
    processed = expert_block(arrived, expert_gate, expert_up, expert_down, mix_tiles)
    returned = lax.all_to_all(processed, ("kv", "blk"), split_axis=0, concat_axis=0, tiled=True)
    layer_sum = combine(returned, mix_tiles, hidden)
    return layer_sum[None]


def solution(mesh):
    return jax.shard_map(
        body,
        mesh=mesh,
        in_specs=(
            P("blk", "kv"),
            P("blk", None, "kv", None),
            P("blk", None, "kv", None),
            P(),
            P("kv"),
            P("kv", None),
            P(("blk", "kv"), None),
            P(("blk", "kv"), None, None),
            P(),
            P(),
            P(("blk", "kv"), None, None),
            P(("kv", "blk"), None, None),
            P(("kv", "blk"), None, None),
            P(("kv", "blk"), None, None),
        ),
        out_specs=P(("blk", "kv"), None, None),
        check_vma=False,
    )
```

```python
import math

import jax
import jax.numpy as jnp
from jax import lax
from jax.experimental import pallas as pl
from jax.experimental.pallas import tpu as pltpu
from jax.sharding import PartitionSpec as P

NEG_FILL = -1e30
EPSILON = 1e-06
MESH = pl.DeviceIdType.MESH


def attend_reduce_kernel(
    n_kv, q_ref, k_ref, v_ref, first_ref, sink_ref, proj_ref, out_ref, att, part, held, send_sem, recv_sem
):
    me = lax.axis_index("kv")
    blk = lax.axis_index("blk")
    barrier = pltpu.get_barrier_semaphore()
    for step in range(1, n_kv):
        peer = lax.rem(me + step, n_kv)
        pl.semaphore_signal(barrier, inc=1, device_id=(peer, blk), device_id_type=MESH)
    requests, heads, head_dim = q_ref.shape
    window = k_ref.shape[1]
    scale = 1.0 / math.sqrt(head_dim)
    sink = sink_ref[...]
    positions = lax.broadcasted_iota(jnp.int32, (heads, window), 1)
    for r in range(requests):
        scores = lax.dot_general(
            q_ref[r], k_ref[r], (((1,), (1,)), ((), ())), preferred_element_type=jnp.float32
        ) * scale
        valid = positions >= first_ref[pl.ds(r, 1), :]
        masked = jnp.where(valid, scores, NEG_FILL)
        top = jnp.maximum(jnp.max(masked, axis=1, keepdims=True), sink)
        weights = jnp.where(valid, jnp.exp(masked - top), 0.0)
        denominator = jnp.sum(weights, axis=1, keepdims=True) + jnp.exp(sink - top)
        numerator = jnp.dot(
            weights.astype(jnp.bfloat16), v_ref[r], preferred_element_type=jnp.float32
        )
        att[:, pl.ds(r, 1), :] = (numerator / denominator).astype(jnp.bfloat16).astype(
            jnp.float32
        )[:, None, :]
    total = jnp.zeros((requests, proj_ref.shape[1]), jnp.float32)
    for h in range(heads):
        total = total + jnp.dot(
            att[h].astype(jnp.bfloat16),
            proj_ref[pl.ds(h * head_dim, head_dim), :],
            preferred_element_type=jnp.float32,
        )
    part[...] = total[:, None, :]
    pl.semaphore_wait(barrier, n_kv - 1)
    for step in range(1, n_kv):
        peer = lax.rem(me + step, n_kv)
        pltpu.make_async_remote_copy(
            src_ref=part.at[peer],
            dst_ref=held.at[me],
            send_sem=send_sem.at[peer],
            recv_sem=recv_sem.at[me],
            device_id=(peer, blk),
            device_id_type=MESH,
        ).start()
    own = part[me]
    for step in range(1, n_kv):
        peer = lax.rem(me + step, n_kv)
        arrival = pltpu.make_async_remote_copy(
            src_ref=part.at[peer],
            dst_ref=held.at[peer],
            send_sem=send_sem.at[peer],
            recv_sem=recv_sem.at[peer],
            device_id=(peer, blk),
            device_id_type=MESH,
        )
        arrival.wait_send()
        arrival.wait_recv()
    for step in range(1, n_kv):
        peer = lax.rem(me + step, n_kv)
        own = own + held[peer]
    out_ref[...] = own


def attend_reduce(queries, keys, values, first_valid, sinks, out_proj, n_kv):
    requests = queries.shape[0]
    heads = sinks.shape[0]
    head_dim = keys.shape[2]
    width = out_proj.shape[1]
    return pl.pallas_call(
        lambda *refs: attend_reduce_kernel(n_kv, *refs),
        out_shape=jax.ShapeDtypeStruct((1, width), jnp.float32),
        in_specs=[pl.BlockSpec(memory_space=pltpu.VMEM)] * 6,
        out_specs=pl.BlockSpec(memory_space=pltpu.VMEM),
        scratch_shapes=[
            pltpu.VMEM((heads, requests, head_dim), jnp.float32),
            pltpu.VMEM((requests, 1, width), jnp.float32),
            pltpu.VMEM((n_kv, 1, width), jnp.float32),
            pltpu.SemaphoreType.DMA((n_kv,)),
            pltpu.SemaphoreType.DMA((n_kv,)),
        ],
        compiler_params=pltpu.CompilerParams(
            collective_id=0, has_side_effects=True, vmem_limit_bytes=48 * 1024 * 1024
        ),
    )(
        queries.reshape(requests, heads, head_dim),
        keys,
        values,
        first_valid.reshape(requests, 1),
        sinks.reshape(heads, 1),
        out_proj,
    )


LANE = 256
GROUP = 16


def _wire_shape(width, used):
    return ((width // LANE) * used, LANE)


def dispatch_kernel(used, ids_ref, rows_ref, out_ref, staged):
    chunks = out_ref.shape[0]
    pieces = rows_ref.shape[1] // LANE
    tile_rows = GROUP * used
    top_k, tokens = ids_ref.shape

    def tile(i, carry):
        slot = lax.broadcasted_iota(jnp.int32, (tile_rows, tokens), 0) + i * tile_rows
        ids = ids_ref[...]
        hit = slot == ids[0:1, :]
        for k in range(1, top_k):
            hit = jnp.logical_or(hit, slot == ids[k : k + 1, :])
        staged[...] = jnp.dot(
            hit.astype(jnp.bfloat16), rows_ref[...], preferred_element_type=jnp.float32
        ).astype(staged.dtype)
        for jl in range(GROUP):
            j = i * GROUP + jl
            for q in range(pieces):
                out_ref[j, pl.ds(q * used, used), :] = staged[
                    pl.ds(jl * used, used), pl.ds(q * LANE, LANE)
                ]
        return carry

    lax.fori_loop(0, chunks // GROUP, tile, 0)


def dispatch(slot_ids_t, rows, chunks, used):
    width = rows.shape[1]
    return pl.pallas_call(
        lambda *refs: dispatch_kernel(used, *refs),
        out_shape=jax.ShapeDtypeStruct((chunks,) + _wire_shape(width, used), jnp.bfloat16),
        in_specs=[pl.BlockSpec(memory_space=pltpu.VMEM)] * 2,
        out_specs=pl.BlockSpec(memory_space=pltpu.VMEM),
        scratch_shapes=[pltpu.VMEM((GROUP * used, width), jnp.bfloat16)],
        compiler_params=pltpu.CompilerParams(vmem_limit_bytes=48 * 1024 * 1024),
    )(slot_ids_t, rows)


def _gather_tile(i, used, src_ref, dst):
    pieces = dst.shape[1] // LANE
    for jl in range(GROUP):
        j = i * GROUP + jl
        for q in range(pieces):
            dst[pl.ds(jl * used, used), pl.ds(q * LANE, LANE)] = src_ref[j, pl.ds(q * used, used), :]


def expert_kernel(x_ref, gate_ref, up_ref, down_ref, order_ref, out_ref, rows_in, rows_out):
    chunks, wire_rows, _ = x_ref.shape
    width = gate_ref.shape[0]
    pieces = width // LANE
    used = wire_rows // pieces

    def tile(i, carry):
        _gather_tile(i, used, x_ref, rows_in)
        rows = rows_in[...]
        gate_act = jnp.dot(rows, gate_ref[...], preferred_element_type=jnp.float32)
        up_act = jnp.dot(rows, up_ref[...], preferred_element_type=jnp.float32)
        inner_act = (gate_act / (1.0 + jnp.exp(-gate_act)) * up_act).astype(jnp.bfloat16)
        rows_out[...] = jnp.dot(
            inner_act, down_ref[...], preferred_element_type=jnp.float32
        ).astype(rows_out.dtype)
        for jl in range(GROUP):
            j = i * GROUP + jl
            for q in range(pieces):
                out_ref[j, pl.ds(q * used, used), :] = rows_out[
                    pl.ds(jl * used, used), pl.ds(q * LANE, LANE)
                ]
        return carry

    lax.fori_loop(0, chunks // GROUP, tile, 0)


def expert_block(arrived, gate_weights, up_weights, down_weights, order):
    chunks, wire_rows, _ = arrived.shape
    width = gate_weights.shape[1]
    used = wire_rows // (width // LANE)
    return pl.pallas_call(
        expert_kernel,
        out_shape=jax.ShapeDtypeStruct(arrived.shape, jnp.bfloat16),
        in_specs=[pl.BlockSpec(memory_space=pltpu.VMEM)] * 4 + [pl.BlockSpec(memory_space=pl.ANY)],
        out_specs=pl.BlockSpec(memory_space=pltpu.VMEM),
        scratch_shapes=[
            pltpu.VMEM((GROUP * used, width), jnp.bfloat16),
            pltpu.VMEM((GROUP * used, width), jnp.bfloat16),
        ],
        compiler_params=pltpu.CompilerParams(vmem_limit_bytes=60 * 1024 * 1024),
    )(arrived, gate_weights[0], up_weights[0], down_weights[0], order)


def combine_kernel(ret_ref, mix_ref, hidden_ref, out_ref, rows, total):
    chunks, wire_rows, _ = ret_ref.shape
    width = rows.shape[1]
    used = wire_rows // (width // LANE)
    tokens = hidden_ref.shape[0]
    total[...] = jnp.zeros(total.shape, total.dtype)

    def tile(i, carry):
        _gather_tile(i, used, ret_ref, rows)
        total[...] += jnp.dot(mix_ref[i], rows[...], preferred_element_type=jnp.float32)
        return carry

    lax.fori_loop(0, chunks // GROUP, tile, 0)
    both = total[...]
    out_ref[...] = (
        hidden_ref[...].astype(jnp.float32) + both[:tokens] + both[tokens:]
    ).astype(out_ref.dtype)


def combine(returned, mix_both, hidden):
    chunks, wire_rows, _ = returned.shape
    width = hidden.shape[1]
    used = wire_rows // (width // LANE)
    return pl.pallas_call(
        combine_kernel,
        out_shape=jax.ShapeDtypeStruct(hidden.shape, jnp.bfloat16),
        in_specs=[pl.BlockSpec(memory_space=pltpu.VMEM)] * 3,
        out_specs=pl.BlockSpec(memory_space=pltpu.VMEM),
        scratch_shapes=[
            pltpu.VMEM((GROUP * used, width), jnp.bfloat16),
            pltpu.VMEM((mix_both.shape[1], width), jnp.float32),
        ],
        compiler_params=pltpu.CompilerParams(vmem_limit_bytes=48 * 1024 * 1024),
    )(returned, mix_both, hidden)


def body(
    queries,
    cache_keys,
    cache_values,
    lengths,
    sinks,
    out_proj,
    decode_resid,
    prefill_hidden,
    norm_gain,
    router,
    routes,
    expert_gate,
    expert_up,
    expert_down,
):
    n_kv = lax.axis_size("kv")
    my_block = lax.axis_index("blk")
    per_block = queries.shape[0]
    head_count = sinks.shape[0]
    head_dim = cache_keys.shape[3]
    window = cache_keys.shape[1]
    my_lengths = lax.dynamic_slice_in_dim(lengths, my_block * per_block, per_block)
    first_valid = window - jnp.minimum(my_lengths, window)
    projected = attend_reduce(
        queries,
        cache_keys[:, :, 0, :],
        cache_values[:, :, 0, :],
        first_valid,
        sinks,
        out_proj,
        n_kv,
    )
    decoded = (decode_resid.astype(jnp.float32) + projected).astype(jnp.bfloat16)
    hidden = jnp.concatenate([decoded, prefill_hidden[0]], axis=0)
    hidden_f = hidden.astype(jnp.float32)
    mean_sq = jnp.mean(hidden_f * hidden_f, axis=1, keepdims=True)
    normed = (hidden_f * lax.rsqrt(mean_sq + EPSILON) * norm_gain).astype(jnp.bfloat16)

    experts = router.shape[1]
    chosen_ids = routes[0]
    tokens, top_k = chosen_ids.shape
    model_width = hidden.shape[1]
    capacity = 14
    logits = jnp.dot(normed, router, preferred_element_type=jnp.float32)
    one_hot = chosen_ids[..., None] == jnp.arange(experts, dtype=jnp.int32)
    chosen = jnp.sum(jnp.where(one_hot, logits[:, None, :], 0.0), axis=2)
    gate_probs = jax.nn.softmax(chosen, axis=1)
    row_hot = jnp.any(one_hot, axis=1).astype(jnp.int32)
    earlier = jnp.cumsum(row_hot, axis=0) - row_hot
    slot_rank = jnp.sum(jnp.where(one_hot, earlier[:, None, :], 0), axis=2)
    rank_hot = slot_rank[..., None] == jnp.arange(capacity, dtype=jnp.int32)
    fills = one_hot[..., None] & rank_hot[:, :, None, :]
    tiles = experts // GROUP
    tile_rows = GROUP * capacity
    slot_ids = chosen_ids * capacity + slot_rank
    outgoing = dispatch(slot_ids.T, normed, experts, capacity)
    arrived = lax.all_to_all(outgoing, ("kv", "blk"), split_axis=0, concat_axis=0, tiled=True)
    processed = expert_block(arrived, expert_gate, expert_up, expert_down, gate_probs)
    returned = lax.all_to_all(processed, ("kv", "blk"), split_axis=0, concat_axis=0, tiled=True)
    mix = jnp.sum(jnp.where(fills, gate_probs[..., None, None], 0.0), axis=1)
    mix = mix.reshape(tokens, experts * capacity)
    mix_hi = mix.astype(jnp.bfloat16)
    mix_lo = (mix - mix_hi.astype(jnp.float32)).astype(jnp.bfloat16)
    mix_both = jnp.concatenate([mix_hi, mix_lo], axis=0)
    mix_tiles = mix_both.reshape(2 * tokens, tiles, tile_rows).transpose(1, 0, 2)
    layer_sum = combine(returned, mix_tiles, hidden)
    return layer_sum[None]


def solution(mesh):
    return jax.shard_map(
        body,
        mesh=mesh,
        in_specs=(
            P("blk", "kv"),
            P("blk", None, "kv", None),
            P("blk", None, "kv", None),
            P(),
            P("kv"),
            P("kv", None),
            P(("blk", "kv"), None),
            P(("blk", "kv"), None, None),
            P(),
            P(),
            P(("blk", "kv"), None, None),
            P(("kv", "blk"), None, None),
            P(("kv", "blk"), None, None),
            P(("kv", "blk"), None, None),
        ),
        out_specs=P(("blk", "kv"), None, None),
        check_vma=False,
    )
```

```python
import math

import jax
import jax.numpy as jnp
from jax import lax
from jax.experimental import pallas as pl
from jax.experimental.pallas import tpu as pltpu
from jax.sharding import PartitionSpec as P

NEG_FILL = -1e30
EPSILON = 1e-06
MESH = pl.DeviceIdType.MESH


def attend_reduce_kernel(
    n_kv, q_ref, k_ref, v_ref, first_ref, sink_ref, proj_ref, out_ref, att, part, held, send_sem, recv_sem
):
    me = lax.axis_index("kv")
    blk = lax.axis_index("blk")
    barrier = pltpu.get_barrier_semaphore()
    for step in range(1, n_kv):
        peer = lax.rem(me + step, n_kv)
        pl.semaphore_signal(barrier, inc=1, device_id=(peer, blk), device_id_type=MESH)
    requests, heads, head_dim = q_ref.shape
    window = k_ref.shape[1]
    scale = 1.0 / math.sqrt(head_dim)
    sink = sink_ref[...]
    positions = lax.broadcasted_iota(jnp.int32, (heads, window), 1)
    for r in range(requests):
        scores = lax.dot_general(
            q_ref[r], k_ref[r], (((1,), (1,)), ((), ())), preferred_element_type=jnp.float32
        ) * scale
        valid = positions >= first_ref[pl.ds(r, 1), :]
        masked = jnp.where(valid, scores, NEG_FILL)
        top = jnp.maximum(jnp.max(masked, axis=1, keepdims=True), sink)
        weights = jnp.where(valid, jnp.exp(masked - top), 0.0)
        denominator = jnp.sum(weights, axis=1, keepdims=True) + jnp.exp(sink - top)
        numerator = jnp.dot(
            weights.astype(jnp.bfloat16), v_ref[r], preferred_element_type=jnp.float32
        )
        attended = (numerator / denominator).astype(jnp.bfloat16)
        for h in range(heads):
            att[pl.ds(r, 1), pl.ds(h * head_dim, head_dim)] = attended[h : h + 1, :]
    total = jnp.dot(att[...], proj_ref[...], preferred_element_type=jnp.float32)
    part[...] = total[:, None, :]
    pl.semaphore_wait(barrier, n_kv - 1)
    for step in range(1, n_kv):
        peer = lax.rem(me + step, n_kv)
        pltpu.make_async_remote_copy(
            src_ref=part.at[peer],
            dst_ref=held.at[me],
            send_sem=send_sem.at[peer],
            recv_sem=recv_sem.at[me],
            device_id=(peer, blk),
            device_id_type=MESH,
        ).start()
    own = part[me]
    for step in range(1, n_kv):
        peer = lax.rem(me + step, n_kv)
        arrival = pltpu.make_async_remote_copy(
            src_ref=part.at[peer],
            dst_ref=held.at[peer],
            send_sem=send_sem.at[peer],
            recv_sem=recv_sem.at[peer],
            device_id=(peer, blk),
            device_id_type=MESH,
        )
        arrival.wait_send()
        arrival.wait_recv()
    for step in range(1, n_kv):
        peer = lax.rem(me + step, n_kv)
        own = own + held[peer]
    out_ref[...] = own


def attend_reduce(queries, keys, values, first_valid, sinks, out_proj, n_kv):
    requests = queries.shape[0]
    heads = sinks.shape[0]
    head_dim = keys.shape[2]
    width = out_proj.shape[1]
    return pl.pallas_call(
        lambda *refs: attend_reduce_kernel(n_kv, *refs),
        out_shape=jax.ShapeDtypeStruct((1, width), jnp.float32),
        in_specs=[pl.BlockSpec(memory_space=pltpu.VMEM)] * 6,
        out_specs=pl.BlockSpec(memory_space=pltpu.VMEM),
        scratch_shapes=[
            pltpu.VMEM((requests, heads * head_dim), jnp.bfloat16),
            pltpu.VMEM((requests, 1, width), jnp.float32),
            pltpu.VMEM((n_kv, 1, width), jnp.float32),
            pltpu.SemaphoreType.DMA((n_kv,)),
            pltpu.SemaphoreType.DMA((n_kv,)),
        ],
        compiler_params=pltpu.CompilerParams(
            collective_id=0, has_side_effects=True, vmem_limit_bytes=48 * 1024 * 1024
        ),
    )(
        queries.reshape(requests, heads, head_dim),
        keys,
        values,
        first_valid.reshape(requests, 1),
        sinks.reshape(heads, 1),
        out_proj,
    )


LANE = 256
GROUP = 16


def _wire_shape(width, used):
    return ((width // LANE) * used, LANE)


def dispatch_kernel(used, ids_ref, rows_ref, out_ref, staged):
    chunks = out_ref.shape[0]
    pieces = rows_ref.shape[1] // LANE
    tile_rows = GROUP * used
    top_k, tokens = ids_ref.shape

    def tile(i, carry):
        slot = lax.broadcasted_iota(jnp.int32, (tile_rows, tokens), 0) + i * tile_rows
        ids = ids_ref[...]
        hit = slot == ids[0:1, :]
        for k in range(1, top_k):
            hit = jnp.logical_or(hit, slot == ids[k : k + 1, :])
        staged[...] = jnp.dot(
            hit.astype(jnp.bfloat16), rows_ref[...], preferred_element_type=jnp.float32
        ).astype(staged.dtype)
        for jl in range(GROUP):
            j = i * GROUP + jl
            for q in range(pieces):
                out_ref[j, pl.ds(q * used, used), :] = staged[
                    pl.ds(jl * used, used), pl.ds(q * LANE, LANE)
                ]
        return carry

    lax.fori_loop(0, chunks // GROUP, tile, 0)


def dispatch(slot_ids_t, rows, chunks, used):
    width = rows.shape[1]
    return pl.pallas_call(
        lambda *refs: dispatch_kernel(used, *refs),
        out_shape=jax.ShapeDtypeStruct((chunks,) + _wire_shape(width, used), jnp.bfloat16),
        in_specs=[pl.BlockSpec(memory_space=pltpu.VMEM)] * 2,
        out_specs=pl.BlockSpec(memory_space=pltpu.VMEM),
        scratch_shapes=[pltpu.VMEM((GROUP * used, width), jnp.bfloat16)],
        compiler_params=pltpu.CompilerParams(vmem_limit_bytes=48 * 1024 * 1024),
    )(slot_ids_t, rows)


def _gather_tile(i, used, src_ref, dst):
    pieces = dst.shape[1] // LANE
    for jl in range(GROUP):
        j = i * GROUP + jl
        for q in range(pieces):
            dst[pl.ds(jl * used, used), pl.ds(q * LANE, LANE)] = src_ref[j, pl.ds(q * used, used), :]


def expert_kernel(x_ref, gate_ref, up_ref, down_ref, out_ref, rows_in, rows_out):
    chunks, wire_rows, _ = x_ref.shape
    width = gate_ref.shape[0]
    pieces = width // LANE
    used = wire_rows // pieces

    def tile(i, carry):
        _gather_tile(i, used, x_ref, rows_in)
        rows = rows_in[...]
        gate_act = jnp.dot(rows, gate_ref[...], preferred_element_type=jnp.float32)
        up_act = jnp.dot(rows, up_ref[...], preferred_element_type=jnp.float32)
        inner_act = (gate_act / (1.0 + jnp.exp(-gate_act)) * up_act).astype(jnp.bfloat16)
        rows_out[...] = jnp.dot(
            inner_act, down_ref[...], preferred_element_type=jnp.float32
        ).astype(rows_out.dtype)
        for jl in range(GROUP):
            j = i * GROUP + jl
            for q in range(pieces):
                out_ref[j, pl.ds(q * used, used), :] = rows_out[
                    pl.ds(jl * used, used), pl.ds(q * LANE, LANE)
                ]
        return carry

    lax.fori_loop(0, chunks // GROUP, tile, 0)


def expert_block(arrived, gate_weights, up_weights, down_weights):
    chunks, wire_rows, _ = arrived.shape
    width = gate_weights.shape[1]
    used = wire_rows // (width // LANE)
    return pl.pallas_call(
        expert_kernel,
        out_shape=jax.ShapeDtypeStruct(arrived.shape, jnp.bfloat16),
        in_specs=[pl.BlockSpec(memory_space=pltpu.VMEM)] * 4,
        out_specs=pl.BlockSpec(memory_space=pltpu.VMEM),
        scratch_shapes=[
            pltpu.VMEM((GROUP * used, width), jnp.bfloat16),
            pltpu.VMEM((GROUP * used, width), jnp.bfloat16),
        ],
        compiler_params=pltpu.CompilerParams(vmem_limit_bytes=60 * 1024 * 1024),
    )(arrived, gate_weights[0], up_weights[0], down_weights[0])


def combine_kernel(ret_ref, mix_ref, hidden_ref, out_ref, rows, total):
    chunks, wire_rows, _ = ret_ref.shape
    width = rows.shape[1]
    used = wire_rows // (width // LANE)
    tokens = hidden_ref.shape[0]
    total[...] = jnp.zeros(total.shape, total.dtype)

    def tile(i, carry):
        _gather_tile(i, used, ret_ref, rows)
        total[...] += jnp.dot(mix_ref[i], rows[...], preferred_element_type=jnp.float32)
        return carry

    lax.fori_loop(0, chunks // GROUP, tile, 0)
    both = total[...]
    out_ref[...] = (
        hidden_ref[...].astype(jnp.float32) + both[:tokens] + both[tokens:]
    ).astype(out_ref.dtype)


def combine(returned, mix_both, hidden):
    chunks, wire_rows, _ = returned.shape
    width = hidden.shape[1]
    used = wire_rows // (width // LANE)
    return pl.pallas_call(
        combine_kernel,
        out_shape=jax.ShapeDtypeStruct(hidden.shape, jnp.bfloat16),
        in_specs=[pl.BlockSpec(memory_space=pltpu.VMEM)] * 3,
        out_specs=pl.BlockSpec(memory_space=pltpu.VMEM),
        scratch_shapes=[
            pltpu.VMEM((GROUP * used, width), jnp.bfloat16),
            pltpu.VMEM((mix_both.shape[1], width), jnp.float32),
        ],
        compiler_params=pltpu.CompilerParams(vmem_limit_bytes=48 * 1024 * 1024),
    )(returned, mix_both, hidden)


def body(
    queries,
    cache_keys,
    cache_values,
    lengths,
    sinks,
    out_proj,
    decode_resid,
    prefill_hidden,
    norm_gain,
    router,
    routes,
    expert_gate,
    expert_up,
    expert_down,
):
    n_kv = lax.axis_size("kv")
    my_block = lax.axis_index("blk")
    per_block = queries.shape[0]
    head_count = sinks.shape[0]
    head_dim = cache_keys.shape[3]
    window = cache_keys.shape[1]
    my_lengths = lax.dynamic_slice_in_dim(lengths, my_block * per_block, per_block)
    first_valid = window - jnp.minimum(my_lengths, window)
    projected = attend_reduce(
        queries,
        cache_keys[:, :, 0, :],
        cache_values[:, :, 0, :],
        first_valid,
        sinks,
        out_proj,
        n_kv,
    )
    decoded = (decode_resid.astype(jnp.float32) + projected).astype(jnp.bfloat16)
    hidden = jnp.concatenate([decoded, prefill_hidden[0]], axis=0)
    hidden_f = hidden.astype(jnp.float32)
    mean_sq = jnp.mean(hidden_f * hidden_f, axis=1, keepdims=True)
    normed = (hidden_f * lax.rsqrt(mean_sq + EPSILON) * norm_gain).astype(jnp.bfloat16)

    experts = router.shape[1]
    chosen_ids = routes[0]
    tokens, top_k = chosen_ids.shape
    model_width = hidden.shape[1]
    capacity = 14
    logits = jnp.dot(normed, router, preferred_element_type=jnp.float32)
    one_hot = chosen_ids[..., None] == jnp.arange(experts, dtype=jnp.int32)
    chosen = jnp.sum(jnp.where(one_hot, logits[:, None, :], 0.0), axis=2)
    gate_probs = jax.nn.softmax(chosen, axis=1)
    row_hot = jnp.any(one_hot, axis=1).astype(jnp.int32)
    earlier = jnp.cumsum(row_hot, axis=0) - row_hot
    slot_rank = jnp.sum(jnp.where(one_hot, earlier[:, None, :], 0), axis=2)
    rank_hot = slot_rank[..., None] == jnp.arange(capacity, dtype=jnp.int32)
    fills = one_hot[..., None] & rank_hot[:, :, None, :]
    tiles = experts // GROUP
    tile_rows = GROUP * capacity
    slot_ids = chosen_ids * capacity + slot_rank
    outgoing = dispatch(slot_ids.T, normed, experts, capacity)
    arrived = lax.all_to_all(outgoing, ("kv", "blk"), split_axis=0, concat_axis=0, tiled=True)
    processed = expert_block(arrived, expert_gate, expert_up, expert_down)
    returned = lax.all_to_all(processed, ("kv", "blk"), split_axis=0, concat_axis=0, tiled=True)
    mix = jnp.sum(jnp.where(fills, gate_probs[..., None, None], 0.0), axis=1)
    mix = mix.reshape(tokens, experts * capacity)
    mix_hi = mix.astype(jnp.bfloat16)
    mix_lo = (mix - mix_hi.astype(jnp.float32)).astype(jnp.bfloat16)
    mix_both = jnp.concatenate([mix_hi, mix_lo], axis=0)
    mix_tiles = mix_both.reshape(2 * tokens, tiles, tile_rows).transpose(1, 0, 2)
    layer_sum = combine(returned, mix_tiles, hidden)
    return layer_sum[None]


def solution(mesh):
    return jax.shard_map(
        body,
        mesh=mesh,
        in_specs=(
            P("blk", "kv"),
            P("blk", None, "kv", None),
            P("blk", None, "kv", None),
            P(),
            P("kv"),
            P("kv", None),
            P(("blk", "kv"), None),
            P(("blk", "kv"), None, None),
            P(),
            P(),
            P(("blk", "kv"), None, None),
            P(("kv", "blk"), None, None),
            P(("kv", "blk"), None, None),
            P(("kv", "blk"), None, None),
        ),
        out_specs=P(("blk", "kv"), None, None),
        check_vma=False,
    )
```

```python
import math

import jax
import jax.numpy as jnp
from jax import lax
from jax.experimental import pallas as pl
from jax.experimental.pallas import tpu as pltpu
from jax.sharding import PartitionSpec as P

NEG_FILL = -1e30
EPSILON = 1e-06
MESH = pl.DeviceIdType.MESH


def attend_reduce_kernel(
    n_kv, q_ref, k_ref, v_ref, first_ref, sink_ref, proj_ref, out_ref, att, part, held, send_sem, recv_sem
):
    me = lax.axis_index("kv")
    blk = lax.axis_index("blk")
    barrier = pltpu.get_barrier_semaphore()
    for step in range(1, n_kv):
        peer = lax.rem(me + step, n_kv)
        pl.semaphore_signal(barrier, inc=1, device_id=(peer, blk), device_id_type=MESH)
    requests, heads, head_dim = q_ref.shape
    window = k_ref.shape[1]
    scale = 1.0 / math.sqrt(head_dim)
    sink = sink_ref[...]
    positions = lax.broadcasted_iota(jnp.int32, (heads, window), 1)
    for r in range(requests):
        scores = lax.dot_general(
            q_ref[r], k_ref[r], (((1,), (1,)), ((), ())), preferred_element_type=jnp.float32
        ) * scale
        valid = positions >= first_ref[pl.ds(r, 1), :]
        masked = jnp.where(valid, scores, NEG_FILL)
        top = jnp.maximum(jnp.max(masked, axis=1, keepdims=True), sink)
        weights = jnp.where(valid, jnp.exp(masked - top), 0.0)
        denominator = jnp.sum(weights, axis=1, keepdims=True) + jnp.exp(sink - top)
        numerator = jnp.dot(
            weights.astype(jnp.bfloat16), v_ref[r], preferred_element_type=jnp.float32
        )
        attended = (numerator / denominator).astype(jnp.bfloat16)
        for h in range(heads):
            att[pl.ds(r, 1), pl.ds(h * head_dim, head_dim)] = attended[h : h + 1, :]
    total = jnp.dot(att[...], proj_ref[...], preferred_element_type=jnp.float32)
    part[...] = total[:, None, :]
    pl.semaphore_wait(barrier, n_kv - 1)
    for step in range(1, n_kv):
        peer = lax.rem(me + step, n_kv)
        pltpu.make_async_remote_copy(
            src_ref=part.at[peer],
            dst_ref=held.at[me],
            send_sem=send_sem.at[peer],
            recv_sem=recv_sem.at[me],
            device_id=(peer, blk),
            device_id_type=MESH,
        ).start()
    own = part[me]
    for step in range(1, n_kv):
        peer = lax.rem(me + step, n_kv)
        arrival = pltpu.make_async_remote_copy(
            src_ref=part.at[peer],
            dst_ref=held.at[peer],
            send_sem=send_sem.at[peer],
            recv_sem=recv_sem.at[peer],
            device_id=(peer, blk),
            device_id_type=MESH,
        )
        arrival.wait_send()
        arrival.wait_recv()
    for step in range(1, n_kv):
        peer = lax.rem(me + step, n_kv)
        own = own + held[peer]
    out_ref[...] = own


def attend_reduce(queries, keys, values, first_valid, sinks, out_proj, n_kv):
    requests = queries.shape[0]
    heads = sinks.shape[0]
    head_dim = keys.shape[2]
    width = out_proj.shape[1]
    return pl.pallas_call(
        lambda *refs: attend_reduce_kernel(n_kv, *refs),
        out_shape=jax.ShapeDtypeStruct((1, width), jnp.float32),
        in_specs=[pl.BlockSpec(memory_space=pltpu.VMEM)] * 6,
        out_specs=pl.BlockSpec(memory_space=pltpu.VMEM),
        scratch_shapes=[
            pltpu.VMEM((requests, heads * head_dim), jnp.bfloat16),
            pltpu.VMEM((requests, 1, width), jnp.float32),
            pltpu.VMEM((n_kv, 1, width), jnp.float32),
            pltpu.SemaphoreType.DMA((n_kv,)),
            pltpu.SemaphoreType.DMA((n_kv,)),
        ],
        compiler_params=pltpu.CompilerParams(
            collective_id=0, has_side_effects=True, vmem_limit_bytes=48 * 1024 * 1024
        ),
    )(
        queries.reshape(requests, heads, head_dim),
        keys,
        values,
        first_valid.reshape(requests, 1),
        sinks.reshape(heads, 1),
        out_proj,
    )


LANE = 256
GROUP = 16
FFN_GROUP = 64


def _wire_shape(width, used):
    return ((width // LANE) * used, LANE)


def dispatch_kernel(used, ids_ref, rows_ref, out_ref, staged):
    chunks = out_ref.shape[0]
    pieces = rows_ref.shape[1] // LANE
    tile_rows = GROUP * used
    top_k, tokens = ids_ref.shape

    def tile(i, carry):
        slot = lax.broadcasted_iota(jnp.int32, (tile_rows, tokens), 0) + i * tile_rows
        ids = ids_ref[...]
        hit = slot == ids[0:1, :]
        for k in range(1, top_k):
            hit = jnp.logical_or(hit, slot == ids[k : k + 1, :])
        staged[...] = jnp.dot(
            hit.astype(jnp.bfloat16), rows_ref[...], preferred_element_type=jnp.float32
        ).astype(staged.dtype)
        for jl in range(GROUP):
            j = i * GROUP + jl
            for q in range(pieces):
                out_ref[j, pl.ds(q * used, used), :] = staged[
                    pl.ds(jl * used, used), pl.ds(q * LANE, LANE)
                ]
        return carry

    lax.fori_loop(0, chunks // GROUP, tile, 0)


def dispatch(slot_ids_t, rows, chunks, used):
    width = rows.shape[1]
    return pl.pallas_call(
        lambda *refs: dispatch_kernel(used, *refs),
        out_shape=jax.ShapeDtypeStruct((chunks,) + _wire_shape(width, used), jnp.bfloat16),
        in_specs=[pl.BlockSpec(memory_space=pltpu.VMEM)] * 2,
        out_specs=pl.BlockSpec(memory_space=pltpu.VMEM),
        scratch_shapes=[pltpu.VMEM((GROUP * used, width), jnp.bfloat16)],
        compiler_params=pltpu.CompilerParams(vmem_limit_bytes=48 * 1024 * 1024),
    )(slot_ids_t, rows)


def _gather_tile(i, used, src_ref, dst, group=GROUP):
    pieces = dst.shape[1] // LANE
    for jl in range(group):
        j = i * group + jl
        for q in range(pieces):
            dst[pl.ds(jl * used, used), pl.ds(q * LANE, LANE)] = src_ref[j, pl.ds(q * used, used), :]


def expert_kernel(x_ref, gate_ref, up_ref, down_ref, out_ref, rows_in, rows_out):
    chunks, wire_rows, _ = x_ref.shape
    width = gate_ref.shape[0]
    pieces = width // LANE
    used = wire_rows // pieces

    def tile(i, carry):
        _gather_tile(i, used, x_ref, rows_in, FFN_GROUP)
        rows = rows_in[...]
        gate_act = jnp.dot(rows, gate_ref[...], preferred_element_type=jnp.float32)
        up_act = jnp.dot(rows, up_ref[...], preferred_element_type=jnp.float32)
        inner_act = (gate_act / (1.0 + jnp.exp(-gate_act)) * up_act).astype(jnp.bfloat16)
        rows_out[...] = jnp.dot(
            inner_act, down_ref[...], preferred_element_type=jnp.float32
        ).astype(rows_out.dtype)
        for jl in range(FFN_GROUP):
            j = i * FFN_GROUP + jl
            for q in range(pieces):
                out_ref[j, pl.ds(q * used, used), :] = rows_out[
                    pl.ds(jl * used, used), pl.ds(q * LANE, LANE)
                ]
        return carry

    lax.fori_loop(0, chunks // FFN_GROUP, tile, 0)


def expert_block(arrived, gate_weights, up_weights, down_weights):
    chunks, wire_rows, _ = arrived.shape
    width = gate_weights.shape[1]
    used = wire_rows // (width // LANE)
    return pl.pallas_call(
        expert_kernel,
        out_shape=jax.ShapeDtypeStruct(arrived.shape, jnp.bfloat16),
        in_specs=[pl.BlockSpec(memory_space=pltpu.VMEM)] * 4,
        out_specs=pl.BlockSpec(memory_space=pltpu.VMEM),
        scratch_shapes=[
            pltpu.VMEM((FFN_GROUP * used, width), jnp.bfloat16),
            pltpu.VMEM((FFN_GROUP * used, width), jnp.bfloat16),
        ],
        compiler_params=pltpu.CompilerParams(vmem_limit_bytes=60 * 1024 * 1024),
    )(arrived, gate_weights[0], up_weights[0], down_weights[0])


def combine_kernel(ret_ref, mix_ref, hidden_ref, out_ref, rows, total):
    chunks, wire_rows, _ = ret_ref.shape
    width = rows.shape[1]
    used = wire_rows // (width // LANE)
    tokens = hidden_ref.shape[0]
    total[...] = jnp.zeros(total.shape, total.dtype)

    def tile(i, carry):
        _gather_tile(i, used, ret_ref, rows)
        total[...] += jnp.dot(mix_ref[i], rows[...], preferred_element_type=jnp.float32)
        return carry

    lax.fori_loop(0, chunks // GROUP, tile, 0)
    both = total[...]
    out_ref[...] = (
        hidden_ref[...].astype(jnp.float32) + both[:tokens] + both[tokens:]
    ).astype(out_ref.dtype)


def combine(returned, mix_both, hidden):
    chunks, wire_rows, _ = returned.shape
    width = hidden.shape[1]
    used = wire_rows // (width // LANE)
    return pl.pallas_call(
        combine_kernel,
        out_shape=jax.ShapeDtypeStruct(hidden.shape, jnp.bfloat16),
        in_specs=[pl.BlockSpec(memory_space=pltpu.VMEM)] * 3,
        out_specs=pl.BlockSpec(memory_space=pltpu.VMEM),
        scratch_shapes=[
            pltpu.VMEM((GROUP * used, width), jnp.bfloat16),
            pltpu.VMEM((mix_both.shape[1], width), jnp.float32),
        ],
        compiler_params=pltpu.CompilerParams(vmem_limit_bytes=48 * 1024 * 1024),
    )(returned, mix_both, hidden)


def body(
    queries,
    cache_keys,
    cache_values,
    lengths,
    sinks,
    out_proj,
    decode_resid,
    prefill_hidden,
    norm_gain,
    router,
    routes,
    expert_gate,
    expert_up,
    expert_down,
):
    n_kv = lax.axis_size("kv")
    my_block = lax.axis_index("blk")
    per_block = queries.shape[0]
    head_count = sinks.shape[0]
    head_dim = cache_keys.shape[3]
    window = cache_keys.shape[1]
    my_lengths = lax.dynamic_slice_in_dim(lengths, my_block * per_block, per_block)
    first_valid = window - jnp.minimum(my_lengths, window)
    projected = attend_reduce(
        queries,
        cache_keys[:, :, 0, :],
        cache_values[:, :, 0, :],
        first_valid,
        sinks,
        out_proj,
        n_kv,
    )
    decoded = (decode_resid.astype(jnp.float32) + projected).astype(jnp.bfloat16)
    hidden = jnp.concatenate([decoded, prefill_hidden[0]], axis=0)
    hidden_f = hidden.astype(jnp.float32)
    mean_sq = jnp.mean(hidden_f * hidden_f, axis=1, keepdims=True)
    normed = (hidden_f * lax.rsqrt(mean_sq + EPSILON) * norm_gain).astype(jnp.bfloat16)

    experts = router.shape[1]
    chosen_ids = routes[0]
    tokens, top_k = chosen_ids.shape
    model_width = hidden.shape[1]
    capacity = 14
    logits = jnp.dot(normed, router, preferred_element_type=jnp.float32)
    one_hot = chosen_ids[..., None] == jnp.arange(experts, dtype=jnp.int32)
    chosen = jnp.sum(jnp.where(one_hot, logits[:, None, :], 0.0), axis=2)
    gate_probs = jax.nn.softmax(chosen, axis=1)
    row_hot = jnp.any(one_hot, axis=1).astype(jnp.int32)
    earlier = jnp.cumsum(row_hot, axis=0) - row_hot
    slot_rank = jnp.sum(jnp.where(one_hot, earlier[:, None, :], 0), axis=2)
    rank_hot = slot_rank[..., None] == jnp.arange(capacity, dtype=jnp.int32)
    fills = one_hot[..., None] & rank_hot[:, :, None, :]
    tiles = experts // GROUP
    tile_rows = GROUP * capacity
    slot_ids = chosen_ids * capacity + slot_rank
    outgoing = dispatch(slot_ids.T, normed, experts, capacity)
    arrived = lax.all_to_all(outgoing, ("kv", "blk"), split_axis=0, concat_axis=0, tiled=True)
    processed = expert_block(arrived, expert_gate, expert_up, expert_down)
    returned = lax.all_to_all(processed, ("kv", "blk"), split_axis=0, concat_axis=0, tiled=True)
    mix = jnp.sum(jnp.where(fills, gate_probs[..., None, None], 0.0), axis=1)
    mix = mix.reshape(tokens, experts * capacity)
    mix_hi = mix.astype(jnp.bfloat16)
    mix_lo = (mix - mix_hi.astype(jnp.float32)).astype(jnp.bfloat16)
    mix_both = jnp.concatenate([mix_hi, mix_lo], axis=0)
    mix_tiles = mix_both.reshape(2 * tokens, tiles, tile_rows).transpose(1, 0, 2)
    layer_sum = combine(returned, mix_tiles, hidden)
    return layer_sum[None]


def solution(mesh):
    return jax.shard_map(
        body,
        mesh=mesh,
        in_specs=(
            P("blk", "kv"),
            P("blk", None, "kv", None),
            P("blk", None, "kv", None),
            P(),
            P("kv"),
            P("kv", None),
            P(("blk", "kv"), None),
            P(("blk", "kv"), None, None),
            P(),
            P(),
            P(("blk", "kv"), None, None),
            P(("kv", "blk"), None, None),
            P(("kv", "blk"), None, None),
            P(("kv", "blk"), None, None),
        ),
        out_specs=P(("blk", "kv"), None, None),
        check_vma=False,
    )
```

```python
import math

import jax
import jax.numpy as jnp
from jax import lax
from jax.experimental import pallas as pl
from jax.experimental.pallas import tpu as pltpu
from jax.sharding import PartitionSpec as P

NEG_FILL = -1e30
EPSILON = 1e-06
MESH = pl.DeviceIdType.MESH


def attend_reduce_kernel(
    n_kv, q_ref, k_ref, v_ref, first_ref, sink_ref, proj_ref, out_ref, att, part, held, send_sem, recv_sem
):
    me = lax.axis_index("kv")
    blk = lax.axis_index("blk")
    barrier = pltpu.get_barrier_semaphore()
    for step in range(1, n_kv):
        peer = lax.rem(me + step, n_kv)
        pl.semaphore_signal(barrier, inc=1, device_id=(peer, blk), device_id_type=MESH)
    requests, heads, head_dim = q_ref.shape
    window = k_ref.shape[1]
    scale = 1.0 / math.sqrt(head_dim)
    sink = sink_ref[...]
    positions = lax.broadcasted_iota(jnp.int32, (heads, window), 1)
    for r in range(requests):
        scores = lax.dot_general(
            q_ref[r], k_ref[r], (((1,), (1,)), ((), ())), preferred_element_type=jnp.float32
        ) * scale
        valid = positions >= first_ref[pl.ds(r, 1), :]
        masked = jnp.where(valid, scores, NEG_FILL)
        top = jnp.maximum(jnp.max(masked, axis=1, keepdims=True), sink)
        weights = jnp.where(valid, jnp.exp(masked - top), 0.0)
        denominator = jnp.sum(weights, axis=1, keepdims=True) + jnp.exp(sink - top)
        numerator = jnp.dot(
            weights.astype(jnp.bfloat16), v_ref[r], preferred_element_type=jnp.float32
        )
        attended = (numerator / denominator).astype(jnp.bfloat16)
        for h in range(heads):
            att[pl.ds(r, 1), pl.ds(h * head_dim, head_dim)] = attended[h : h + 1, :]
    total = jnp.dot(att[...], proj_ref[...], preferred_element_type=jnp.float32)
    part[...] = total[:, None, :]
    pl.semaphore_wait(barrier, n_kv - 1)
    for step in range(1, n_kv):
        peer = lax.rem(me + step, n_kv)
        pltpu.make_async_remote_copy(
            src_ref=part.at[peer],
            dst_ref=held.at[me],
            send_sem=send_sem.at[peer],
            recv_sem=recv_sem.at[me],
            device_id=(peer, blk),
            device_id_type=MESH,
        ).start()
    own = part[me]
    for step in range(1, n_kv):
        peer = lax.rem(me + step, n_kv)
        arrival = pltpu.make_async_remote_copy(
            src_ref=part.at[peer],
            dst_ref=held.at[peer],
            send_sem=send_sem.at[peer],
            recv_sem=recv_sem.at[peer],
            device_id=(peer, blk),
            device_id_type=MESH,
        )
        arrival.wait_send()
        arrival.wait_recv()
    for step in range(1, n_kv):
        peer = lax.rem(me + step, n_kv)
        own = own + held[peer]
    out_ref[...] = own


def attend_reduce(queries, keys, values, first_valid, sinks, out_proj, n_kv):
    requests = queries.shape[0]
    heads = sinks.shape[0]
    head_dim = keys.shape[2]
    width = out_proj.shape[1]
    return pl.pallas_call(
        lambda *refs: attend_reduce_kernel(n_kv, *refs),
        out_shape=jax.ShapeDtypeStruct((1, width), jnp.float32),
        in_specs=[pl.BlockSpec(memory_space=pltpu.VMEM)] * 6,
        out_specs=pl.BlockSpec(memory_space=pltpu.VMEM),
        scratch_shapes=[
            pltpu.VMEM((requests, heads * head_dim), jnp.bfloat16),
            pltpu.VMEM((requests, 1, width), jnp.float32),
            pltpu.VMEM((n_kv, 1, width), jnp.float32),
            pltpu.SemaphoreType.DMA((n_kv,)),
            pltpu.SemaphoreType.DMA((n_kv,)),
        ],
        compiler_params=pltpu.CompilerParams(
            collective_id=0, has_side_effects=True, vmem_limit_bytes=48 * 1024 * 1024
        ),
    )(
        queries.reshape(requests, heads, head_dim),
        keys,
        values,
        first_valid.reshape(requests, 1),
        sinks.reshape(heads, 1),
        out_proj,
    )


LANE = 256
GROUP = 32
FFN_GROUP = 64


def _wire_shape(width, used):
    return ((width // LANE) * used, LANE)


def dispatch_kernel(used, ids_ref, rows_ref, out_ref, staged):
    chunks = out_ref.shape[0]
    pieces = rows_ref.shape[1] // LANE
    tile_rows = GROUP * used
    top_k, tokens = ids_ref.shape

    def tile(i, carry):
        slot = lax.broadcasted_iota(jnp.int32, (tile_rows, tokens), 0) + i * tile_rows
        ids = ids_ref[...]
        hit = slot == ids[0:1, :]
        for k in range(1, top_k):
            hit = jnp.logical_or(hit, slot == ids[k : k + 1, :])
        staged[...] = jnp.dot(
            hit.astype(jnp.bfloat16), rows_ref[...], preferred_element_type=jnp.float32
        ).astype(staged.dtype)
        for jl in range(GROUP):
            j = i * GROUP + jl
            for q in range(pieces):
                out_ref[j, pl.ds(q * used, used), :] = staged[
                    pl.ds(jl * used, used), pl.ds(q * LANE, LANE)
                ]
        return carry

    lax.fori_loop(0, chunks // GROUP, tile, 0)


def dispatch(slot_ids_t, rows, chunks, used):
    width = rows.shape[1]
    return pl.pallas_call(
        lambda *refs: dispatch_kernel(used, *refs),
        out_shape=jax.ShapeDtypeStruct((chunks,) + _wire_shape(width, used), jnp.bfloat16),
        in_specs=[pl.BlockSpec(memory_space=pltpu.VMEM)] * 2,
        out_specs=pl.BlockSpec(memory_space=pltpu.VMEM),
        scratch_shapes=[pltpu.VMEM((GROUP * used, width), jnp.bfloat16)],
        compiler_params=pltpu.CompilerParams(vmem_limit_bytes=48 * 1024 * 1024),
    )(slot_ids_t, rows)


def _gather_tile(i, used, src_ref, dst, group=GROUP):
    pieces = dst.shape[1] // LANE
    for jl in range(group):
        j = i * group + jl
        for q in range(pieces):
            dst[pl.ds(jl * used, used), pl.ds(q * LANE, LANE)] = src_ref[j, pl.ds(q * used, used), :]


def expert_kernel(x_ref, gate_ref, up_ref, down_ref, out_ref, rows_in, rows_out):
    chunks, wire_rows, _ = x_ref.shape
    width = gate_ref.shape[0]
    pieces = width // LANE
    used = wire_rows // pieces

    def tile(i, carry):
        _gather_tile(i, used, x_ref, rows_in, FFN_GROUP)
        rows = rows_in[...]
        gate_act = jnp.dot(rows, gate_ref[...], preferred_element_type=jnp.float32)
        up_act = jnp.dot(rows, up_ref[...], preferred_element_type=jnp.float32)
        inner_act = (gate_act / (1.0 + jnp.exp(-gate_act)) * up_act).astype(jnp.bfloat16)
        rows_out[...] = jnp.dot(
            inner_act, down_ref[...], preferred_element_type=jnp.float32
        ).astype(rows_out.dtype)
        for jl in range(FFN_GROUP):
            j = i * FFN_GROUP + jl
            for q in range(pieces):
                out_ref[j, pl.ds(q * used, used), :] = rows_out[
                    pl.ds(jl * used, used), pl.ds(q * LANE, LANE)
                ]
        return carry

    lax.fori_loop(0, chunks // FFN_GROUP, tile, 0)


def expert_block(arrived, gate_weights, up_weights, down_weights):
    chunks, wire_rows, _ = arrived.shape
    width = gate_weights.shape[1]
    used = wire_rows // (width // LANE)
    return pl.pallas_call(
        expert_kernel,
        out_shape=jax.ShapeDtypeStruct(arrived.shape, jnp.bfloat16),
        in_specs=[pl.BlockSpec(memory_space=pltpu.VMEM)] * 4,
        out_specs=pl.BlockSpec(memory_space=pltpu.VMEM),
        scratch_shapes=[
            pltpu.VMEM((FFN_GROUP * used, width), jnp.bfloat16),
            pltpu.VMEM((FFN_GROUP * used, width), jnp.bfloat16),
        ],
        compiler_params=pltpu.CompilerParams(vmem_limit_bytes=60 * 1024 * 1024),
    )(arrived, gate_weights[0], up_weights[0], down_weights[0])


def combine_kernel(ret_ref, mix_ref, hidden_ref, out_ref, rows, total):
    chunks, wire_rows, _ = ret_ref.shape
    width = rows.shape[1]
    used = wire_rows // (width // LANE)
    tokens = hidden_ref.shape[0]
    total[...] = jnp.zeros(total.shape, total.dtype)

    def tile(i, carry):
        _gather_tile(i, used, ret_ref, rows)
        total[...] += jnp.dot(mix_ref[i], rows[...], preferred_element_type=jnp.float32)
        return carry

    lax.fori_loop(0, chunks // GROUP, tile, 0)
    both = total[...]
    out_ref[...] = (
        hidden_ref[...].astype(jnp.float32) + both[:tokens] + both[tokens:]
    ).astype(out_ref.dtype)


def combine(returned, mix_both, hidden):
    chunks, wire_rows, _ = returned.shape
    width = hidden.shape[1]
    used = wire_rows // (width // LANE)
    return pl.pallas_call(
        combine_kernel,
        out_shape=jax.ShapeDtypeStruct(hidden.shape, jnp.bfloat16),
        in_specs=[pl.BlockSpec(memory_space=pltpu.VMEM)] * 3,
        out_specs=pl.BlockSpec(memory_space=pltpu.VMEM),
        scratch_shapes=[
            pltpu.VMEM((GROUP * used, width), jnp.bfloat16),
            pltpu.VMEM((mix_both.shape[1], width), jnp.float32),
        ],
        compiler_params=pltpu.CompilerParams(vmem_limit_bytes=48 * 1024 * 1024),
    )(returned, mix_both, hidden)


def body(
    queries,
    cache_keys,
    cache_values,
    lengths,
    sinks,
    out_proj,
    decode_resid,
    prefill_hidden,
    norm_gain,
    router,
    routes,
    expert_gate,
    expert_up,
    expert_down,
):
    n_kv = lax.axis_size("kv")
    my_block = lax.axis_index("blk")
    per_block = queries.shape[0]
    head_count = sinks.shape[0]
    head_dim = cache_keys.shape[3]
    window = cache_keys.shape[1]
    my_lengths = lax.dynamic_slice_in_dim(lengths, my_block * per_block, per_block)
    first_valid = window - jnp.minimum(my_lengths, window)
    projected = attend_reduce(
        queries,
        cache_keys[:, :, 0, :],
        cache_values[:, :, 0, :],
        first_valid,
        sinks,
        out_proj,
        n_kv,
    )
    decoded = (decode_resid.astype(jnp.float32) + projected).astype(jnp.bfloat16)
    hidden = jnp.concatenate([decoded, prefill_hidden[0]], axis=0)
    hidden_f = hidden.astype(jnp.float32)
    mean_sq = jnp.mean(hidden_f * hidden_f, axis=1, keepdims=True)
    normed = (hidden_f * lax.rsqrt(mean_sq + EPSILON) * norm_gain).astype(jnp.bfloat16)

    experts = router.shape[1]
    chosen_ids = routes[0]
    tokens, top_k = chosen_ids.shape
    model_width = hidden.shape[1]
    capacity = 14
    logits = jnp.dot(normed, router, preferred_element_type=jnp.float32)
    one_hot = chosen_ids[..., None] == jnp.arange(experts, dtype=jnp.int32)
    chosen = jnp.sum(jnp.where(one_hot, logits[:, None, :], 0.0), axis=2)
    gate_probs = jax.nn.softmax(chosen, axis=1)
    row_hot = jnp.any(one_hot, axis=1).astype(jnp.int32)
    earlier = jnp.cumsum(row_hot, axis=0) - row_hot
    slot_rank = jnp.sum(jnp.where(one_hot, earlier[:, None, :], 0), axis=2)
    rank_hot = slot_rank[..., None] == jnp.arange(capacity, dtype=jnp.int32)
    fills = one_hot[..., None] & rank_hot[:, :, None, :]
    tiles = experts // GROUP
    tile_rows = GROUP * capacity
    slot_ids = chosen_ids * capacity + slot_rank
    outgoing = dispatch(slot_ids.T, normed, experts, capacity)
    arrived = lax.all_to_all(outgoing, ("kv", "blk"), split_axis=0, concat_axis=0, tiled=True)
    processed = expert_block(arrived, expert_gate, expert_up, expert_down)
    returned = lax.all_to_all(processed, ("kv", "blk"), split_axis=0, concat_axis=0, tiled=True)
    mix = jnp.sum(jnp.where(fills, gate_probs[..., None, None], 0.0), axis=1)
    mix = mix.reshape(tokens, experts * capacity)
    mix_hi = mix.astype(jnp.bfloat16)
    mix_lo = (mix - mix_hi.astype(jnp.float32)).astype(jnp.bfloat16)
    mix_both = jnp.concatenate([mix_hi, mix_lo], axis=0)
    mix_tiles = mix_both.reshape(2 * tokens, tiles, tile_rows).transpose(1, 0, 2)
    layer_sum = combine(returned, mix_tiles, hidden)
    return layer_sum[None]


def solution(mesh):
    return jax.shard_map(
        body,
        mesh=mesh,
        in_specs=(
            P("blk", "kv"),
            P("blk", None, "kv", None),
            P("blk", None, "kv", None),
            P(),
            P("kv"),
            P("kv", None),
            P(("blk", "kv"), None),
            P(("blk", "kv"), None, None),
            P(),
            P(),
            P(("blk", "kv"), None, None),
            P(("kv", "blk"), None, None),
            P(("kv", "blk"), None, None),
            P(("kv", "blk"), None, None),
        ),
        out_specs=P(("blk", "kv"), None, None),
        check_vma=False,
    )
```

```python
import math

import jax
import jax.numpy as jnp
from jax import lax
from jax.experimental import pallas as pl
from jax.experimental.pallas import tpu as pltpu
from jax.sharding import PartitionSpec as P

NEG_FILL = -1e30
EPSILON = 1e-06
MESH = pl.DeviceIdType.MESH


def attend_reduce_kernel(
    n_kv, q_ref, k_ref, v_ref, first_ref, sink_ref, proj_ref, out_ref, att, part, held, send_sem, recv_sem
):
    me = lax.axis_index("kv")
    blk = lax.axis_index("blk")
    barrier = pltpu.get_barrier_semaphore()
    for step in range(1, n_kv):
        peer = lax.rem(me + step, n_kv)
        pl.semaphore_signal(barrier, inc=1, device_id=(peer, blk), device_id_type=MESH)
    requests, heads, head_dim = q_ref.shape
    window = k_ref.shape[1]
    scale = 1.0 / math.sqrt(head_dim)
    sink = sink_ref[...]
    positions = lax.broadcasted_iota(jnp.int32, (heads, window), 1)
    for r in range(requests):
        scores = lax.dot_general(
            q_ref[r], k_ref[r], (((1,), (1,)), ((), ())), preferred_element_type=jnp.float32
        ) * scale
        valid = positions >= first_ref[pl.ds(r, 1), :]
        masked = jnp.where(valid, scores, NEG_FILL)
        top = jnp.maximum(jnp.max(masked, axis=1, keepdims=True), sink)
        weights = jnp.where(valid, jnp.exp(masked - top), 0.0)
        denominator = jnp.sum(weights, axis=1, keepdims=True) + jnp.exp(sink - top)
        numerator = jnp.dot(
            weights.astype(jnp.bfloat16), v_ref[r], preferred_element_type=jnp.float32
        )
        attended = (numerator / denominator).astype(jnp.bfloat16)
        for h in range(heads):
            att[pl.ds(r, 1), pl.ds(h * head_dim, head_dim)] = attended[h : h + 1, :]
    total = jnp.dot(att[...], proj_ref[...], preferred_element_type=jnp.float32)
    part[...] = total[:, None, :]
    pl.semaphore_wait(barrier, n_kv - 1)
    for step in range(1, n_kv):
        peer = lax.rem(me + step, n_kv)
        pltpu.make_async_remote_copy(
            src_ref=part.at[peer],
            dst_ref=held.at[me],
            send_sem=send_sem.at[peer],
            recv_sem=recv_sem.at[me],
            device_id=(peer, blk),
            device_id_type=MESH,
        ).start()
    own = part[me]
    for step in range(1, n_kv):
        peer = lax.rem(me + step, n_kv)
        arrival = pltpu.make_async_remote_copy(
            src_ref=part.at[peer],
            dst_ref=held.at[peer],
            send_sem=send_sem.at[peer],
            recv_sem=recv_sem.at[peer],
            device_id=(peer, blk),
            device_id_type=MESH,
        )
        arrival.wait_send()
        arrival.wait_recv()
    for step in range(1, n_kv):
        peer = lax.rem(me + step, n_kv)
        own = own + held[peer]
    out_ref[...] = own


def attend_reduce(queries, keys, values, first_valid, sinks, out_proj, n_kv):
    requests = queries.shape[0]
    heads = sinks.shape[0]
    head_dim = keys.shape[2]
    width = out_proj.shape[1]
    return pl.pallas_call(
        lambda *refs: attend_reduce_kernel(n_kv, *refs),
        out_shape=jax.ShapeDtypeStruct((1, width), jnp.float32),
        in_specs=[pl.BlockSpec(memory_space=pltpu.VMEM)] * 6,
        out_specs=pl.BlockSpec(memory_space=pltpu.VMEM),
        scratch_shapes=[
            pltpu.VMEM((requests, heads * head_dim), jnp.bfloat16),
            pltpu.VMEM((requests, 1, width), jnp.float32),
            pltpu.VMEM((n_kv, 1, width), jnp.float32),
            pltpu.SemaphoreType.DMA((n_kv,)),
            pltpu.SemaphoreType.DMA((n_kv,)),
        ],
        compiler_params=pltpu.CompilerParams(
            collective_id=0, has_side_effects=True, vmem_limit_bytes=48 * 1024 * 1024
        ),
    )(
        queries.reshape(requests, heads, head_dim),
        keys,
        values,
        first_valid.reshape(requests, 1),
        sinks.reshape(heads, 1),
        out_proj,
    )


LANE = 256
GROUP = 64
FFN_GROUP = 64


def _wire_shape(width, used):
    return ((width // LANE) * used, LANE)


def dispatch_kernel(used, ids_ref, rows_ref, out_ref, staged):
    chunks = out_ref.shape[0]
    pieces = rows_ref.shape[1] // LANE
    tile_rows = GROUP * used
    top_k, tokens = ids_ref.shape

    def tile(i, carry):
        slot = lax.broadcasted_iota(jnp.int32, (tile_rows, tokens), 0) + i * tile_rows
        ids = ids_ref[...]
        hit = slot == ids[0:1, :]
        for k in range(1, top_k):
            hit = jnp.logical_or(hit, slot == ids[k : k + 1, :])
        staged[...] = jnp.dot(
            hit.astype(jnp.bfloat16), rows_ref[...], preferred_element_type=jnp.float32
        ).astype(staged.dtype)
        for jl in range(GROUP):
            j = i * GROUP + jl
            for q in range(pieces):
                out_ref[j, pl.ds(q * used, used), :] = staged[
                    pl.ds(jl * used, used), pl.ds(q * LANE, LANE)
                ]
        return carry

    lax.fori_loop(0, chunks // GROUP, tile, 0)


def dispatch(slot_ids_t, rows, chunks, used):
    width = rows.shape[1]
    return pl.pallas_call(
        lambda *refs: dispatch_kernel(used, *refs),
        out_shape=jax.ShapeDtypeStruct((chunks,) + _wire_shape(width, used), jnp.bfloat16),
        in_specs=[pl.BlockSpec(memory_space=pltpu.VMEM)] * 2,
        out_specs=pl.BlockSpec(memory_space=pltpu.VMEM),
        scratch_shapes=[pltpu.VMEM((GROUP * used, width), jnp.bfloat16)],
        compiler_params=pltpu.CompilerParams(vmem_limit_bytes=48 * 1024 * 1024),
    )(slot_ids_t, rows)


def _gather_tile(i, used, src_ref, dst, group=GROUP):
    pieces = dst.shape[1] // LANE
    for jl in range(group):
        j = i * group + jl
        for q in range(pieces):
            dst[pl.ds(jl * used, used), pl.ds(q * LANE, LANE)] = src_ref[j, pl.ds(q * used, used), :]


def expert_kernel(x_ref, gate_ref, up_ref, down_ref, out_ref, rows_in, rows_out):
    chunks, wire_rows, _ = x_ref.shape
    width = gate_ref.shape[0]
    pieces = width // LANE
    used = wire_rows // pieces

    def tile(i, carry):
        _gather_tile(i, used, x_ref, rows_in, FFN_GROUP)
        rows = rows_in[...]
        gate_act = jnp.dot(rows, gate_ref[...], preferred_element_type=jnp.float32)
        up_act = jnp.dot(rows, up_ref[...], preferred_element_type=jnp.float32)
        inner_act = (gate_act / (1.0 + jnp.exp(-gate_act)) * up_act).astype(jnp.bfloat16)
        rows_out[...] = jnp.dot(
            inner_act, down_ref[...], preferred_element_type=jnp.float32
        ).astype(rows_out.dtype)
        for jl in range(FFN_GROUP):
            j = i * FFN_GROUP + jl
            for q in range(pieces):
                out_ref[j, pl.ds(q * used, used), :] = rows_out[
                    pl.ds(jl * used, used), pl.ds(q * LANE, LANE)
                ]
        return carry

    lax.fori_loop(0, chunks // FFN_GROUP, tile, 0)


def expert_block(arrived, gate_weights, up_weights, down_weights):
    chunks, wire_rows, _ = arrived.shape
    width = gate_weights.shape[1]
    used = wire_rows // (width // LANE)
    return pl.pallas_call(
        expert_kernel,
        out_shape=jax.ShapeDtypeStruct(arrived.shape, jnp.bfloat16),
        in_specs=[pl.BlockSpec(memory_space=pltpu.VMEM)] * 4,
        out_specs=pl.BlockSpec(memory_space=pltpu.VMEM),
        scratch_shapes=[
            pltpu.VMEM((FFN_GROUP * used, width), jnp.bfloat16),
            pltpu.VMEM((FFN_GROUP * used, width), jnp.bfloat16),
        ],
        compiler_params=pltpu.CompilerParams(vmem_limit_bytes=60 * 1024 * 1024),
    )(arrived, gate_weights[0], up_weights[0], down_weights[0])


def combine_kernel(ret_ref, mix_ref, hidden_ref, out_ref, rows, total):
    chunks, wire_rows, _ = ret_ref.shape
    width = rows.shape[1]
    used = wire_rows // (width // LANE)
    tokens = hidden_ref.shape[0]
    total[...] = jnp.zeros(total.shape, total.dtype)

    def tile(i, carry):
        _gather_tile(i, used, ret_ref, rows)
        total[...] += jnp.dot(mix_ref[i], rows[...], preferred_element_type=jnp.float32)
        return carry

    lax.fori_loop(0, chunks // GROUP, tile, 0)
    both = total[...]
    out_ref[...] = (
        hidden_ref[...].astype(jnp.float32) + both[:tokens] + both[tokens:]
    ).astype(out_ref.dtype)


def combine(returned, mix_both, hidden):
    chunks, wire_rows, _ = returned.shape
    width = hidden.shape[1]
    used = wire_rows // (width // LANE)
    return pl.pallas_call(
        combine_kernel,
        out_shape=jax.ShapeDtypeStruct(hidden.shape, jnp.bfloat16),
        in_specs=[pl.BlockSpec(memory_space=pltpu.VMEM)] * 3,
        out_specs=pl.BlockSpec(memory_space=pltpu.VMEM),
        scratch_shapes=[
            pltpu.VMEM((GROUP * used, width), jnp.bfloat16),
            pltpu.VMEM((mix_both.shape[1], width), jnp.float32),
        ],
        compiler_params=pltpu.CompilerParams(vmem_limit_bytes=48 * 1024 * 1024),
    )(returned, mix_both, hidden)


def body(
    queries,
    cache_keys,
    cache_values,
    lengths,
    sinks,
    out_proj,
    decode_resid,
    prefill_hidden,
    norm_gain,
    router,
    routes,
    expert_gate,
    expert_up,
    expert_down,
):
    n_kv = lax.axis_size("kv")
    my_block = lax.axis_index("blk")
    per_block = queries.shape[0]
    head_count = sinks.shape[0]
    head_dim = cache_keys.shape[3]
    window = cache_keys.shape[1]
    my_lengths = lax.dynamic_slice_in_dim(lengths, my_block * per_block, per_block)
    first_valid = window - jnp.minimum(my_lengths, window)
    projected = attend_reduce(
        queries,
        cache_keys[:, :, 0, :],
        cache_values[:, :, 0, :],
        first_valid,
        sinks,
        out_proj,
        n_kv,
    )
    decoded = (decode_resid.astype(jnp.float32) + projected).astype(jnp.bfloat16)
    hidden = jnp.concatenate([decoded, prefill_hidden[0]], axis=0)
    hidden_f = hidden.astype(jnp.float32)
    mean_sq = jnp.mean(hidden_f * hidden_f, axis=1, keepdims=True)
    normed = (hidden_f * lax.rsqrt(mean_sq + EPSILON) * norm_gain).astype(jnp.bfloat16)

    experts = router.shape[1]
    chosen_ids = routes[0]
    tokens, top_k = chosen_ids.shape
    model_width = hidden.shape[1]
    capacity = 14
    logits = jnp.dot(normed, router, preferred_element_type=jnp.float32)
    one_hot = chosen_ids[..., None] == jnp.arange(experts, dtype=jnp.int32)
    chosen = jnp.sum(jnp.where(one_hot, logits[:, None, :], 0.0), axis=2)
    gate_probs = jax.nn.softmax(chosen, axis=1)
    row_hot = jnp.any(one_hot, axis=1).astype(jnp.int32)
    earlier = jnp.cumsum(row_hot, axis=0) - row_hot
    slot_rank = jnp.sum(jnp.where(one_hot, earlier[:, None, :], 0), axis=2)
    rank_hot = slot_rank[..., None] == jnp.arange(capacity, dtype=jnp.int32)
    fills = one_hot[..., None] & rank_hot[:, :, None, :]
    tiles = experts // GROUP
    tile_rows = GROUP * capacity
    slot_ids = chosen_ids * capacity + slot_rank
    outgoing = dispatch(slot_ids.T, normed, experts, capacity)
    arrived = lax.all_to_all(outgoing, ("kv", "blk"), split_axis=0, concat_axis=0, tiled=True)
    processed = expert_block(arrived, expert_gate, expert_up, expert_down)
    returned = lax.all_to_all(processed, ("kv", "blk"), split_axis=0, concat_axis=0, tiled=True)
    mix = jnp.sum(jnp.where(fills, gate_probs[..., None, None], 0.0), axis=1)
    mix = mix.reshape(tokens, experts * capacity)
    mix_hi = mix.astype(jnp.bfloat16)
    mix_lo = (mix - mix_hi.astype(jnp.float32)).astype(jnp.bfloat16)
    mix_both = jnp.concatenate([mix_hi, mix_lo], axis=0)
    mix_tiles = mix_both.reshape(2 * tokens, tiles, tile_rows).transpose(1, 0, 2)
    layer_sum = combine(returned, mix_tiles, hidden)
    return layer_sum[None]


def solution(mesh):
    return jax.shard_map(
        body,
        mesh=mesh,
        in_specs=(
            P("blk", "kv"),
            P("blk", None, "kv", None),
            P("blk", None, "kv", None),
            P(),
            P("kv"),
            P("kv", None),
            P(("blk", "kv"), None),
            P(("blk", "kv"), None, None),
            P(),
            P(),
            P(("blk", "kv"), None, None),
            P(("kv", "blk"), None, None),
            P(("kv", "blk"), None, None),
            P(("kv", "blk"), None, None),
        ),
        out_specs=P(("blk", "kv"), None, None),
        check_vma=False,
    )
```

```python
import math

import jax
import jax.numpy as jnp
from jax import lax
from jax.experimental import pallas as pl
from jax.experimental.pallas import tpu as pltpu
from jax.sharding import PartitionSpec as P

NEG_FILL = -1e30
EPSILON = 1e-06
MESH = pl.DeviceIdType.MESH


def attend_reduce_kernel(
    n_kv, q_ref, k_hbm, v_hbm, first_ref, sink_ref, proj_ref, out_ref, att, part, held, send_sem, recv_sem,
    k_ref, v_ref, load_sem
):
    me = lax.axis_index("kv")
    blk = lax.axis_index("blk")
    barrier = pltpu.get_barrier_semaphore()
    for step in range(1, n_kv):
        peer = lax.rem(me + step, n_kv)
        pl.semaphore_signal(barrier, inc=1, device_id=(peer, blk), device_id_type=MESH)
    requests, heads, head_dim = q_ref.shape
    window = k_ref.shape[1]
    loads = []
    for r in range(requests):
        pair = (
            pltpu.make_async_copy(k_hbm.at[r], k_ref.at[r], load_sem.at[0, r]),
            pltpu.make_async_copy(v_hbm.at[r], v_ref.at[r], load_sem.at[1, r]),
        )
        pair[0].start()
        pair[1].start()
        loads.append(pair)
    scale = 1.0 / math.sqrt(head_dim)
    sink = sink_ref[...]
    positions = lax.broadcasted_iota(jnp.int32, (heads, window), 1)
    for r in range(requests):
        loads[r][0].wait()
        loads[r][1].wait()
        scores = lax.dot_general(
            q_ref[r], k_ref[r], (((1,), (1,)), ((), ())), preferred_element_type=jnp.float32
        ) * scale
        valid = positions >= first_ref[pl.ds(r, 1), :]
        masked = jnp.where(valid, scores, NEG_FILL)
        top = jnp.maximum(jnp.max(masked, axis=1, keepdims=True), sink)
        weights = jnp.where(valid, jnp.exp(masked - top), 0.0)
        denominator = jnp.sum(weights, axis=1, keepdims=True) + jnp.exp(sink - top)
        numerator = jnp.dot(
            weights.astype(jnp.bfloat16), v_ref[r], preferred_element_type=jnp.float32
        )
        attended = (numerator / denominator).astype(jnp.bfloat16)
        for h in range(heads):
            att[pl.ds(r, 1), pl.ds(h * head_dim, head_dim)] = attended[h : h + 1, :]
    total = jnp.dot(att[...], proj_ref[...], preferred_element_type=jnp.float32)
    part[...] = total[:, None, :]
    pl.semaphore_wait(barrier, n_kv - 1)
    for step in range(1, n_kv):
        peer = lax.rem(me + step, n_kv)
        pltpu.make_async_remote_copy(
            src_ref=part.at[peer],
            dst_ref=held.at[me],
            send_sem=send_sem.at[peer],
            recv_sem=recv_sem.at[me],
            device_id=(peer, blk),
            device_id_type=MESH,
        ).start()
    own = part[me]
    for step in range(1, n_kv):
        peer = lax.rem(me + step, n_kv)
        arrival = pltpu.make_async_remote_copy(
            src_ref=part.at[peer],
            dst_ref=held.at[peer],
            send_sem=send_sem.at[peer],
            recv_sem=recv_sem.at[peer],
            device_id=(peer, blk),
            device_id_type=MESH,
        )
        arrival.wait_send()
        arrival.wait_recv()
    for step in range(1, n_kv):
        peer = lax.rem(me + step, n_kv)
        own = own + held[peer]
    out_ref[...] = own


def attend_reduce(queries, keys, values, first_valid, sinks, out_proj, n_kv):
    requests = queries.shape[0]
    heads = sinks.shape[0]
    head_dim = keys.shape[2]
    width = out_proj.shape[1]
    return pl.pallas_call(
        lambda *refs: attend_reduce_kernel(n_kv, *refs),
        out_shape=jax.ShapeDtypeStruct((1, width), jnp.float32),
        in_specs=[pl.BlockSpec(memory_space=pltpu.VMEM)]
        + [pl.BlockSpec(memory_space=pl.ANY)] * 2
        + [pl.BlockSpec(memory_space=pltpu.VMEM)] * 3,
        out_specs=pl.BlockSpec(memory_space=pltpu.VMEM),
        scratch_shapes=[
            pltpu.VMEM((requests, heads * head_dim), jnp.bfloat16),
            pltpu.VMEM((requests, 1, width), jnp.float32),
            pltpu.VMEM((n_kv, 1, width), jnp.float32),
            pltpu.SemaphoreType.DMA((n_kv,)),
            pltpu.SemaphoreType.DMA((n_kv,)),
            pltpu.VMEM(keys.shape, keys.dtype),
            pltpu.VMEM(values.shape, values.dtype),
            pltpu.SemaphoreType.DMA((2, requests)),
        ],
        compiler_params=pltpu.CompilerParams(
            collective_id=0, has_side_effects=True, vmem_limit_bytes=48 * 1024 * 1024
        ),
    )(
        queries.reshape(requests, heads, head_dim),
        keys,
        values,
        first_valid.reshape(requests, 1),
        sinks.reshape(heads, 1),
        out_proj,
    )


LANE = 256
GROUP = 64
FFN_GROUP = 64


def _wire_shape(width, used):
    return ((width // LANE) * used, LANE)


def dispatch_kernel(used, ids_ref, rows_ref, out_ref, staged):
    chunks = out_ref.shape[0]
    pieces = rows_ref.shape[1] // LANE
    tile_rows = GROUP * used
    top_k, tokens = ids_ref.shape

    def tile(i, carry):
        slot = lax.broadcasted_iota(jnp.int32, (tile_rows, tokens), 0) + i * tile_rows
        ids = ids_ref[...]
        hit = slot == ids[0:1, :]
        for k in range(1, top_k):
            hit = jnp.logical_or(hit, slot == ids[k : k + 1, :])
        staged[...] = jnp.dot(
            hit.astype(jnp.bfloat16), rows_ref[...], preferred_element_type=jnp.float32
        ).astype(staged.dtype)
        for jl in range(GROUP):
            j = i * GROUP + jl
            for q in range(pieces):
                out_ref[j, pl.ds(q * used, used), :] = staged[
                    pl.ds(jl * used, used), pl.ds(q * LANE, LANE)
                ]
        return carry

    lax.fori_loop(0, chunks // GROUP, tile, 0)


def dispatch(slot_ids_t, rows, chunks, used):
    width = rows.shape[1]
    return pl.pallas_call(
        lambda *refs: dispatch_kernel(used, *refs),
        out_shape=jax.ShapeDtypeStruct((chunks,) + _wire_shape(width, used), jnp.bfloat16),
        in_specs=[pl.BlockSpec(memory_space=pltpu.VMEM)] * 2,
        out_specs=pl.BlockSpec(memory_space=pltpu.VMEM),
        scratch_shapes=[pltpu.VMEM((GROUP * used, width), jnp.bfloat16)],
        compiler_params=pltpu.CompilerParams(vmem_limit_bytes=48 * 1024 * 1024),
    )(slot_ids_t, rows)


def _gather_tile(i, used, src_ref, dst, group=GROUP):
    pieces = dst.shape[1] // LANE
    for jl in range(group):
        j = i * group + jl
        for q in range(pieces):
            dst[pl.ds(jl * used, used), pl.ds(q * LANE, LANE)] = src_ref[j, pl.ds(q * used, used), :]


def expert_kernel(x_ref, gate_ref, up_ref, down_ref, out_ref, rows_in, rows_out):
    chunks, wire_rows, _ = x_ref.shape
    width = gate_ref.shape[0]
    pieces = width // LANE
    used = wire_rows // pieces

    def tile(i, carry):
        _gather_tile(i, used, x_ref, rows_in, FFN_GROUP)
        rows = rows_in[...]
        gate_act = jnp.dot(rows, gate_ref[...], preferred_element_type=jnp.float32)
        up_act = jnp.dot(rows, up_ref[...], preferred_element_type=jnp.float32)
        inner_act = (gate_act / (1.0 + jnp.exp(-gate_act)) * up_act).astype(jnp.bfloat16)
        rows_out[...] = jnp.dot(
            inner_act, down_ref[...], preferred_element_type=jnp.float32
        ).astype(rows_out.dtype)
        for jl in range(FFN_GROUP):
            j = i * FFN_GROUP + jl
            for q in range(pieces):
                out_ref[j, pl.ds(q * used, used), :] = rows_out[
                    pl.ds(jl * used, used), pl.ds(q * LANE, LANE)
                ]
        return carry

    lax.fori_loop(0, chunks // FFN_GROUP, tile, 0)


def expert_block(arrived, gate_weights, up_weights, down_weights):
    chunks, wire_rows, _ = arrived.shape
    width = gate_weights.shape[1]
    used = wire_rows // (width // LANE)
    return pl.pallas_call(
        expert_kernel,
        out_shape=jax.ShapeDtypeStruct(arrived.shape, jnp.bfloat16),
        in_specs=[pl.BlockSpec(memory_space=pltpu.VMEM)] * 4,
        out_specs=pl.BlockSpec(memory_space=pltpu.VMEM),
        scratch_shapes=[
            pltpu.VMEM((FFN_GROUP * used, width), jnp.bfloat16),
            pltpu.VMEM((FFN_GROUP * used, width), jnp.bfloat16),
        ],
        compiler_params=pltpu.CompilerParams(vmem_limit_bytes=60 * 1024 * 1024),
    )(arrived, gate_weights[0], up_weights[0], down_weights[0])


def combine_kernel(ret_ref, mix_ref, hidden_ref, out_ref, rows, total):
    chunks, wire_rows, _ = ret_ref.shape
    width = rows.shape[1]
    used = wire_rows // (width // LANE)
    tokens = hidden_ref.shape[0]
    total[...] = jnp.zeros(total.shape, total.dtype)

    def tile(i, carry):
        _gather_tile(i, used, ret_ref, rows)
        total[...] += jnp.dot(mix_ref[i], rows[...], preferred_element_type=jnp.float32)
        return carry

    lax.fori_loop(0, chunks // GROUP, tile, 0)
    both = total[...]
    out_ref[...] = (
        hidden_ref[...].astype(jnp.float32) + both[:tokens] + both[tokens:]
    ).astype(out_ref.dtype)


def combine(returned, mix_both, hidden):
    chunks, wire_rows, _ = returned.shape
    width = hidden.shape[1]
    used = wire_rows // (width // LANE)
    return pl.pallas_call(
        combine_kernel,
        out_shape=jax.ShapeDtypeStruct(hidden.shape, jnp.bfloat16),
        in_specs=[pl.BlockSpec(memory_space=pltpu.VMEM)] * 3,
        out_specs=pl.BlockSpec(memory_space=pltpu.VMEM),
        scratch_shapes=[
            pltpu.VMEM((GROUP * used, width), jnp.bfloat16),
            pltpu.VMEM((mix_both.shape[1], width), jnp.float32),
        ],
        compiler_params=pltpu.CompilerParams(vmem_limit_bytes=48 * 1024 * 1024),
    )(returned, mix_both, hidden)


def body(
    queries,
    cache_keys,
    cache_values,
    lengths,
    sinks,
    out_proj,
    decode_resid,
    prefill_hidden,
    norm_gain,
    router,
    routes,
    expert_gate,
    expert_up,
    expert_down,
):
    n_kv = lax.axis_size("kv")
    my_block = lax.axis_index("blk")
    per_block = queries.shape[0]
    head_count = sinks.shape[0]
    head_dim = cache_keys.shape[3]
    window = cache_keys.shape[1]
    my_lengths = lax.dynamic_slice_in_dim(lengths, my_block * per_block, per_block)
    first_valid = window - jnp.minimum(my_lengths, window)
    projected = attend_reduce(
        queries,
        cache_keys[:, :, 0, :],
        cache_values[:, :, 0, :],
        first_valid,
        sinks,
        out_proj,
        n_kv,
    )
    decoded = (decode_resid.astype(jnp.float32) + projected).astype(jnp.bfloat16)
    hidden = jnp.concatenate([decoded, prefill_hidden[0]], axis=0)
    hidden_f = hidden.astype(jnp.float32)
    mean_sq = jnp.mean(hidden_f * hidden_f, axis=1, keepdims=True)
    normed = (hidden_f * lax.rsqrt(mean_sq + EPSILON) * norm_gain).astype(jnp.bfloat16)

    experts = router.shape[1]
    chosen_ids = routes[0]
    tokens, top_k = chosen_ids.shape
    model_width = hidden.shape[1]
    capacity = 14
    logits = jnp.dot(normed, router, preferred_element_type=jnp.float32)
    one_hot = chosen_ids[..., None] == jnp.arange(experts, dtype=jnp.int32)
    chosen = jnp.sum(jnp.where(one_hot, logits[:, None, :], 0.0), axis=2)
    gate_probs = jax.nn.softmax(chosen, axis=1)
    row_hot = jnp.any(one_hot, axis=1).astype(jnp.int32)
    earlier = jnp.cumsum(row_hot, axis=0) - row_hot
    slot_rank = jnp.sum(jnp.where(one_hot, earlier[:, None, :], 0), axis=2)
    rank_hot = slot_rank[..., None] == jnp.arange(capacity, dtype=jnp.int32)
    fills = one_hot[..., None] & rank_hot[:, :, None, :]
    tiles = experts // GROUP
    tile_rows = GROUP * capacity
    slot_ids = chosen_ids * capacity + slot_rank
    outgoing = dispatch(slot_ids.T, normed, experts, capacity)
    arrived = lax.all_to_all(outgoing, ("kv", "blk"), split_axis=0, concat_axis=0, tiled=True)
    processed = expert_block(arrived, expert_gate, expert_up, expert_down)
    returned = lax.all_to_all(processed, ("kv", "blk"), split_axis=0, concat_axis=0, tiled=True)
    mix = jnp.sum(jnp.where(fills, gate_probs[..., None, None], 0.0), axis=1)
    mix = mix.reshape(tokens, experts * capacity)
    mix_hi = mix.astype(jnp.bfloat16)
    mix_lo = (mix - mix_hi.astype(jnp.float32)).astype(jnp.bfloat16)
    mix_both = jnp.concatenate([mix_hi, mix_lo], axis=0)
    mix_tiles = mix_both.reshape(2 * tokens, tiles, tile_rows).transpose(1, 0, 2)
    layer_sum = combine(returned, mix_tiles, hidden)
    return layer_sum[None]


def solution(mesh):
    return jax.shard_map(
        body,
        mesh=mesh,
        in_specs=(
            P("blk", "kv"),
            P("blk", None, "kv", None),
            P("blk", None, "kv", None),
            P(),
            P("kv"),
            P("kv", None),
            P(("blk", "kv"), None),
            P(("blk", "kv"), None, None),
            P(),
            P(),
            P(("blk", "kv"), None, None),
            P(("kv", "blk"), None, None),
            P(("kv", "blk"), None, None),
            P(("kv", "blk"), None, None),
        ),
        out_specs=P(("blk", "kv"), None, None),
        check_vma=False,
    )
```

```python
import math

import jax
import jax.numpy as jnp
from jax import lax
from jax.experimental import pallas as pl
from jax.experimental.pallas import tpu as pltpu
from jax.sharding import PartitionSpec as P

NEG_FILL = -1e30
EPSILON = 1e-06
MESH = pl.DeviceIdType.MESH


def attend_reduce_kernel(
    n_kv, q_ref, k_ref, v_ref, first_ref, sink_ref, proj_ref, out_ref, att, part, held, send_sem, recv_sem
):
    me = lax.axis_index("kv")
    blk = lax.axis_index("blk")
    barrier = pltpu.get_barrier_semaphore()
    for step in range(1, n_kv):
        peer = lax.rem(me + step, n_kv)
        pl.semaphore_signal(barrier, inc=1, device_id=(peer, blk), device_id_type=MESH)
    requests, heads, head_dim = q_ref.shape
    window = k_ref.shape[1]
    scale = 1.0 / math.sqrt(head_dim)
    sink = sink_ref[...]
    positions = lax.broadcasted_iota(jnp.int32, (heads, window), 1)
    for r in range(requests):
        scores = lax.dot_general(
            q_ref[r], k_ref[r], (((1,), (1,)), ((), ())), preferred_element_type=jnp.float32
        ) * scale
        valid = positions >= first_ref[pl.ds(r, 1), :]
        masked = jnp.where(valid, scores, NEG_FILL)
        top = jnp.maximum(jnp.max(masked, axis=1, keepdims=True), sink)
        weights = jnp.where(valid, jnp.exp(masked - top), 0.0)
        denominator = jnp.sum(weights, axis=1, keepdims=True) + jnp.exp(sink - top)
        numerator = jnp.dot(
            weights.astype(jnp.bfloat16), v_ref[r], preferred_element_type=jnp.float32
        )
        attended = (numerator / denominator).astype(jnp.bfloat16)
        for h in range(heads):
            att[pl.ds(r, 1), pl.ds(h * head_dim, head_dim)] = attended[h : h + 1, :]
    total = jnp.dot(att[...], proj_ref[...], preferred_element_type=jnp.float32)
    part[...] = total[:, None, :]
    pl.semaphore_wait(barrier, n_kv - 1)
    for step in range(1, n_kv):
        peer = lax.rem(me + step, n_kv)
        pltpu.make_async_remote_copy(
            src_ref=part.at[peer],
            dst_ref=held.at[me],
            send_sem=send_sem.at[peer],
            recv_sem=recv_sem.at[me],
            device_id=(peer, blk),
            device_id_type=MESH,
        ).start()
    own = part[me]
    for step in range(1, n_kv):
        peer = lax.rem(me + step, n_kv)
        arrival = pltpu.make_async_remote_copy(
            src_ref=part.at[peer],
            dst_ref=held.at[peer],
            send_sem=send_sem.at[peer],
            recv_sem=recv_sem.at[peer],
            device_id=(peer, blk),
            device_id_type=MESH,
        )
        arrival.wait_send()
        arrival.wait_recv()
    for step in range(1, n_kv):
        peer = lax.rem(me + step, n_kv)
        own = own + held[peer]
    out_ref[...] = own


def attend_reduce(queries, keys, values, first_valid, sinks, out_proj, n_kv):
    requests = queries.shape[0]
    heads = sinks.shape[0]
    head_dim = keys.shape[2]
    width = out_proj.shape[1]
    return pl.pallas_call(
        lambda *refs: attend_reduce_kernel(n_kv, *refs),
        out_shape=jax.ShapeDtypeStruct((1, width), jnp.float32),
        in_specs=[pl.BlockSpec(memory_space=pltpu.VMEM)] * 6,
        out_specs=pl.BlockSpec(memory_space=pltpu.VMEM),
        scratch_shapes=[
            pltpu.VMEM((requests, heads * head_dim), jnp.bfloat16),
            pltpu.VMEM((requests, 1, width), jnp.float32),
            pltpu.VMEM((n_kv, 1, width), jnp.float32),
            pltpu.SemaphoreType.DMA((n_kv,)),
            pltpu.SemaphoreType.DMA((n_kv,)),
        ],
        compiler_params=pltpu.CompilerParams(
            collective_id=0, has_side_effects=True, vmem_limit_bytes=48 * 1024 * 1024
        ),
    )(
        queries.reshape(requests, heads, head_dim),
        keys,
        values,
        first_valid.reshape(requests, 1),
        sinks.reshape(heads, 1),
        out_proj,
    )


LANE = 256
GROUP = 64
FFN_GROUP = 128


def _wire_shape(width, used):
    return ((width // LANE) * used, LANE)


def dispatch_kernel(used, ids_ref, rows_ref, out_ref, staged):
    chunks = out_ref.shape[0]
    pieces = rows_ref.shape[1] // LANE
    tile_rows = GROUP * used
    top_k, tokens = ids_ref.shape

    def tile(i, carry):
        slot = lax.broadcasted_iota(jnp.int32, (tile_rows, tokens), 0) + i * tile_rows
        ids = ids_ref[...]
        hit = slot == ids[0:1, :]
        for k in range(1, top_k):
            hit = jnp.logical_or(hit, slot == ids[k : k + 1, :])
        staged[...] = jnp.dot(
            hit.astype(jnp.bfloat16), rows_ref[...], preferred_element_type=jnp.float32
        ).astype(staged.dtype)
        for jl in range(GROUP):
            j = i * GROUP + jl
            for q in range(pieces):
                out_ref[j, pl.ds(q * used, used), :] = staged[
                    pl.ds(jl * used, used), pl.ds(q * LANE, LANE)
                ]
        return carry

    lax.fori_loop(0, chunks // GROUP, tile, 0)


def dispatch(slot_ids_t, rows, chunks, used):
    width = rows.shape[1]
    return pl.pallas_call(
        lambda *refs: dispatch_kernel(used, *refs),
        out_shape=jax.ShapeDtypeStruct((chunks,) + _wire_shape(width, used), jnp.bfloat16),
        in_specs=[pl.BlockSpec(memory_space=pltpu.VMEM)] * 2,
        out_specs=pl.BlockSpec(memory_space=pltpu.VMEM),
        scratch_shapes=[pltpu.VMEM((GROUP * used, width), jnp.bfloat16)],
        compiler_params=pltpu.CompilerParams(vmem_limit_bytes=48 * 1024 * 1024),
    )(slot_ids_t, rows)


def _gather_tile(i, used, src_ref, dst, group=GROUP):
    pieces = dst.shape[1] // LANE
    for jl in range(group):
        j = i * group + jl
        for q in range(pieces):
            dst[pl.ds(jl * used, used), pl.ds(q * LANE, LANE)] = src_ref[j, pl.ds(q * used, used), :]


def expert_kernel(x_ref, gate_ref, up_ref, down_ref, out_ref, rows_in, rows_out):
    chunks, wire_rows, _ = x_ref.shape
    width = gate_ref.shape[0]
    pieces = width // LANE
    used = wire_rows // pieces

    def tile(i, carry):
        _gather_tile(i, used, x_ref, rows_in, FFN_GROUP)
        rows = rows_in[...]
        gate_act = jnp.dot(rows, gate_ref[...], preferred_element_type=jnp.float32)
        up_act = jnp.dot(rows, up_ref[...], preferred_element_type=jnp.float32)
        inner_act = (gate_act / (1.0 + jnp.exp(-gate_act)) * up_act).astype(jnp.bfloat16)
        rows_out[...] = jnp.dot(
            inner_act, down_ref[...], preferred_element_type=jnp.float32
        ).astype(rows_out.dtype)
        for jl in range(FFN_GROUP):
            j = i * FFN_GROUP + jl
            for q in range(pieces):
                out_ref[j, pl.ds(q * used, used), :] = rows_out[
                    pl.ds(jl * used, used), pl.ds(q * LANE, LANE)
                ]
        return carry

    lax.fori_loop(0, chunks // FFN_GROUP, tile, 0)


def expert_block(arrived, gate_weights, up_weights, down_weights):
    chunks, wire_rows, _ = arrived.shape
    width = gate_weights.shape[1]
    used = wire_rows // (width // LANE)
    return pl.pallas_call(
        expert_kernel,
        out_shape=jax.ShapeDtypeStruct(arrived.shape, jnp.bfloat16),
        in_specs=[pl.BlockSpec(memory_space=pltpu.VMEM)] * 4,
        out_specs=pl.BlockSpec(memory_space=pltpu.VMEM),
        scratch_shapes=[
            pltpu.VMEM((FFN_GROUP * used, width), jnp.bfloat16),
            pltpu.VMEM((FFN_GROUP * used, width), jnp.bfloat16),
        ],
        compiler_params=pltpu.CompilerParams(vmem_limit_bytes=60 * 1024 * 1024),
    )(arrived, gate_weights[0], up_weights[0], down_weights[0])


def combine_kernel(ret_ref, mix_ref, hidden_ref, out_ref, rows, total):
    chunks, wire_rows, _ = ret_ref.shape
    width = rows.shape[1]
    used = wire_rows // (width // LANE)
    tokens = hidden_ref.shape[0]
    total[...] = jnp.zeros(total.shape, total.dtype)

    def tile(i, carry):
        _gather_tile(i, used, ret_ref, rows)
        total[...] += jnp.dot(mix_ref[i], rows[...], preferred_element_type=jnp.float32)
        return carry

    lax.fori_loop(0, chunks // GROUP, tile, 0)
    both = total[...]
    out_ref[...] = (
        hidden_ref[...].astype(jnp.float32) + both[:tokens] + both[tokens:]
    ).astype(out_ref.dtype)


def combine(returned, mix_both, hidden):
    chunks, wire_rows, _ = returned.shape
    width = hidden.shape[1]
    used = wire_rows // (width // LANE)
    return pl.pallas_call(
        combine_kernel,
        out_shape=jax.ShapeDtypeStruct(hidden.shape, jnp.bfloat16),
        in_specs=[pl.BlockSpec(memory_space=pltpu.VMEM)] * 3,
        out_specs=pl.BlockSpec(memory_space=pltpu.VMEM),
        scratch_shapes=[
            pltpu.VMEM((GROUP * used, width), jnp.bfloat16),
            pltpu.VMEM((mix_both.shape[1], width), jnp.float32),
        ],
        compiler_params=pltpu.CompilerParams(vmem_limit_bytes=48 * 1024 * 1024),
    )(returned, mix_both, hidden)


def body(
    queries,
    cache_keys,
    cache_values,
    lengths,
    sinks,
    out_proj,
    decode_resid,
    prefill_hidden,
    norm_gain,
    router,
    routes,
    expert_gate,
    expert_up,
    expert_down,
):
    n_kv = lax.axis_size("kv")
    my_block = lax.axis_index("blk")
    per_block = queries.shape[0]
    head_count = sinks.shape[0]
    head_dim = cache_keys.shape[3]
    window = cache_keys.shape[1]
    my_lengths = lax.dynamic_slice_in_dim(lengths, my_block * per_block, per_block)
    first_valid = window - jnp.minimum(my_lengths, window)
    projected = attend_reduce(
        queries,
        cache_keys[:, :, 0, :],
        cache_values[:, :, 0, :],
        first_valid,
        sinks,
        out_proj,
        n_kv,
    )
    decoded = (decode_resid.astype(jnp.float32) + projected).astype(jnp.bfloat16)
    hidden = jnp.concatenate([decoded, prefill_hidden[0]], axis=0)
    hidden_f = hidden.astype(jnp.float32)
    mean_sq = jnp.mean(hidden_f * hidden_f, axis=1, keepdims=True)
    normed = (hidden_f * lax.rsqrt(mean_sq + EPSILON) * norm_gain).astype(jnp.bfloat16)

    experts = router.shape[1]
    chosen_ids = routes[0]
    tokens, top_k = chosen_ids.shape
    model_width = hidden.shape[1]
    capacity = 14
    logits = jnp.dot(normed, router, preferred_element_type=jnp.float32)
    one_hot = chosen_ids[..., None] == jnp.arange(experts, dtype=jnp.int32)
    chosen = jnp.sum(jnp.where(one_hot, logits[:, None, :], 0.0), axis=2)
    gate_probs = jax.nn.softmax(chosen, axis=1)
    row_hot = jnp.any(one_hot, axis=1).astype(jnp.int32)
    earlier = jnp.cumsum(row_hot, axis=0) - row_hot
    slot_rank = jnp.sum(jnp.where(one_hot, earlier[:, None, :], 0), axis=2)
    rank_hot = slot_rank[..., None] == jnp.arange(capacity, dtype=jnp.int32)
    fills = one_hot[..., None] & rank_hot[:, :, None, :]
    tiles = experts // GROUP
    tile_rows = GROUP * capacity
    slot_ids = chosen_ids * capacity + slot_rank
    outgoing = dispatch(slot_ids.T, normed, experts, capacity)
    arrived = lax.all_to_all(outgoing, ("kv", "blk"), split_axis=0, concat_axis=0, tiled=True)
    processed = expert_block(arrived, expert_gate, expert_up, expert_down)
    returned = lax.all_to_all(processed, ("kv", "blk"), split_axis=0, concat_axis=0, tiled=True)
    mix = jnp.sum(jnp.where(fills, gate_probs[..., None, None], 0.0), axis=1)
    mix = mix.reshape(tokens, experts * capacity)
    mix_hi = mix.astype(jnp.bfloat16)
    mix_lo = (mix - mix_hi.astype(jnp.float32)).astype(jnp.bfloat16)
    mix_both = jnp.concatenate([mix_hi, mix_lo], axis=0)
    mix_tiles = mix_both.reshape(2 * tokens, tiles, tile_rows).transpose(1, 0, 2)
    layer_sum = combine(returned, mix_tiles, hidden)
    return layer_sum[None]


def solution(mesh):
    return jax.shard_map(
        body,
        mesh=mesh,
        in_specs=(
            P("blk", "kv"),
            P("blk", None, "kv", None),
            P("blk", None, "kv", None),
            P(),
            P("kv"),
            P("kv", None),
            P(("blk", "kv"), None),
            P(("blk", "kv"), None, None),
            P(),
            P(),
            P(("blk", "kv"), None, None),
            P(("kv", "blk"), None, None),
            P(("kv", "blk"), None, None),
            P(("kv", "blk"), None, None),
        ),
        out_specs=P(("blk", "kv"), None, None),
        check_vma=False,
    )
```
